32 devices in a mesh: dp: 4 (over y, x), expert: 4 (over z), fsdp: 2 (over core).
Axes of the slice: x: 2, y: 2, z: 4, core: 2. Of those that a mesh axis runs over, the one named last changes fastest.
Arguments:
- inputs: bfloat16 [2, 32, 1024, 512], P(None, ('dp', 'expert', 'fsdp')), may hold values from -6 to 6
- lengths: int32 [2, 32], replicated, may hold values from 256 to 1024, as said below
- routes: int32 [1, 2, 32, 1024, 8], P(None, None, ('dp', 'expert', 'fsdp')), may hold values from 0 to 23, all different within a row; in each aligned block of 1024 rows (0 to 1023, 1024 to 2047, ..., all dimensions but the last counted through in order) at most 384 rows name the same one
- ln1_gain: bfloat16 [1, 512], P(None, 'fsdp'), may hold values from 0.5 to 1.5
- ln1_bias: bfloat16 [1, 512], P(None, 'fsdp'), may hold values from -0.5 to 0.5
- kv_weight: bfloat16 [1, 512, 128], P(None, 'fsdp'), may hold values from -0.25 to 0.25
- router_weight: bfloat16 [1, 512, 24], P(None, 'fsdp'), may hold values from -0.125 to 0.125
- query_weight: bfloat16 [1, 24, 512, 64], P(None, 'expert', 'fsdp'), may hold values from -0.5 to 0.5
- out_weight: bfloat16 [1, 24, 512, 64], P(None, 'expert', 'fsdp'), may hold values from -1.5 to 1.5
- ln2_gain: bfloat16 [1, 512], P(None, 'fsdp'), may hold values from 0.5 to 1.5
- ln2_bias: bfloat16 [1, 512], P(None, 'fsdp'), may hold values from -0.5 to 0.5
- up_weight: bfloat16 [1, 512, 2048], P(None, 'fsdp'), may hold values from -0.25 to 0.25
- up_bias: bfloat16 [1, 2048], P(None, 'fsdp'), may hold values from -0.5 to 0.5
- down_weight: bfloat16 [1, 2048, 512], P(None, 'fsdp'), may hold values from -0.125 to 0.125
- down_bias: bfloat16 [1, 512], P(None, 'fsdp'), may hold values from -0.5 to 0.5
- out_cotangent: float32 [2, 32, 1024, 512], P(None, ('dp', 'expert', 'fsdp')), may hold values from -6 to 6
Outputs:
- outputs: float32 [2, 32, 1024, 512], P(None, ('dp', 'expert', 'fsdp'))
- input_grad: float32 [2, 32, 1024, 512], P(None, ('dp', 'expert', 'fsdp'))
- ln1_gain_grad: float32 [1, 512], P(None, ('dp', 'expert', 'fsdp'))
- ln1_bias_grad: float32 [1, 512], P(None, ('dp', 'expert', 'fsdp'))
- kv_weight_grad: float32 [1, 512, 128], P(None, ('dp', 'expert', 'fsdp'))
- router_weight_grad: float32 [1, 512, 24], P(None, ('dp', 'expert', 'fsdp'))
- query_weight_grad: float32 [1, 24, 512, 64], P(None, 'expert', ('dp', 'fsdp'))
- out_weight_grad: float32 [1, 24, 512, 64], P(None, 'expert', ('dp', 'fsdp'))
- ln2_gain_grad: float32 [1, 512], P(None, ('dp', 'expert', 'fsdp'))
- ln2_bias_grad: float32 [1, 512], P(None, ('dp', 'expert', 'fsdp'))
- up_weight_grad: float32 [1, 512, 2048], P(None, ('dp', 'expert', 'fsdp'))
- up_bias_grad: float32 [1, 2048], P(None, ('dp', 'expert', 'fsdp'))
- down_weight_grad: float32 [1, 2048, 512], P(None, ('dp', 'expert', 'fsdp'))
- down_bias_grad: float32 [1, 512], P(None, ('dp', 'expert', 'fsdp'))
The draws below stay inside these ranges and needn't reach their ends.
Inputs may be any that keep to these rules, and one draw needn't show every extreme that they name: `lengths`: one value or more in every micro-batch is exactly 1024, one exactly 256. `routes`: each token names 8 different experts; among the 1024 slots of one sequence in one layer and micro-batch at most 384 name the same expert, a bound that some block reaches.
All inputs are finite; a program needn't handle non-finite values.
Results may differ from the reference program's by a relative error of at most 0.017.
Values may be sent and summed in bfloat16 or wider, within the bound.
No kernel may reach another device: no remote copies, remote signals or barrier semaphores. Data moves between devices by JAX's collectives and lax.ppermute only.
A program may use at most 448 MiB of HBM per device.

```python
import math
import jax
import jax.numpy as jnp
import numpy as np
from jax import lax

D = 512
H = 64
E = 24
TOPK = 8
FF = 2048
LAYERS = 1
MICRO = 2
SLOTS = 1024
MIN_LEN = 256
CAP = 384
SEQS = 32


def draw_lengths(key, part):
    key_lens, key_order = jax.random.split(key, 2)
    drawn = jax.random.randint(key_lens, (MICRO, SEQS), MIN_LEN, SLOTS + 1)
    ranking = jax.vmap(lambda one_key: jax.random.permutation(one_key, SEQS))(jax.random.split(key_order, MICRO))
    column = lax.broadcasted_iota(jnp.int32, (MICRO, SEQS), 1)
    drawn = jnp.where(column == ranking[:, 0:1], SLOTS, drawn)
    drawn = jnp.where(column == ranking[:, 1:2], MIN_LEN, drawn)
    return drawn.astype(jnp.int32)


def level_of(stream_key, extent, cuts, low, high):
    loudness, own = 1.0, jax.random.fold_in(stream_key, 6)
    for position, blocks in cuts:
        steps = jnp.exp(jax.random.uniform(jax.random.fold_in(own, position), (blocks,), jnp.float32, low / len(cuts), high / len(cuts)))
        loudness = loudness * jnp.repeat(steps, extent[position] // blocks).reshape([-1 if axis == position else 1 for axis in range(len(extent))])
    return loudness


def shared_out(stream_key, own, number, rows, count, top, bound, skew):
    sequence = jax.random.permutation(stream_key, count)
    crowded, ordinary = load_shares(count, rows * top, bound, skew, True), load_shares(count, rows * top, bound, skew, False)
    places = jnp.arange(count)

    def named(sizes, offset_by):
        used = int((sizes > 0).sum())
        fixed = max(1, used // 4)
        moved = fixed + (places - fixed + offset_by * (used - fixed)) % max(1, count - fixed)
        return jnp.zeros((count,), jnp.int32).at[sequence[jnp.where(places < fixed, places, moved)]].set(jnp.asarray(sizes, jnp.int32))

    sizes = jnp.where(number % 4 == 0, named(crowded, number // 4), named(ordinary, number - number // 4 - 1))
    mixed = jax.random.permutation(jax.random.fold_in(own, 3), count)
    giver, receiver = mixed[0:count // 2 * 2:2], mixed[1:count // 2 * 2:2]
    room = jnp.minimum(sizes[giver] - 1, bound - sizes[receiver]) // 2
    room = jnp.where((giver == sequence[0]) | (receiver == sequence[0]) | (sizes[receiver] == 0), 0, jnp.maximum(room, 0))
    moved = jax.random.randint(jax.random.fold_in(own, 4), (count // 2,), 0, 1 << 20) % (room + 1)
    sizes = sizes.at[giver].add(-moved).at[receiver].add(moved)
    items = jnp.searchsorted(jnp.cumsum(sizes), jnp.arange(rows * top), side="right").astype(jnp.int32)
    grid = items.reshape(top, rows).T
    grid = grid[jax.random.permutation(jax.random.fold_in(own, 1), rows)]
    offset_by = jax.random.randint(jax.random.fold_in(own, 2), (rows, 1), 0, top)
    return jnp.take_along_axis(grid, (jnp.arange(top)[None, :] + offset_by) % top, axis=1)


def load_shares(number_of, total, bound, slope, full):
    weights = [(1 << 20) // math.isqrt(standing ** slope) + 1 for standing in range(1, number_of + 1)]
    largest = bound if full else min(bound, max(-(-total // number_of), total * weights[0] // sum(weights)))
    least = 1 if total - largest >= number_of - 1 else 0
    counts, spare = [largest] + [least] * (number_of - 1), total - largest - least * (number_of - 1)
    while spare > 0:
        movable = [i for i in range(1, number_of) if counts[i] < largest] or [i for i in range(1, number_of) if counts[i] < bound]
        mass, budget = sum([weights[i] for i in movable]), spare
        for i in movable:
            more = min(bound - counts[i], max(1, budget * weights[i] // mass), spare)
            counts[i] = counts[i] + more
            spare = spare - more
    return np.array(counts)


def normal_values(stream_key, dims, spread, most, pieces=(), dtype=jnp.bfloat16):
    values = jax.random.normal(stream_key, dims, jnp.float32) * spread
    if len(pieces) > 0:
        values = level_of(stream_key, dims, pieces, -0.22, 0.18) * values
    return jnp.clip(values, min=-most, max=most).astype(dtype)


def setup_inputs(seed: int = 0) -> dict:
    key_of = jax.random.split(jax.random.key(seed), 17)
    inputs = normal_values(key_of[0], (MICRO, SEQS, SLOTS, D), 1.0, 6.0, ((1, 32),))
    lengths = draw_lengths(jax.random.fold_in(key_of[16], 71), 0)
    routes_keys = jax.random.split(jax.random.fold_in(key_of[2], 1), LAYERS * MICRO * SEQS * SLOTS // SLOTS)
    routes_turns = jax.random.permutation(jax.random.fold_in(key_of[2], 3), LAYERS * MICRO * SEQS * SLOTS // SLOTS)
    routes = jax.vmap(lambda own, number: shared_out(jax.random.fold_in(key_of[2], 2), own, number, SLOTS, E, TOPK, CAP, 1))(routes_keys, routes_turns).reshape((LAYERS, MICRO, SEQS, SLOTS, TOPK))
    ln1_gain = jnp.clip(1.0 + 0.1 * jax.random.normal(key_of[3], (LAYERS, D), jnp.float32), 0.5, 1.5).astype(jnp.bfloat16)
    ln1_bias = normal_values(key_of[4], (LAYERS, D), 0.1, 0.5, ((1, 2),))
    kv_weight = normal_values(key_of[5], (LAYERS, D, 2 * H), D ** -0.5, 0.25, ((1, 2),))
    router_weight = normal_values(key_of[6], (LAYERS, D, E), (4 * D) ** -0.5, 0.125, ((1, 2),))
    query_weight = normal_values(key_of[7], (LAYERS, E, D, H), (D // 4) ** -0.5, 0.5, ((1, 4), (2, 2)))
    out_weight = normal_values(key_of[8], (LAYERS, E, D, H), (H // 4) ** -0.5, 1.5, ((1, 4), (2, 2)))
    ln2_gain = jnp.clip(1.0 + 0.1 * jax.random.normal(key_of[9], (LAYERS, D), jnp.float32), 0.5, 1.5).astype(jnp.bfloat16)
    ln2_bias = normal_values(key_of[10], (LAYERS, D), 0.1, 0.5, ((1, 2),))
    up_weight = normal_values(key_of[11], (LAYERS, D, FF), D ** -0.5, 0.25, ((1, 2),))
    up_bias = normal_values(key_of[12], (LAYERS, FF), 0.1, 0.5, ((1, 2),))
    down_weight = normal_values(key_of[13], (LAYERS, FF, D), FF ** -0.5, 0.125, ((1, 2),))
    down_bias = normal_values(key_of[14], (LAYERS, D), 0.1, 0.5, ((1, 2),))
    out_cotangent = normal_values(key_of[15], (MICRO, SEQS, SLOTS, D), 1.0, 6.0, ((1, 32),), jnp.float32)
    return {"inputs": inputs, "lengths": lengths, "routes": routes, "ln1_gain": ln1_gain, "ln1_bias": ln1_bias, "kv_weight": kv_weight, "router_weight": router_weight, "query_weight": query_weight, "out_weight": out_weight, "ln2_gain": ln2_gain, "ln2_bias": ln2_bias, "up_weight": up_weight, "up_bias": up_bias, "down_weight": down_weight, "down_bias": down_bias, "out_cotangent": out_cotangent}


@jax.custom_vjp
def low(v):
    return lax.optimization_barrier(v.astype(jnp.bfloat16)).astype(jnp.float32)

@jax.custom_vjp
def low_back(v):
    return v

def low_keep(v):
    return (low(v), None)

def low_pass(kept, grad):
    return (grad,)

def back_keep(v):
    return (v, None)

def back_low(kept, grad):
    return (low(grad),)
low.defvjp(low_keep, low_pass)
low_back.defvjp(back_keep, back_low)
HIGHEST_PRECISION = lax.Precision.HIGHEST

def layer_normalize(values, gain_vec, shift_vec):
    center = values - lax.optimization_barrier(jnp.mean(values, -1, keepdims=True))
    return center * lax.rsqrt(lax.optimization_barrier(jnp.mean(center * center, -1, keepdims=True)) + 1e-05) * gain_vec + shift_vec

def attend(query_rows, kv_rows, seq_length):
    head_width = query_rows.shape[-1]
    scores = jnp.einsum('ikh,jh->ikj', query_rows, kv_rows[:, :head_width], precision=HIGHEST_PRECISION) * (1.0 / math.sqrt(head_width))
    scores = low_back(scores)
    place_ids = lax.broadcasted_iota(jnp.int32, scores.shape, 0)
    column = lax.broadcasted_iota(jnp.int32, scores.shape, 2)
    allowed = (column <= place_ids) & (column < seq_length)
    scores = jnp.where(allowed, scores, -1e+30)
    prob_rows = low(jax.nn.softmax(scores, axis=-1))
    context = jnp.einsum('ikj,jh->ikh', prob_rows, kv_rows[:, head_width:], precision=HIGHEST_PRECISION)
    return low_back(low(context))

def block_layer(layer_state, weights, route_now, seq_lengths):
    norm_gain_vector, norm_shift, kv_proj, router_proj, head_query, head_out, ffn_gain, ffn_shift, up_proj, up_shift, down_proj, down_shift = weights
    experts = router_proj.shape[1]
    hidden = low(layer_normalize(layer_state, norm_gain_vector, norm_shift))
    kv_all = low_back(low(jnp.einsum('gsd,dc->gsc', hidden, kv_proj, precision=HIGHEST_PRECISION)))
    logits = jnp.einsum('gsd,de->gse', hidden, router_proj, precision=HIGHEST_PRECISION)
    picked = jnp.take_along_axis(logits, route_now, axis=-1)
    gate_probs = jax.nn.softmax(picked, axis=-1)
    chosen = (route_now[..., None] == lax.broadcasted_iota(jnp.int32, (1, 1, 1, experts), 3)).astype(jnp.float32)
    copies = low_back(jnp.broadcast_to(hidden[:, :, None, :], hidden.shape[:2] + (experts, hidden.shape[2])))
    queries = low_back(low(jnp.einsum('gsed,edh->gseh', copies, head_query, precision=HIGHEST_PRECISION)))
    picked_query = jnp.einsum('gske,gseh->gskh', chosen, queries, precision=HIGHEST_PRECISION)
    context = lax.map(jax.checkpoint(lambda element: attend(element[0], element[1], element[2])), (picked_query, kv_all, seq_lengths))
    spread_context = jnp.einsum('gske,gskh->gseh', chosen, context, precision=HIGHEST_PRECISION)
    answer = low_back(low(jnp.einsum('gseh,edh->gsed', spread_context, head_out, precision=HIGHEST_PRECISION)))
    gate_table = jnp.einsum('gske,gsk->gse', chosen, gate_probs, precision=HIGHEST_PRECISION)
    mixed_state = layer_state + jnp.einsum('gse,gsed->gsd', gate_table, answer, precision=HIGHEST_PRECISION)
    hidden_mid = low(layer_normalize(mixed_state, ffn_gain, ffn_shift))
    before_act = low_back(jnp.einsum('gsd,df->gsf', hidden_mid, up_proj, precision=HIGHEST_PRECISION) + up_shift)
    active = low(jax.nn.gelu(before_act, approximate=True))
    return mixed_state + low_back(jnp.einsum('gsf,fd->gsd', active, down_proj, precision=HIGHEST_PRECISION) + down_shift)

def reference(inputs, lengths, routes, ln1_gain, ln1_bias, kv_weight, router_weight, query_weight, out_weight, ln2_gain, ln2_bias, up_weight, up_bias, down_weight, down_bias, out_cotangent):
    params_all = tuple((element.astype(jnp.float32) for element in (ln1_gain, ln1_bias, kv_weight, router_weight, query_weight, out_weight, ln2_gain, ln2_bias, up_weight, up_bias, down_weight, down_bias)))
    group_count = MICRO * SEQS // 2
    states = inputs.astype(jnp.float32).reshape(group_count, 2, SLOTS, D)
    cotangents = out_cotangent.astype(jnp.float32).reshape(group_count, 2, SLOTS, D)
    route_groups = jnp.moveaxis(routes.reshape(LAYERS, group_count, 2, SLOTS, TOPK), 1, 0)
    length_groups = lengths.reshape(group_count, 2)

    def run_layers(layer_state, params_now, route_now, seq_lengths):
        for layer_at in range(LAYERS):
            layer_state = block_layer(layer_state, tuple((element[layer_at] for element in params_now)), route_now[layer_at], seq_lengths)
        return layer_state

    def group_step(totals, element):
        layer_state, cotangent, route_now, seq_lengths = element
        result, pull = jax.vjp(lambda state_in, params_in: run_layers(state_in, params_in, route_now, seq_lengths), layer_state, params_all)
        valid_rows = (lax.broadcasted_iota(jnp.int32, (2, SLOTS), 1) < seq_lengths[:, None]).astype(jnp.float32)
        grad_state, grad_params = pull(cotangent * valid_rows[:, :, None])
        return (tuple((summed + added for summed, added in zip(totals, grad_params))), (result, grad_state))
    totals, (results, grad_states) = lax.scan(group_step, tuple((jnp.zeros_like(element) for element in params_all)), (states, cotangents, route_groups, length_groups))
    return (results.reshape(MICRO, SEQS, SLOTS, D), grad_states.reshape(MICRO, SEQS, SLOTS, D), totals[0], totals[1], totals[2], totals[3], totals[4], totals[5], totals[6], totals[7], totals[8], totals[9], totals[10], totals[11])
```

```python
import functools

import jax
import jax.numpy as jnp
from jax import lax
from jax.experimental import pallas as pl
from jax.experimental.pallas import tpu as pltpu
from jax.sharding import PartitionSpec as P

EPSILON = 1e-05
NEGATIVE = -1e30
GELU_SCALE = 0.7978845608028654
GELU_CUBIC = 0.044715
BLOCK = 256
AXES = ("dp", "expert", "fsdp")
F32 = jnp.float32
BF16 = jnp.bfloat16
VMEM_BYTES = 60 << 20


def dot_nn(left, right):
    return lax.dot_general(left, right, (((1,), (0,)), ((), ())), preferred_element_type=F32)


def dot_nt(left, right):
    return lax.dot_general(left, right, (((1,), (1,)), ((), ())), preferred_element_type=F32)


def dot_tn(left, right):
    return lax.dot_general(left, right, (((0,), (0,)), ((), ())), preferred_element_type=F32)


def normalize(values):
    center = values - jnp.mean(values, -1, keepdims=True)
    spread = lax.rsqrt(jnp.mean(center * center, -1, keepdims=True) + EPSILON)
    return center * spread, spread


def fold_rows(values, combine):
    rows, columns = values.shape
    return combine(values.reshape(rows // 8, 8, columns), 0)


def pick_slots(table_ref, slot, picks, width, span):
    experts = slot.shape[0]
    picked = []
    for pick in range(picks):
        value = table_ref[pick * width : (pick + 1) * width, :]
        for expert in range(pick + 1, experts - picks + pick + 1):
            hit = jnp.broadcast_to(slot[expert : expert + 1, :], (width, span)) == pick
            value = jnp.where(hit, table_ref[expert * width : (expert + 1) * width, :], value)
        picked.append(value)
    return picked


def spread_slots(read, slot, expert, picks, width, span):
    experts = slot.shape[0]
    row = jnp.broadcast_to(slot[expert : expert + 1, :], (width, span))
    value = jnp.zeros((width, span), F32)
    for pick in range(max(0, expert - experts + picks), min(expert, picks - 1) + 1):
        value = jnp.where(row == pick, read(pick), value)
    return value


def forward_kernel(
    lens,
    x_ref,
    route_ref,
    gain_ref,
    shift_ref,
    w_ref,
    wk_ref,
    wv_ref,
    hid_ref,
    kaug_ref,
    vaug_ref,
    kt_ref,
    q_ref,
    ctx_ref,
    lse_ref,
    gate_ref,
    slot_ref,
    table,
    qaug,
    scores,
    vt,
    acc,
):
    block = pl.program_id(1)
    length = lens[pl.program_id(0)]
    span = x_ref.shape[2]
    experts = slot_ref.shape[2]
    picks = route_ref.shape[2]
    width = kt_ref.shape[3]
    half = w_ref.shape[2]
    rows = picks * span

    normed, _ = normalize(x_ref[0, 0].astype(F32))
    hid = (normed * gain_ref[...] + shift_ref[...]).astype(BF16)
    hid_ref[0, 0] = hid
    table[...] = dot_nt(w_ref[0], hid[:, :half]) + dot_nt(w_ref[1], hid[:, half:])
    head = experts * width
    kt_ref[0, 0, 0] = table[head : head + width, :].astype(BF16)
    vt[block] = table[head + width : head + 2 * width, :].astype(BF16)

    lane = lax.broadcasted_iota(jnp.int32, (span, 2 * width), 1)
    place = block * span + lax.broadcasted_iota(jnp.int32, (span, 2 * width), 0)
    ones = jnp.where(lane < width + 4, 1.0, 0.0)
    cut = jnp.where(place < length, 0.0, NEGATIVE)
    keys = jnp.where(lane < width, dot_nn(hid, wk_ref[...]), jnp.where(lane == width, cut, ones))
    kaug_ref[0, block] = keys.astype(BF16)
    vals = jnp.where(lane < width, dot_nn(hid, wv_ref[...]), ones)
    vaug_ref[0, block] = vals.astype(BF16)

    logits = table[head + 2 * width : head + 2 * width + experts, :]
    expert_id = lax.broadcasted_iota(jnp.int32, (experts, span), 0)
    chosen = jnp.zeros((experts, span), F32)
    for pick in range(picks):
        chosen = jnp.where(expert_id == route_ref[0, 0, pick : pick + 1, :], 1.0, chosen)
    lower = jnp.where(
        lax.broadcasted_iota(jnp.int32, (experts, experts), 1)
        < lax.broadcasted_iota(jnp.int32, (experts, experts), 0),
        1.0,
        0.0,
    )
    slot = jnp.where(chosen > 0.0, dot_nn(lower, chosen), -1.0).astype(jnp.int32)
    slot_ref[0, 0] = slot
    masked = jnp.where(chosen > 0.0, logits, NEGATIVE)
    raised = jnp.where(chosen > 0.0, jnp.exp(masked - jnp.max(masked, 0, keepdims=True)), 0.0)
    gate_ref[0, 0] = raised / jnp.sum(raised, 0, keepdims=True)

    picked = pick_slots(table, slot, picks, width, span)
    for pick in range(picks):
        qaug[0:width, pick * span : (pick + 1) * span] = (
            picked[pick].astype(BF16) * (width**-0.5)
        ).astype(BF16)
    q_ref[0, 0] = qaug[0:width, :]
    side = lax.broadcasted_iota(jnp.int32, (width, rows), 0)
    qaug[width : 2 * width, :] = jnp.where(side == 0, 1.0, 0.0).astype(BF16)

    def score_step(at, top):
        part = dot_nn(kaug_ref[0, at], qaug[...])
        scores[at] = part
        return jnp.maximum(top, fold_rows(part, jnp.max))

    used = jnp.minimum(block, (length + span - 1) // span)
    top = lax.fori_loop(0, used, score_step, jnp.full((8, rows), NEGATIVE, F32))
    causal = lax.broadcasted_iota(jnp.int32, (span, rows), 0) <= (
        lax.broadcasted_iota(jnp.int32, (span, rows), 1) & (span - 1)
    )
    part = jnp.where(causal, dot_nn(kaug_ref[0, block], qaug[...]), NEGATIVE)
    top = jnp.maximum(top, fold_rows(part, jnp.max))
    top = jnp.max(top, 0, keepdims=True)
    raised = jnp.exp(part - top)
    acc[...] = dot_nn(vt[block], raised.astype(BF16))
    total = fold_rows(raised, jnp.sum)

    def value_step(at, total):
        raised = jnp.exp(scores[at] - top)
        acc[...] += dot_nn(vt[at], raised.astype(BF16))
        return total + fold_rows(raised, jnp.sum)

    total = lax.fori_loop(0, used, value_step, total)
    total = jnp.sum(total, 0, keepdims=True)
    ctx_ref[0, 0] = (acc[...] * (1.0 / total)).astype(BF16)
    lse_ref[0, 0] = top + jnp.log(total)


def middle_kernel(
    lens,
    x_ref,
    ctx_ref,
    gate_ref,
    slot_ref,
    cot_ref,
    w_ref,
    gain_ref,
    shift_ref,
    up_ref,
    up_shift_ref,
    down_ref,
    down_shift_ref,
    out_ref,
    mid_ref,
    do_ref,
    delta_ref,
    gl_ref,
    down_grad_ref,
    up_grad_ref,
    wo_grad_ref,
    small_ref,
    up_shift_grad_ref,
    gated,
    cexp,
    table,
    down_acc,
    up_acc,
    wo_acc,
):
    micro = pl.program_id(0)
    block = pl.program_id(1)
    length = lens[micro]
    span = x_ref.shape[2]
    experts = slot_ref.shape[2]
    width = ctx_ref.shape[2]
    picks = ctx_ref.shape[3] // span
    half = w_ref.shape[2]
    first = (micro == 0) & (block == 0)
    last = (micro == pl.num_programs(0) - 1) & (block == pl.num_programs(1) - 1)

    @pl.when(first)
    def _():
        down_acc[...] = jnp.zeros_like(down_acc)
        up_acc[...] = jnp.zeros_like(up_acc)
        wo_acc[...] = jnp.zeros_like(wo_acc)
        small_ref[...] = jnp.zeros_like(small_ref)
        up_shift_grad_ref[...] = jnp.zeros_like(up_shift_grad_ref)

    slot = slot_ref[0, 0]
    gates = gate_ref[0, 0]
    gate = [
        jnp.sum(jnp.where(slot == pick, gates, 0.0), 0, keepdims=True) for pick in range(picks)
    ]
    for pick in range(picks):
        at = slice(pick * span, (pick + 1) * span)
        gated[:, at] = ctx_ref[0, 0, :, at].astype(F32) * gate[pick]
    for expert in range(experts):
        cexp[expert * width : (expert + 1) * width, :] = spread_slots(
            lambda pick: gated[:, pick * span : (pick + 1) * span],
            slot,
            expert,
            picks,
            width,
            span,
        ).astype(BF16)
    mixed = x_ref[0, 0].astype(F32) + jnp.concatenate(
        [dot_tn(cexp[...], w_ref[0]), dot_tn(cexp[...], w_ref[1])], 1
    )
    normed, spread = normalize(mixed)
    hid = (normed * gain_ref[...] + shift_ref[...]).astype(BF16)
    place = block * span + lax.broadcasted_iota(jnp.int32, (span, 1), 0)
    grad = jnp.where(place < length, cot_ref[0, 0], 0.0)
    grad_b = grad.astype(BF16)
    hid_t = hid.T
    out = mixed + down_shift_ref[...]
    back = jnp.zeros_like(mixed)
    hidden_units = up_ref.shape[1]
    step = min(hidden_units, 512)
    for at in range(0, hidden_units, step):
        cut = slice(at, at + step)
        pre = dot_nn(hid, up_ref[:, cut]) + up_shift_ref[:, cut]
        square = pre * pre
        bent = jnp.tanh(pre * (GELU_SCALE + (GELU_SCALE * GELU_CUBIC) * square))
        rise = 0.5 + 0.5 * bent
        active = (pre * rise).astype(BF16)
        slope = rise + (0.5 * pre) * (1.0 - bent * bent) * (
            GELU_SCALE + (3.0 * GELU_SCALE * GELU_CUBIC) * square
        )
        grad_pre = dot_nt(grad_b, down_ref[cut, :]) * slope
        grad_pre_b = grad_pre.astype(BF16)
        out = out + dot_nn(active, down_ref[cut, :])
        back = back + dot_nt(grad_pre_b, up_ref[:, cut])
        down_acc[cut, :] += dot_nn(active.T, grad_b)
        up_acc[:, cut] += dot_nn(hid_t, grad_pre_b)
        up_shift_grad_ref[:, cut] += fold_rows(grad_pre, jnp.sum)
    out_ref[0, 0] = out
    scaled = back * gain_ref[...]
    mid = grad + spread * (
        scaled
        - jnp.mean(scaled, -1, keepdims=True)
        - normed * jnp.mean(scaled * normed, -1, keepdims=True)
    )
    mid_ref[0, 0] = mid
    small_ref[0] += fold_rows(back * normed, jnp.sum)
    small_ref[1] += fold_rows(back, jnp.sum)
    small_ref[2] += fold_rows(grad_b.astype(F32), jnp.sum)

    mid_b = mid.astype(BF16)
    wo_acc[...] += dot_nt(mid_b.T, cexp[...])
    table[...] = dot_nt(w_ref[0], mid_b[:, :half]) + dot_nt(w_ref[1], mid_b[:, half:])
    picked = pick_slots(table, slot, picks, width, span)
    grad_gate = []
    for pick in range(picks):
        at = slice(pick * span, (pick + 1) * span)
        ctx = ctx_ref[0, 0, :, at].astype(F32)
        grad_gate.append(jnp.sum(picked[pick] * ctx, 0, keepdims=True))
        grad_ctx = (picked[pick] * gate[pick]).astype(BF16)
        do_ref[0, 0, :, at] = grad_ctx
        delta_ref[0, 0, :, at] = jnp.sum(grad_ctx.astype(F32) * ctx, 0, keepdims=True)
    average = gate[0] * grad_gate[0]
    for pick in range(1, picks):
        average = average + gate[pick] * grad_gate[pick]
    grad_logits = jnp.zeros((experts, span), F32)
    for pick in range(picks):
        grad_logits = jnp.where(
            slot == pick, gate[pick] * (grad_gate[pick] - average), grad_logits
        )
    gl_ref[0, 0] = grad_logits

    @pl.when(last)
    def _():
        down_grad_ref[...] = down_acc[...].astype(BF16)
        up_grad_ref[...] = up_acc[...].astype(BF16)
        wo_grad_ref[...] = wo_acc[...].astype(BF16)


def split_three(values):
    high = values.astype(BF16).astype(F32)
    rest = values - high
    middle = rest.astype(BF16).astype(F32)
    return high, middle, rest - middle


def backward_kernel(
    lens,
    hid_ref,
    kaug_ref,
    vaug_ref,
    kt_ref,
    q_ref,
    lse_ref,
    do_ref,
    delta_ref,
    slot_ref,
    gl_ref,
    r_ref,
    w_grad_ref,
    qaug,
    daug,
    dq,
    dkt,
    dvt,
    w_acc,
):
    micro = pl.program_id(0)
    step = pl.program_id(1)
    blocks = pl.num_programs(1)
    block = blocks - 1 - step
    length = lens[micro]
    span = hid_ref.shape[2]
    experts = slot_ref.shape[2]
    width = q_ref.shape[2]
    rows = q_ref.shape[3]
    picks = rows // span
    head = experts * width

    @pl.when((micro == 0) & (step == 0))
    def _():
        w_acc[...] = jnp.zeros_like(w_acc)

    @pl.when(step == 0)
    def _():
        dkt[...] = jnp.zeros_like(dkt)
        dvt[...] = jnp.zeros_like(dvt)

    @pl.when(block * span >= length)
    def _():
        r_ref[...] = jnp.zeros_like(r_ref)

    @pl.when(block * span < length)
    def _():
        side = lax.broadcasted_iota(jnp.int32, (width, rows), 0)
        qaug[0:width, :] = q_ref[0, 0]
        high, middle, low = split_three(-lse_ref[0, 0])
        qaug[width : 2 * width, :] = jnp.where(
            side == 0,
            1.0,
            jnp.where(side == 1, high, jnp.where(side == 2, middle, jnp.where(side == 3, low, 0.0))),
        ).astype(BF16)
        daug[0:width, :] = do_ref[0, 0]
        high, middle, low = split_three(-delta_ref[0, 0])
        daug[width : 2 * width, :] = jnp.where(
            side == 0, high, jnp.where(side == 1, middle, jnp.where(side == 2, low, 0.0))
        ).astype(BF16)

        def key_step(at, probs):
            probs_b = probs.astype(BF16)
            slopes = (probs * dot_nn(vaug_ref[0, at], daug[...])).astype(BF16)
            dvt[at] += dot_nt(daug[0:width, :], probs_b)
            dkt[at] += dot_nt(qaug[0:width, :], slopes)
            return dot_nn(kt_ref[0, at], slopes)

        causal = lax.broadcasted_iota(jnp.int32, (span, rows), 0) <= (
            lax.broadcasted_iota(jnp.int32, (span, rows), 1) & (span - 1)
        )
        dq[...] = key_step(
            block, jnp.where(causal, jnp.exp(dot_nn(kaug_ref[0, block], qaug[...])), 0.0)
        )

        def body(at, carry):
            dq[...] += key_step(at, jnp.exp(dot_nn(kaug_ref[0, at], qaug[...])))
            return carry

        lax.fori_loop(0, block, body, 0)
        dq[...] = dq[...] * (width**-0.5)
        slot = slot_ref[0, 0]
        for expert in range(experts):
            r_ref[0, 0, expert * width : (expert + 1) * width, :] = spread_slots(
                lambda pick: dq[:, pick * span : (pick + 1) * span],
                slot,
                expert,
                picks,
                width,
                span,
            ).astype(BF16)
        r_ref[0, 0, head : head + width, :] = dkt[block].astype(BF16)
        r_ref[0, 0, head + width : head + 2 * width, :] = dvt[block].astype(BF16)
        tail = r_ref.shape[2] - head - 2 * width
        r_ref[0, 0, head + 2 * width :, :] = jnp.concatenate(
            [gl_ref[0, 0], jnp.zeros((tail - experts, span), F32)], 0
        ).astype(BF16)
        w_acc[...] += dot_nt(hid_ref[0, 0].T, r_ref[0, 0])

    @pl.when((micro == pl.num_programs(0) - 1) & (step == blocks - 1))
    def _():
        w_grad_ref[...] = w_acc[...].astype(BF16)


def input_kernel(x_ref, mid_ref, r_ref, w_ref, gain_ref, out_ref, small_ref):
    first = (pl.program_id(0) == 0) & (pl.program_id(1) == 0)

    @pl.when(first)
    def _():
        small_ref[...] = jnp.zeros_like(small_ref)

    back = jnp.concatenate(
        [dot_tn(r_ref[0, 0], w_ref[0]), dot_tn(r_ref[0, 0], w_ref[1])], 1
    )
    normed, spread = normalize(x_ref[0, 0].astype(F32))
    scaled = back * gain_ref[...]
    out_ref[0, 0] = mid_ref[0, 0] + spread * (
        scaled
        - jnp.mean(scaled, -1, keepdims=True)
        - normed * jnp.mean(scaled * normed, -1, keepdims=True)
    )
    small_ref[0] += fold_rows(back * normed, jnp.sum)
    small_ref[1] += fold_rows(back, jnp.sum)


def full(shape):
    return pl.BlockSpec(shape, lambda *ids: (0,) * len(shape))


def blocked(shape):
    tail = (0,) * (len(shape) - 2)
    return pl.BlockSpec((1, 1) + tuple(shape[2:]), lambda m, i, *refs: (m, i) + tail)


def reversed_blocks(shape):
    tail = (0,) * (len(shape) - 2)
    last = shape[1] - 1
    return pl.BlockSpec((1, 1) + tuple(shape[2:]), lambda m, i, *refs: (m, last - i) + tail)


def whole(shape):
    tail = (0,) * (len(shape) - 1)
    return pl.BlockSpec((1,) + tuple(shape[1:]), lambda m, i, *refs: (m,) + tail)


def struct(shape, dtype):
    return jax.ShapeDtypeStruct(shape, dtype)


def params():
    return pltpu.CompilerParams(
        dimension_semantics=("arbitrary", "arbitrary"), vmem_limit_bytes=VMEM_BYTES
    )


def cost(flops, transcendentals, moved):
    return pl.CostEstimate(flops=flops, transcendentals=transcendentals, bytes_accessed=moved)


def exchange(value, axis, distance):
    count = lax.axis_size(axis)
    return lax.ppermute(value, axis, [(at, at ^ distance) for at in range(count)])


def permute_groups(value, index):
    groups = value.shape[0]
    bit = 1
    while bit < groups:
        pairs = value.reshape((groups // (2 * bit), 2, bit) + value.shape[1:])
        value = jnp.where((index & bit) != 0, pairs[:, ::-1].reshape(value.shape), value)
        bit *= 2
    return value


def pick_at(value, index, dim):
    return lax.dynamic_index_in_dim(value, index, dim, keepdims=False)


def reduce_axis(value, axis, dim, relative=False, keep=False):
    count = lax.axis_size(axis)
    me = lax.axis_index(axis)
    base = 0 if relative else me
    total = pick_at(value, base, dim).astype(F32)
    for distance in range(1, count):
        sent = pick_at(value, distance if relative else me ^ distance, dim)
        total = total + exchange(sent, axis, distance).astype(F32)
    return total if keep else total.astype(BF16)


def local(
    inputs,
    lengths,
    routes,
    ln1_gain,
    ln1_bias,
    kv_weight,
    router_weight,
    query_weight,
    out_weight,
    ln2_gain,
    ln2_bias,
    up_weight,
    up_bias,
    down_weight,
    down_bias,
    out_cotangent,
):
    micro_count, _, slots, model = inputs.shape
    experts = router_weight.shape[2]
    width = query_weight.shape[3]
    picks = routes.shape[4]
    hidden_units = up_weight.shape[2]
    dp_size, z_size, f_size = (lax.axis_size(axis) for axis in AXES)
    z_at = lax.axis_index("expert")
    seq_index = (lax.axis_index("dp") * z_size + z_at) * f_size + lax.axis_index("fsdp")
    own_experts = experts // z_size
    half = model // f_size
    span = min(BLOCK, slots)
    blocks = slots // span
    rows = picks * span
    head = experts * width
    spare = -(-experts // 16) * 16
    all_rows = head + 2 * width + spare

    def gather(value, dim):
        return lax.all_gather(value, "fsdp", axis=dim, tiled=True)

    lens = lax.dynamic_index_in_dim(lengths, seq_index, 1, keepdims=False)

    def transposed_heads(weight):
        own = jnp.swapaxes(weight[0], 1, 2).reshape(own_experts * width, half)
        return [own] + [exchange(own, "expert", distance) for distance in range(1, z_size)]

    query_parts = transposed_heads(query_weight)
    out_parts = transposed_heads(out_weight)
    router_t = router_weight[0].T.reshape(z_size, own_experts, half)
    router_t = permute_groups(router_t, z_at).reshape(experts, half)
    router_t = jnp.pad(router_t, ((0, spare - experts), (0, 0)))
    proj = lax.all_gather(
        jnp.concatenate(query_parts + [kv_weight[0].T, router_t], 0), "fsdp", axis=0
    )
    out_proj = lax.all_gather(jnp.concatenate(out_parts, 0), "fsdp", axis=0)
    kv_full = gather(kv_weight[0], 0)
    key_weight = jnp.pad(kv_full[:, :width], ((0, 0), (0, width)))
    value_weight = jnp.pad(kv_full[:, width:], ((0, 0), (0, width)))
    gains = gather(jnp.concatenate([ln1_gain, ln1_bias, ln2_gain, ln2_bias, down_bias], 0), 1)
    gains = gains.astype(F32)
    gain1, shift1, gain2, shift2, down_shift = (gains[at : at + 1] for at in range(5))
    up_shift = gather(up_bias, 1).astype(F32)
    up_full = gather(up_weight[0], 0)
    down_full = gather(down_weight[0], 0)

    local_routes = routes[0, :, 0]
    local_routes = ((local_routes // own_experts) ^ z_at) * own_experts + local_routes % own_experts
    route_t = jnp.swapaxes(local_routes.reshape(micro_count, blocks, span, picks), 2, 3)
    states = inputs.reshape(micro_count, blocks, span, model)
    cotangent = out_cotangent.reshape(micro_count, blocks, span, model)

    grid = (micro_count, blocks)
    hid_s = struct((micro_count, blocks, span, model), BF16)
    aug_s = struct((micro_count, blocks, span, 2 * width), BF16)
    kt_s = struct((micro_count, blocks, 1, width, span), BF16)
    q_s = struct((micro_count, blocks, width, rows), BF16)
    row_s = struct((micro_count, blocks, 1, rows), F32)
    gate_s = struct((micro_count, blocks, experts, span), F32)
    slot_s = struct((micro_count, blocks, experts, span), jnp.int32)
    tokens = micro_count * slots
    pair_flops = tokens * picks * slots * width
    hid, kaug, vaug, kt, q, ctx, lse, gates, slot = pl.pallas_call(
        forward_kernel,
        name="forward",
        grid_spec=pltpu.PrefetchScalarGridSpec(
            num_scalar_prefetch=1,
            grid=grid,
            in_specs=[
                blocked(states.shape),
                blocked(route_t.shape),
                full(gain1.shape),
                full(shift1.shape),
                full(proj.shape),
                full(key_weight.shape),
                full(value_weight.shape),
            ],
            out_specs=[
                blocked(hid_s.shape),
                whole(aug_s.shape),
                whole(aug_s.shape),
                blocked(kt_s.shape),
                blocked(q_s.shape),
                blocked(q_s.shape),
                blocked(row_s.shape),
                blocked(gate_s.shape),
                blocked(slot_s.shape),
            ],
            scratch_shapes=[
                pltpu.VMEM((all_rows, span), F32),
                pltpu.VMEM((2 * width, rows), BF16),
                pltpu.VMEM((blocks, span, rows), F32),
                pltpu.VMEM((blocks, width, span), BF16),
                pltpu.VMEM((width, rows), F32),
            ],
        ),
        out_shape=[hid_s, aug_s, aug_s, kt_s, q_s, q_s, row_s, gate_s, slot_s],
        compiler_params=params(),
        cost_estimate=cost(2 * tokens * model * all_rows + 8 * pair_flops, 0, 8 << 20),
    )(lens, states, route_t, gain1, shift1, proj, key_weight, value_weight)

    state_s = struct((micro_count, blocks, span, model), F32)
    outputs, mid, grad_ctx, delta, grad_logits, down_grad, up_grad, wo_grad, small2, up_small = (
        pl.pallas_call(
            middle_kernel,
            name="middle",
            grid_spec=pltpu.PrefetchScalarGridSpec(
                num_scalar_prefetch=1,
                grid=grid,
                in_specs=[
                    blocked(states.shape),
                    blocked(q_s.shape),
                    blocked(gate_s.shape),
                    blocked(slot_s.shape),
                    blocked(cotangent.shape),
                    full(out_proj.shape),
                    full(gain2.shape),
                    full(shift2.shape),
                    full(up_full.shape),
                    full(up_shift.shape),
                    full(down_full.shape),
                    full(down_shift.shape),
                ],
                out_specs=[
                    blocked(state_s.shape),
                    blocked(state_s.shape),
                    blocked(q_s.shape),
                    blocked(row_s.shape),
                    blocked(gate_s.shape),
                    full((hidden_units, model)),
                    full((model, hidden_units)),
                    full((model, head)),
                    full((3, 8, model)),
                    full((8, hidden_units)),
                ],
                scratch_shapes=[
                    pltpu.VMEM((width, rows), F32),
                    pltpu.VMEM((head, span), BF16),
                    pltpu.VMEM((head, span), F32),
                    pltpu.VMEM((hidden_units, model), F32),
                    pltpu.VMEM((model, hidden_units), F32),
                    pltpu.VMEM((model, head), F32),
                ],
            ),
            out_shape=[
                state_s,
                state_s,
                q_s,
                row_s,
                gate_s,
                struct((hidden_units, model), BF16),
                struct((model, hidden_units), BF16),
                struct((model, head), BF16),
                struct((3, 8, model), F32),
                struct((8, hidden_units), F32),
            ],
            compiler_params=params(),
            cost_estimate=cost(
                2 * tokens * model * (6 * hidden_units + 3 * head), 0, 24 << 20
            ),
        )(
            lens,
            states,
            ctx,
            gates,
            slot,
            cotangent,
            out_proj,
            gain2,
            shift2,
            up_full,
            up_shift,
            down_full,
            down_shift,
        )
    )

    r_s = struct((micro_count, blocks, all_rows, span), BF16)
    routed, w_grad = pl.pallas_call(
        backward_kernel,
        name="backward",
        grid_spec=pltpu.PrefetchScalarGridSpec(
            num_scalar_prefetch=1,
            grid=grid,
            in_specs=[
                reversed_blocks(hid_s.shape),
                whole(aug_s.shape),
                whole(aug_s.shape),
                whole((micro_count, blocks, width, span)),
                reversed_blocks(q_s.shape),
                reversed_blocks(row_s.shape),
                reversed_blocks(q_s.shape),
                reversed_blocks(row_s.shape),
                reversed_blocks(slot_s.shape),
                reversed_blocks(gate_s.shape),
            ],
            out_specs=[reversed_blocks(r_s.shape), full((model, all_rows))],
            scratch_shapes=[
                pltpu.VMEM((2 * width, rows), BF16),
                pltpu.VMEM((2 * width, rows), BF16),
                pltpu.VMEM((width, rows), F32),
                pltpu.VMEM((blocks, width, span), F32),
                pltpu.VMEM((blocks, width, span), F32),
                pltpu.VMEM((model, all_rows), F32),
            ],
        ),
        out_shape=[r_s, struct((model, all_rows), BF16)],
        compiler_params=params(),
        cost_estimate=cost(2 * tokens * model * all_rows + 20 * pair_flops, 0, 24 << 20),
    )(
        lens,
        hid,
        kaug,
        vaug,
        kt.reshape(micro_count, blocks, width, span),
        q,
        lse,
        grad_ctx,
        delta,
        slot,
        grad_logits,
    )

    input_grad, small1 = pl.pallas_call(
        input_kernel,
        name="input_back",
        grid_spec=pltpu.PrefetchScalarGridSpec(
            num_scalar_prefetch=0,
            grid=grid,
            in_specs=[
                blocked(states.shape),
                blocked(state_s.shape),
                blocked(r_s.shape),
                full(proj.shape),
                full(gain1.shape),
            ],
            out_specs=[blocked(state_s.shape), full((2, 8, model))],
        ),
        out_shape=[state_s, struct((2, 8, model), F32)],
        compiler_params=params(),
        cost_estimate=cost(2 * tokens * model * all_rows, 0, 20 << 20),
    )(states, mid, routed, proj, gain1)

    def reduce_shared(value, chunk):
        value = value.reshape(dp_size, z_size, f_size, chunk, value.shape[1])
        value = reduce_axis(value, "fsdp", 2)
        value = reduce_axis(value, "dp", 0)
        return reduce_axis(value, "expert", 0, keep=True)

    def reduce_heads(value):
        chunk = model // (dp_size * f_size)
        value = value.reshape(dp_size, f_size, chunk, z_size, own_experts * width)
        value = reduce_axis(value, "fsdp", 1)
        value = reduce_axis(value, "dp", 0)
        value = reduce_axis(value, "expert", 1, relative=True, keep=True)
        return jnp.swapaxes(value.reshape(chunk, own_experts, width), 0, 1)[None]

    devices = dp_size * z_size * f_size
    up_weight_grad = reduce_shared(up_grad, model // devices)
    down_weight_grad = reduce_shared(down_grad, hidden_units // devices)
    out_weight_grad = reduce_heads(wo_grad)
    query_weight_grad = reduce_heads(w_grad[:, :head])

    chunk = model // devices
    router_grad = w_grad[:, head + 2 * width : head + 2 * width + experts].astype(F32)
    router_grad = permute_groups(router_grad.T.reshape(z_size, own_experts, model), z_at)
    router_grad = jnp.pad(router_grad.reshape(experts, model).T, ((0, 0), (0, spare - experts)))
    narrow = jnp.concatenate([w_grad[:, head : head + 2 * width].astype(F32), router_grad], 1)
    narrow = narrow.reshape(devices, chunk * (2 * width + spare))
    vectors = jnp.concatenate([jnp.sum(small1, 1), jnp.sum(small2, 1)], 0)
    vectors = jnp.swapaxes(vectors.reshape(5, devices, chunk), 0, 1).reshape(devices, 5 * chunk)
    up_vector = jnp.sum(up_small, 0).reshape(devices, hidden_units // devices)
    packed = jnp.concatenate([narrow, vectors, up_vector], 1)
    packed = lax.all_to_all(packed, AXES, split_axis=0, concat_axis=0, tiled=True)
    packed = jnp.sum(packed.reshape(devices, -1), 0)
    cut = chunk * (2 * width + spare)
    narrow = packed[:cut].reshape(chunk, 2 * width + spare)
    vectors = packed[cut : cut + 5 * chunk].reshape(5, 1, chunk)
    up_vector = packed[cut + 5 * chunk :][None]
    shape = (micro_count, 1, slots, model)
    return (
        outputs.reshape(shape),
        input_grad.reshape(shape),
        vectors[0],
        vectors[1],
        narrow[None, :, : 2 * width],
        narrow[None, :, 2 * width : 2 * width + experts],
        query_weight_grad,
        out_weight_grad,
        vectors[2],
        vectors[3],
        up_weight_grad[None],
        up_vector,
        down_weight_grad[None],
        vectors[4],
    )


def solution(mesh):
    shards = P(None, AXES, None, None)
    return jax.shard_map(
        local,
        mesh=mesh,
        in_specs=(
            shards,
            P(),
            P(None, None, AXES, None, None),
            P(None, "fsdp"),
            P(None, "fsdp"),
            P(None, "fsdp", None),
            P(None, "fsdp", None),
            P(None, "expert", "fsdp", None),
            P(None, "expert", "fsdp", None),
            P(None, "fsdp"),
            P(None, "fsdp"),
            P(None, "fsdp", None),
            P(None, "fsdp"),
            P(None, "fsdp", None),
            P(None, "fsdp"),
            shards,
        ),
        out_specs=(
            shards,
            shards,
            P(None, AXES),
            P(None, AXES),
            P(None, AXES, None),
            P(None, AXES, None),
            P(None, "expert", ("dp", "fsdp"), None),
            P(None, "expert", ("dp", "fsdp"), None),
            P(None, AXES),
            P(None, AXES),
            P(None, AXES, None),
            P(None, AXES),
            P(None, AXES, None),
            P(None, AXES),
        ),
        check_vma=False,
    )
```

```python
import functools

import jax
import jax.numpy as jnp
from jax import lax
from jax.experimental import pallas as pl
from jax.experimental.pallas import tpu as pltpu
from jax.sharding import PartitionSpec as P

EPSILON = 1e-05
NEGATIVE = -1e30
GELU_SCALE = 0.7978845608028654
GELU_CUBIC = 0.044715
BLOCK = 256
AXES = ("dp", "expert", "fsdp")
F32 = jnp.float32
BF16 = jnp.bfloat16
VMEM_BYTES = 60 << 20


def dot_nn(left, right):
    return lax.dot_general(left, right, (((1,), (0,)), ((), ())), preferred_element_type=F32)


def dot_nt(left, right):
    return lax.dot_general(left, right, (((1,), (1,)), ((), ())), preferred_element_type=F32)


def dot_tn(left, right):
    return lax.dot_general(left, right, (((0,), (0,)), ((), ())), preferred_element_type=F32)


def normalize(values):
    center = values - jnp.mean(values, -1, keepdims=True)
    spread = lax.rsqrt(jnp.mean(center * center, -1, keepdims=True) + EPSILON)
    return center * spread, spread


def fold_rows(values, combine):
    rows, columns = values.shape
    return combine(values.reshape(rows // 8, 8, columns), 0)


def pick_slots(table_ref, slot, picks, width, span):
    experts = slot.shape[0]
    picked = []
    for pick in range(picks):
        value = table_ref[pick * width : (pick + 1) * width, :]
        for expert in range(pick + 1, experts - picks + pick + 1):
            hit = jnp.broadcast_to(slot[expert : expert + 1, :], (width, span)) == pick
            value = jnp.where(hit, table_ref[expert * width : (expert + 1) * width, :], value)
        picked.append(value)
    return picked


def spread_slots(read, slot, expert, picks, width, span):
    experts = slot.shape[0]
    row = jnp.broadcast_to(slot[expert : expert + 1, :], (width, span))
    value = jnp.zeros((width, span), F32)
    for pick in range(max(0, expert - experts + picks), min(expert, picks - 1) + 1):
        value = jnp.where(row == pick, read(pick), value)
    return value


def forward_kernel(
    lens,
    x_ref,
    route_ref,
    vec_ref,
    w_ref,
    hid_ref,
    kaug_ref,
    vaug_ref,
    kt_ref,
    q_ref,
    ctx_ref,
    lse_ref,
    gate_ref,
    slot_ref,
    table,
    qaug,
    scores,
    vt,
    acc,
):
    block = pl.program_id(1)
    length = lens[pl.program_id(0)]
    span = x_ref.shape[2]
    experts = slot_ref.shape[2]
    picks = route_ref.shape[2]
    width = kt_ref.shape[3]
    half = w_ref.shape[2]
    rows = picks * span

    normed, _ = normalize(x_ref[0, 0].astype(F32))
    hid = (normed * vec_ref[0:1, :] + vec_ref[1:2, :]).astype(BF16)
    hid_ref[0, 0] = hid
    table[...] = dot_nt(w_ref[0], hid[:, :half]) + dot_nt(w_ref[1], hid[:, half:])
    head = experts * width
    kt_ref[0, 0, 0] = table[head : head + width, :].astype(BF16)
    vt[block] = table[head + width : head + 2 * width, :].astype(BF16)

    lane = lax.broadcasted_iota(jnp.int32, (span, 2 * width), 1)
    place = block * span + lax.broadcasted_iota(jnp.int32, (span, 2 * width), 0)
    ones = jnp.where(lane < width + 4, 1.0, 0.0)
    cut = jnp.where(place < length, 0.0, NEGATIVE)
    both = dot_nt(hid[:, :half], w_ref[0, head : head + 2 * width, :])
    both = both + dot_nt(hid[:, half:], w_ref[1, head : head + 2 * width, :])
    keys = jnp.where(lane < width, both, jnp.where(lane == width, cut, ones))
    kaug_ref[0, block] = keys.astype(BF16)
    vals = jnp.where(lane < width, pltpu.roll(both, width, 1), ones)
    vaug_ref[0, block] = vals.astype(BF16)

    logits = table[head + 2 * width : head + 2 * width + experts, :]
    expert_id = lax.broadcasted_iota(jnp.int32, (experts, span), 0)
    chosen = jnp.zeros((experts, span), F32)
    for pick in range(picks):
        chosen = jnp.where(expert_id == route_ref[0, 0, pick : pick + 1, :], 1.0, chosen)
    lower = jnp.where(
        lax.broadcasted_iota(jnp.int32, (experts, experts), 1)
        < lax.broadcasted_iota(jnp.int32, (experts, experts), 0),
        1.0,
        0.0,
    )
    slot = jnp.where(chosen > 0.0, dot_nn(lower, chosen), -1.0).astype(jnp.int32)
    slot_ref[0, 0] = slot
    masked = jnp.where(chosen > 0.0, logits, NEGATIVE)
    raised = jnp.where(chosen > 0.0, jnp.exp(masked - jnp.max(masked, 0, keepdims=True)), 0.0)
    gate_ref[0, 0] = raised / jnp.sum(raised, 0, keepdims=True)

    picked = pick_slots(table, slot, picks, width, span)
    for pick in range(picks):
        qaug[0:width, pick * span : (pick + 1) * span] = (
            picked[pick].astype(BF16) * (width**-0.5)
        ).astype(BF16)
    q_ref[0, 0] = qaug[0:width, :]
    side = lax.broadcasted_iota(jnp.int32, (width, rows), 0)
    qaug[width : 2 * width, :] = jnp.where(side == 0, 1.0, 0.0).astype(BF16)

    def score_step(at, top):
        part = dot_nn(kaug_ref[0, at], qaug[...])
        scores[at] = part
        return jnp.maximum(top, fold_rows(part, jnp.max))

    used = jnp.minimum(block, (length + span - 1) // span)
    top = lax.fori_loop(0, used, score_step, jnp.full((8, rows), NEGATIVE, F32))
    causal = lax.broadcasted_iota(jnp.int32, (span, rows), 0) <= (
        lax.broadcasted_iota(jnp.int32, (span, rows), 1) & (span - 1)
    )
    part = jnp.where(causal, dot_nn(kaug_ref[0, block], qaug[...]), NEGATIVE)
    top = jnp.maximum(top, fold_rows(part, jnp.max))
    top = jnp.max(top, 0, keepdims=True)
    raised = jnp.exp(part - top)
    acc[...] = dot_nn(vt[block], raised.astype(BF16))
    total = fold_rows(raised, jnp.sum)

    def value_step(at, total):
        raised = jnp.exp(scores[at] - top)
        acc[...] += dot_nn(vt[at], raised.astype(BF16))
        return total + fold_rows(raised, jnp.sum)

    total = lax.fori_loop(0, used, value_step, total)
    total = jnp.sum(total, 0, keepdims=True)
    ctx_ref[0, 0] = (acc[...] * (1.0 / total)).astype(BF16)
    lse_ref[0, 0] = top + jnp.log(total)


def middle_kernel(
    lens,
    ids,
    x_ref,
    ctx_ref,
    gate_ref,
    slot_ref,
    cot_ref,
    w_ref,
    vec_ref,
    up_ref,
    up_shift_ref,
    down_ref,
    out_ref,
    mid_ref,
    do_ref,
    delta_ref,
    gl_ref,
    small_ref,
    up_shift_grad_ref,
    *rest,
):
    *grad_refs, gated, cexp, table, down_acc, up_acc, wo_acc = rest
    micro = pl.program_id(0)
    block = pl.program_id(1)
    length = lens[micro]
    span = x_ref.shape[2]
    experts = slot_ref.shape[2]
    width = ctx_ref.shape[2]
    picks = ctx_ref.shape[3] // span
    head = experts * width
    half = w_ref.shape[2]
    first = (micro == 0) & (block == 0)
    last = (micro == pl.num_programs(0) - 1) & (block == pl.num_programs(1) - 1)

    @pl.when(first)
    def _():
        down_acc[...] = jnp.zeros_like(down_acc)
        up_acc[...] = jnp.zeros_like(up_acc)
        wo_acc[...] = jnp.zeros_like(wo_acc)
        small_ref[...] = jnp.zeros_like(small_ref)
        up_shift_grad_ref[...] = jnp.zeros_like(up_shift_grad_ref)

    slot = slot_ref[0, 0]
    gates = gate_ref[0, 0]
    gate = [
        jnp.sum(jnp.where(slot == pick, gates, 0.0), 0, keepdims=True) for pick in range(picks)
    ]
    for pick in range(picks):
        at = slice(pick * span, (pick + 1) * span)
        gated[:, at] = ctx_ref[0, 0, :, at].astype(F32) * gate[pick]
    for expert in range(experts):
        cexp[expert * width : (expert + 1) * width, :] = spread_slots(
            lambda pick: gated[:, pick * span : (pick + 1) * span],
            slot,
            expert,
            picks,
            width,
            span,
        ).astype(BF16)
    mixed = x_ref[0, 0].astype(F32) + jnp.concatenate(
        [dot_tn(cexp[...], w_ref[0]), dot_tn(cexp[...], w_ref[1])], 1
    )
    normed, spread = normalize(mixed)
    hid = (normed * vec_ref[2:3, :] + vec_ref[3:4, :]).astype(BF16)
    place = block * span + lax.broadcasted_iota(jnp.int32, (span, 1), 0)
    grad = jnp.where(place < length, cot_ref[0, 0], 0.0)
    grad_b = grad.astype(BF16)
    hid_t = hid.T
    out = mixed + vec_ref[4:5, :]
    back = jnp.zeros_like(mixed)
    hidden_units = up_ref.shape[1]
    step = min(hidden_units, 512)
    for at in range(0, hidden_units, step):
        cut = slice(at, at + step)
        pre = dot_nn(hid, up_ref[:, cut]) + up_shift_ref[:, cut]
        square = pre * pre
        bent = jnp.tanh(pre * (GELU_SCALE + (GELU_SCALE * GELU_CUBIC) * square))
        rise = 0.5 + 0.5 * bent
        active = (pre * rise).astype(BF16)
        slope = rise + (0.5 * pre) * (1.0 - bent * bent) * (
            GELU_SCALE + (3.0 * GELU_SCALE * GELU_CUBIC) * square
        )
        grad_pre = dot_nt(grad_b, down_ref[cut, :]) * slope
        grad_pre_b = grad_pre.astype(BF16)
        out = out + dot_nn(active, down_ref[cut, :])
        back = back + dot_nt(grad_pre_b, up_ref[:, cut])
        down_acc[cut, :] += dot_nn(active.T, grad_b)
        up_acc[:, cut] += dot_nn(hid_t, grad_pre_b)
        up_shift_grad_ref[:, cut] += fold_rows(grad_pre, jnp.sum)
    out_ref[0, 0] = out
    scaled = back * vec_ref[2:3, :]
    mid = grad + spread * (
        scaled
        - jnp.mean(scaled, -1, keepdims=True)
        - normed * jnp.mean(scaled * normed, -1, keepdims=True)
    )
    mid_ref[0, 0] = mid
    small_ref[0] += fold_rows(back * normed, jnp.sum)
    small_ref[1] += fold_rows(back, jnp.sum)
    small_ref[2] += fold_rows(grad_b.astype(F32), jnp.sum)

    mid_b = mid.astype(BF16)
    wo_acc[...] += dot_nt(mid_b.T, cexp[...])
    table[...] = dot_nt(w_ref[0], mid_b[:, :half]) + dot_nt(w_ref[1], mid_b[:, half:])
    picked = pick_slots(table, slot, picks, width, span)
    grad_gate = []
    for pick in range(picks):
        at = slice(pick * span, (pick + 1) * span)
        ctx = ctx_ref[0, 0, :, at].astype(F32)
        grad_gate.append(jnp.sum(picked[pick] * ctx, 0, keepdims=True))
        grad_ctx = (picked[pick] * gate[pick]).astype(BF16)
        do_ref[0, 0, :, at] = grad_ctx
        delta_ref[0, 0, :, at] = jnp.sum(grad_ctx.astype(F32) * ctx, 0, keepdims=True)
    average = gate[0] * grad_gate[0]
    for pick in range(1, picks):
        average = average + gate[pick] * grad_gate[pick]
    grad_logits = jnp.zeros((experts, span), F32)
    for pick in range(picks):
        grad_logits = jnp.where(
            slot == pick, gate[pick] * (grad_gate[pick] - average), grad_logits
        )
    gl_ref[0, 0] = grad_logits

    @pl.when(last)
    def _():
        if len(grad_refs) == 3:
            for ref, total in zip(grad_refs, (down_acc, up_acc, wo_acc)):
                ref[...] = total[...].astype(BF16)
            return
        targets = grad_refs[0].shape[0] * grad_refs[0].shape[1]
        up_rows = up_acc.shape[0] // (2 * targets)
        down_rows = down_acc.shape[0] // (2 * targets)

        def pack(ref, to, fro, shared, heads):
            at = pack_tiles(ref, to, 0, up_acc, shared * up_rows, up_rows, 0, up_acc.shape[1])
            at = pack_tiles(ref, to, at, down_acc, shared * down_rows, down_rows, 0, down_acc.shape[1])
            rows, columns = heads_chunk(wo_acc.shape[0], head, ref)
            pack_tiles(ref, to, at, wo_acc, heads * rows, rows, fro * columns, columns)

        for_targets(ids, grad_refs, pack)


def pack_tiles(ref, to, at, total, row, rows, column, columns):
    row = pl.multiple_of(row, rows)
    for lane in range(0, columns, 128):
        tile = total[pl.ds(row, rows), column + lane : column + lane + 128]
        ref[to[0], to[1], at : at + rows, :] = tile.astype(BF16)
        at += rows
    return at


def heads_chunk(model, head, ref):
    return model // (2 * ref.shape[0]), head // ref.shape[1]


def for_targets(ids, refs, pack):
    def body(dp_far, carry):
        dp = dp_far ^ ids[0]
        for z_far in range(refs[0].shape[1]):
            for f_far in range(2):
                f = ids[2] ^ f_far
                shared = (dp * refs[0].shape[1] + (z_far ^ ids[1])) * 2 + f
                pack(refs[f_far], (dp_far, z_far), z_far, shared, dp * 2 + f)
        return carry

    lax.fori_loop(0, refs[0].shape[0], body, 0)


def split_three(values):
    high = values.astype(BF16).astype(F32)
    rest = values - high
    middle = rest.astype(BF16).astype(F32)
    return high, middle, rest - middle


def backward_kernel(
    lens,
    ids,
    hid_ref,
    kaug_ref,
    vaug_ref,
    kt_ref,
    q_ref,
    lse_ref,
    do_ref,
    delta_ref,
    slot_ref,
    gl_ref,
    order_ref,
    r_ref,
    *rest,
):
    *grad_refs, qaug, daug, dq, dkt, dvt, w_acc = rest
    micro = pl.program_id(0)
    step = pl.program_id(1)
    blocks = pl.num_programs(1)
    block = blocks - 1 - step
    length = lens[micro]
    span = hid_ref.shape[2]
    experts = slot_ref.shape[2]
    width = q_ref.shape[2]
    rows = q_ref.shape[3]
    picks = rows // span
    head = experts * width

    @pl.when((micro == 0) & (step == 0))
    def _():
        w_acc[...] = jnp.zeros_like(w_acc)

    @pl.when(step == 0)
    def _():
        dkt[...] = jnp.zeros_like(dkt)
        dvt[...] = jnp.zeros_like(dvt)

    @pl.when(block * span >= length)
    def _():
        r_ref[...] = jnp.zeros_like(r_ref)

    @pl.when(block * span < length)
    def _():
        side = lax.broadcasted_iota(jnp.int32, (width, rows), 0)
        qaug[0:width, :] = q_ref[0, 0]
        high, middle, low = split_three(-lse_ref[0, 0])
        qaug[width : 2 * width, :] = jnp.where(
            side == 0,
            1.0,
            jnp.where(side == 1, high, jnp.where(side == 2, middle, jnp.where(side == 3, low, 0.0))),
        ).astype(BF16)
        daug[0:width, :] = do_ref[0, 0]
        high, middle, low = split_three(-delta_ref[0, 0])
        daug[width : 2 * width, :] = jnp.where(
            side == 0, high, jnp.where(side == 1, middle, jnp.where(side == 2, low, 0.0))
        ).astype(BF16)

        def key_step(at, probs):
            probs_b = probs.astype(BF16)
            slopes = (probs * dot_nn(vaug_ref[0, at], daug[...])).astype(BF16)
            dvt[at] += dot_nt(daug[0:width, :], probs_b)
            dkt[at] += dot_nt(qaug[0:width, :], slopes)
            return dot_nn(kt_ref[0, at], slopes)

        causal = lax.broadcasted_iota(jnp.int32, (span, rows), 0) <= (
            lax.broadcasted_iota(jnp.int32, (span, rows), 1) & (span - 1)
        )
        dq[...] = key_step(
            block, jnp.where(causal, jnp.exp(dot_nn(kaug_ref[0, block], qaug[...])), 0.0)
        )

        def body(at, carry):
            dq[...] += key_step(at, jnp.exp(dot_nn(kaug_ref[0, at], qaug[...])))
            return carry

        lax.fori_loop(0, block, body, 0)
        dq[...] = dq[...] * (width**-0.5)
        slot = slot_ref[0, 0]
        for expert in range(experts):
            r_ref[0, 0, expert * width : (expert + 1) * width, :] = spread_slots(
                lambda pick: dq[:, pick * span : (pick + 1) * span],
                slot,
                expert,
                picks,
                width,
                span,
            ).astype(BF16)
        r_ref[0, 0, head : head + width, :] = dkt[block].astype(BF16)
        r_ref[0, 0, head + width : head + 2 * width, :] = dvt[block].astype(BF16)
        tail = r_ref.shape[2] - head - 2 * width
        r_ref[0, 0, head + 2 * width :, :] = jnp.concatenate(
            [gl_ref[0, 0], jnp.zeros((tail - experts, span), F32)], 0
        ).astype(BF16)
        w_acc[:, : r_ref.shape[2]] += dot_nt(hid_ref[0, 0].T, r_ref[0, 0])

    @pl.when((micro == pl.num_programs(0) - 1) & (step == blocks - 1))
    def _():
        if len(grad_refs) == 1:
            grad_refs[0][...] = w_acc[:, : r_ref.shape[2]].astype(BF16)
            return
        routed = head + 2 * width
        spare = order_ref.shape[0]
        w_acc[:, routed:] = dot_nn(
            w_acc[:, routed : routed + spare].astype(BF16), order_ref[...]
        )
        targets = grad_refs[0].shape[0] * grad_refs[0].shape[1]
        shared_rows = w_acc.shape[0] // (2 * targets)

        def pack(ref, to, fro, shared, heads):
            rows, columns = heads_chunk(w_acc.shape[0], head, ref)
            at = pack_tiles(ref, to, 0, w_acc, heads * rows, rows, fro * columns, columns)
            pack_tiles(ref, to, at, w_acc, shared * shared_rows, shared_rows, head, w_acc.shape[1] - head)

        for_targets(ids, grad_refs, pack)


def input_kernel(x_ref, mid_ref, r_ref, w_ref, vec_ref, out_ref, small_ref):
    first = (pl.program_id(0) == 0) & (pl.program_id(1) == 0)

    @pl.when(first)
    def _():
        small_ref[...] = jnp.zeros_like(small_ref)

    back = jnp.concatenate(
        [dot_tn(r_ref[0, 0], w_ref[0]), dot_tn(r_ref[0, 0], w_ref[1])], 1
    )
    normed, spread = normalize(x_ref[0, 0].astype(F32))
    scaled = back * vec_ref[0:1, :]
    out_ref[0, 0] = mid_ref[0, 0] + spread * (
        scaled
        - jnp.mean(scaled, -1, keepdims=True)
        - normed * jnp.mean(scaled * normed, -1, keepdims=True)
    )
    small_ref[0] += fold_rows(back * normed, jnp.sum)
    small_ref[1] += fold_rows(back, jnp.sum)


def full(shape):
    return pl.BlockSpec(shape, lambda *ids: (0,) * len(shape))


def blocked(shape):
    tail = (0,) * (len(shape) - 2)
    return pl.BlockSpec((1, 1) + tuple(shape[2:]), lambda m, i, *refs: (m, i) + tail)


def reversed_blocks(shape):
    tail = (0,) * (len(shape) - 2)
    last = shape[1] - 1
    return pl.BlockSpec((1, 1) + tuple(shape[2:]), lambda m, i, *refs: (m, last - i) + tail)


def whole(shape):
    tail = (0,) * (len(shape) - 1)
    return pl.BlockSpec((1,) + tuple(shape[1:]), lambda m, i, *refs: (m,) + tail)


def struct(shape, dtype):
    return jax.ShapeDtypeStruct(shape, dtype)


def params():
    return pltpu.CompilerParams(
        dimension_semantics=("arbitrary", "arbitrary"), vmem_limit_bytes=VMEM_BYTES
    )


def cost(flops, transcendentals, moved):
    return pl.CostEstimate(flops=flops, transcendentals=transcendentals, bytes_accessed=moved)


def exchange(value, axis, distance):
    count = lax.axis_size(axis)
    return lax.ppermute(value, axis, [(at, at ^ distance) for at in range(count)])


def permute_groups(value, index):
    groups = value.shape[0]
    bit = 1
    while bit < groups:
        pairs = value.reshape((groups // (2 * bit), 2, bit) + value.shape[1:])
        value = jnp.where((index & bit) != 0, pairs[:, ::-1].reshape(value.shape), value)
        bit *= 2
    return value


def pick_at(value, index, dim):
    return lax.dynamic_index_in_dim(value, index, dim, keepdims=False)


def reduce_axis(value, axis, dim, relative=False, keep=False):
    count = lax.axis_size(axis)
    me = lax.axis_index(axis)
    base = 0 if relative else me
    total = pick_at(value, base, dim).astype(F32)
    for distance in range(1, count):
        sent = pick_at(value, distance if relative else me ^ distance, dim)
        total = total + exchange(sent, axis, distance).astype(F32)
    return total if keep else total.astype(BF16)


def core_stage(grads):
    keep, send = grads
    other = exchange(send, "fsdp", 1)
    return [(keep[at].astype(F32) + other[at].astype(F32)).astype(BF16) for at in range(keep.shape[0])]


def split_targets(value, axis):
    return [value[at] for at in range(lax.axis_size(axis))]


def send_stage(parts, axis):
    return [exchange(parts[distance], axis, distance) for distance in range(1, len(parts))]


def total_up(own, received):
    total = own.astype(F32)
    for part in received:
        total = total + part.astype(F32)
    return total


def add_up(own, received):
    return total_up(own, received).astype(BF16)


def open_tiles(value, at, rows, columns):
    count = columns // 128
    tiles = value[at : at + count * rows].reshape(count, rows, 128)
    return jnp.swapaxes(tiles, 0, 1).reshape(rows, columns), at + count * rows


def sum_packed(parts, devices):
    packed = jnp.concatenate(parts, 1)
    packed = lax.all_to_all(packed, AXES, split_axis=0, concat_axis=0, tiled=True)
    packed = jnp.sum(packed.reshape(devices, -1), 0)
    result, at = [], 0
    for part in parts:
        result.append(packed[at : at + part.shape[1]])
        at += part.shape[1]
    return result


def local(
    inputs,
    lengths,
    routes,
    ln1_gain,
    ln1_bias,
    kv_weight,
    router_weight,
    query_weight,
    out_weight,
    ln2_gain,
    ln2_bias,
    up_weight,
    up_bias,
    down_weight,
    down_bias,
    out_cotangent,
):
    micro_count, _, slots, model = inputs.shape
    experts = router_weight.shape[2]
    width = query_weight.shape[3]
    picks = routes.shape[4]
    hidden_units = up_weight.shape[2]
    dp_size, z_size, f_size = (lax.axis_size(axis) for axis in AXES)
    dp_at, z_at, f_at = (lax.axis_index(axis) for axis in AXES)
    ids = jnp.stack([dp_at, z_at, f_at]).astype(jnp.int32)
    seq_index = (dp_at * z_size + z_at) * f_size + f_at
    devices = dp_size * z_size * f_size
    own_experts = experts // z_size
    half = model // f_size
    span = min(BLOCK, slots)
    blocks = slots // span
    rows = picks * span
    head = experts * width
    spare = -(-experts // 16) * 16
    all_rows = head + 2 * width + spare
    chunk = model // devices
    aligned = chunk % 16 == 0 and (head // z_size) % 128 == 0
    lens = lax.dynamic_index_in_dim(lengths, seq_index, 1, keepdims=False)

    def both_halves(own, other, dim):
        near = jnp.concatenate([own, other], dim)
        return jnp.where(f_at == 0, near, jnp.concatenate([other, own], dim))

    def head_parts(own):
        return [own] + [exchange(own, "expert", distance) for distance in range(1, z_size)]

    def transposed(weight):
        return jnp.swapaxes(weight[0], 1, 2).reshape(own_experts * width, half)

    query_parts = head_parts(transposed(query_weight))
    router_t = router_weight[0].T.reshape(z_size, own_experts, half)
    router_t = permute_groups(router_t, z_at).reshape(experts, half)
    router_t = jnp.pad(router_t, ((0, spare - experts), (0, 0)))
    proj = jnp.concatenate(query_parts + [kv_weight[0].T, router_t], 0)
    proj_other = exchange(proj, "fsdp", 1)
    proj = both_halves(proj[None], proj_other[None], 0)
    vectors = jnp.concatenate([ln1_gain, ln1_bias, ln2_gain, ln2_bias, down_bias], 0)
    small = jnp.concatenate([vectors, up_bias.reshape(-1, half)], 0)
    small_other = exchange(small, "fsdp", 1)
    vectors = both_halves(vectors, small_other[:5], 1).astype(F32)
    up_shift = both_halves(up_bias, small_other[5:].reshape(1, -1), 1).astype(F32)

    own_out, proj = lax.optimization_barrier((transposed(out_weight), proj))
    out_parts = head_parts(own_out)
    up_full = lax.all_gather(up_weight[0], "fsdp", axis=0, tiled=True)
    down_full = lax.all_gather(down_weight[0], "fsdp", axis=0, tiled=True)

    local_routes = routes[0, :, 0]
    local_routes = ((local_routes // own_experts) ^ z_at) * own_experts + local_routes % own_experts
    route_t = jnp.swapaxes(local_routes.reshape(micro_count, blocks, span, picks), 2, 3)
    states = inputs.reshape(micro_count, blocks, span, model)
    cotangent = out_cotangent.reshape(micro_count, blocks, span, model)

    grid = (micro_count, blocks)
    hid_s = struct((micro_count, blocks, span, model), BF16)
    aug_s = struct((micro_count, blocks, span, 2 * width), BF16)
    kt_s = struct((micro_count, blocks, 1, width, span), BF16)
    q_s = struct((micro_count, blocks, width, rows), BF16)
    row_s = struct((micro_count, blocks, 1, rows), F32)
    gate_s = struct((micro_count, blocks, experts, span), F32)
    slot_s = struct((micro_count, blocks, experts, span), jnp.int32)
    tokens = micro_count * slots
    pair_flops = tokens * picks * slots * width
    hid, kaug, vaug, kt, q, ctx, lse, gates, slot = pl.pallas_call(
        forward_kernel,
        name="forward",
        grid_spec=pltpu.PrefetchScalarGridSpec(
            num_scalar_prefetch=1,
            grid=grid,
            in_specs=[
                blocked(states.shape),
                blocked(route_t.shape),
                full(vectors.shape),
                full(proj.shape),
            ],
            out_specs=[
                blocked(hid_s.shape),
                whole(aug_s.shape),
                whole(aug_s.shape),
                blocked(kt_s.shape),
                blocked(q_s.shape),
                blocked(q_s.shape),
                blocked(row_s.shape),
                blocked(gate_s.shape),
                blocked(slot_s.shape),
            ],
            scratch_shapes=[
                pltpu.VMEM((all_rows, span), F32),
                pltpu.VMEM((2 * width, rows), BF16),
                pltpu.VMEM((blocks, span, rows), F32),
                pltpu.VMEM((blocks, width, span), BF16),
                pltpu.VMEM((width, rows), F32),
            ],
        ),
        out_shape=[hid_s, aug_s, aug_s, kt_s, q_s, q_s, row_s, gate_s, slot_s],
        compiler_params=params(),
        cost_estimate=cost(2 * tokens * model * all_rows + 16 * pair_flops, 0, 64 << 20),
    )(lens, states, route_t, vectors, proj)

    ctx, up_full, down_full, *out_parts = lax.optimization_barrier(
        (ctx, up_full, down_full, *out_parts)
    )
    out_proj = jnp.concatenate(out_parts, 0)[None]
    out_proj = both_halves(out_proj, exchange(out_proj, "fsdp", 1), 0)
    state_s = struct((micro_count, blocks, span, model), F32)
    mid_rows = chunk * hidden_units * 2 // 128 + head // z_size * (chunk * z_size) // 128
    late_rows = head // z_size * (chunk * z_size) // 128 + 2 * chunk
    if aligned:
        mid_grads = [struct((dp_size, z_size, mid_rows, 128), BF16)] * 2
        late_grads = [struct((dp_size, z_size, late_rows, 128), BF16)] * 2
    else:
        mid_grads = [
            struct((hidden_units, model), BF16),
            struct((model, hidden_units), BF16),
            struct((model, head), BF16),
        ]
        late_grads = [struct((model, all_rows), BF16)]
    outputs, mid, grad_ctx, delta, grad_logits, small2, up_small, *mid_grads = pl.pallas_call(
        middle_kernel,
        name="middle",
        grid_spec=pltpu.PrefetchScalarGridSpec(
            num_scalar_prefetch=2,
            grid=grid,
            in_specs=[
                blocked(states.shape),
                blocked(q_s.shape),
                blocked(gate_s.shape),
                blocked(slot_s.shape),
                blocked(cotangent.shape),
                full(out_proj.shape),
                full(vectors.shape),
                full(up_full.shape),
                full(up_shift.shape),
                full(down_full.shape),
            ],
            out_specs=[
                blocked(state_s.shape),
                blocked(state_s.shape),
                blocked(q_s.shape),
                blocked(row_s.shape),
                blocked(gate_s.shape),
                full((3, 8, model)),
                full((8, hidden_units)),
            ]
            + [full(leaf.shape) for leaf in mid_grads],
            scratch_shapes=[
                pltpu.VMEM((width, rows), F32),
                pltpu.VMEM((head, span), BF16),
                pltpu.VMEM((head, span), F32),
                pltpu.VMEM((hidden_units, model), F32),
                pltpu.VMEM((model, hidden_units), F32),
                pltpu.VMEM((model, head), F32),
            ],
        ),
        out_shape=[
            state_s,
            state_s,
            q_s,
            row_s,
            gate_s,
            struct((3, 8, model), F32),
            struct((8, hidden_units), F32),
        ]
        + mid_grads,
        compiler_params=params(),
        cost_estimate=cost(2 * tokens * model * (6 * hidden_units + 3 * head), 0, 200 << 20),
    )(
        lens,
        ids,
        states,
        ctx,
        gates,
        slot,
        cotangent,
        out_proj,
        vectors,
        up_full,
        up_shift,
        down_full,
    )

    if aligned:
        mid_sums = core_stage(mid_grads)
        grad_ctx, *mid_sums = lax.optimization_barrier((grad_ctx, *mid_sums))
        mid_received = send_stage(mid_sums, "dp")

    expert_id = jnp.arange(experts)
    moved = ((expert_id // own_experts) ^ z_at) * own_experts + expert_id % own_experts
    order = jnp.pad(
        (jnp.arange(spare)[:, None] == moved[None, :]).astype(BF16), ((0, 0), (0, 128 - experts))
    )
    r_s = struct((micro_count, blocks, all_rows, span), BF16)
    routed, *late_grads = pl.pallas_call(
        backward_kernel,
        name="backward",
        grid_spec=pltpu.PrefetchScalarGridSpec(
            num_scalar_prefetch=2,
            grid=grid,
            in_specs=[
                reversed_blocks(hid_s.shape),
                whole(aug_s.shape),
                whole(aug_s.shape),
                whole((micro_count, blocks, width, span)),
                reversed_blocks(q_s.shape),
                reversed_blocks(row_s.shape),
                reversed_blocks(q_s.shape),
                reversed_blocks(row_s.shape),
                reversed_blocks(slot_s.shape),
                reversed_blocks(gate_s.shape),
                full(order.shape),
            ],
            out_specs=[reversed_blocks(r_s.shape)] + [full(leaf.shape) for leaf in late_grads],
            scratch_shapes=[
                pltpu.VMEM((2 * width, rows), BF16),
                pltpu.VMEM((2 * width, rows), BF16),
                pltpu.VMEM((width, rows), F32),
                pltpu.VMEM((blocks, width, span), F32),
                pltpu.VMEM((blocks, width, span), F32),
                pltpu.VMEM((model, head + 2 * width + 128), F32),
            ],
        ),
        out_shape=[r_s] + late_grads,
        compiler_params=params(),
        cost_estimate=cost(2 * tokens * model * all_rows + 40 * pair_flops, 0, 100 << 20),
    )(
        lens,
        ids,
        hid,
        kaug,
        vaug,
        kt.reshape(micro_count, blocks, width, span),
        q,
        lse,
        grad_ctx,
        delta,
        slot,
        grad_logits,
        order,
    )

    if aligned:
        *mid_received, late_grads[0], late_grads[1] = lax.optimization_barrier(
            (*mid_received, *late_grads)
        )
        late_sums = core_stage(late_grads)
        mid_sums = split_targets(add_up(mid_sums[0], mid_received), "expert")
        routed, *late_sums = lax.optimization_barrier((routed, *late_sums))
        late_received = send_stage(late_sums, "dp")
        mid_received = send_stage(mid_sums, "expert")

    input_grad, small1 = pl.pallas_call(
        input_kernel,
        name="input_back",
        grid_spec=pltpu.PrefetchScalarGridSpec(
            num_scalar_prefetch=0,
            grid=grid,
            in_specs=[
                blocked(states.shape),
                blocked(state_s.shape),
                blocked(r_s.shape),
                full(proj.shape),
                full(vectors.shape),
            ],
            out_specs=[blocked(state_s.shape), full((2, 8, model))],
        ),
        out_shape=[state_s, struct((2, 8, model), F32)],
        compiler_params=params(),
        cost_estimate=cost(2 * tokens * model * all_rows, 0, 40 << 20),
    )(states, mid, routed, proj, vectors)

    if aligned:
        small1, *received = lax.optimization_barrier((small1, *late_received, *mid_received))
        late_received = received[: dp_size - 1]
        mid_received = received[dp_size - 1 :]
    small = jnp.concatenate([jnp.sum(small1, 1), jnp.sum(small2, 1)], 0)
    small = jnp.swapaxes(small.reshape(5, devices, chunk), 0, 1).reshape(devices, 5 * chunk)
    up_small = jnp.sum(up_small, 0).reshape(devices, hidden_units // devices)
    packed = [small, up_small]

    def open_heads(value):
        return jnp.swapaxes(value.reshape(-1, own_experts, width), 0, 1)[None]

    if aligned:
        late_sums = split_targets(add_up(late_sums[0], late_received), "expert")
        late_received = send_stage(late_sums, "expert")
        mid_total = total_up(mid_sums[0], mid_received)
        up_weight_grad, at = open_tiles(mid_total, 0, chunk, hidden_units)
        down_weight_grad, at = open_tiles(mid_total, at, hidden_units // devices, model)
        out_weight_grad, at = open_tiles(mid_total, at, chunk * z_size, head // z_size)
        packed = sum_packed(packed, devices)
        late_total = total_up(late_sums[0], late_received)
        query_weight_grad, at = open_tiles(late_total, 0, chunk * z_size, head // z_size)
        kv_grad = late_total[at : at + chunk]
        router_grad = late_total[at + chunk : at + 2 * chunk, :experts]
        query_weight_grad, out_weight_grad = map(open_heads, (query_weight_grad, out_weight_grad))
    else:
        down_grad, up_grad, wo_grad = mid_grads
        w_grad = late_grads[0]

        def reduce_shared(value, part):
            value = value.reshape(dp_size, z_size, f_size, part, value.shape[1])
            value = reduce_axis(value, "fsdp", 2)
            value = reduce_axis(value, "dp", 0)
            return reduce_axis(value, "expert", 0, keep=True)

        def reduce_heads(value):
            value = value.reshape(dp_size, f_size, chunk * z_size, z_size, own_experts * width)
            value = reduce_axis(value, "fsdp", 1)
            value = reduce_axis(value, "dp", 0)
            return open_heads(reduce_axis(value, "expert", 1, relative=True, keep=True))

        up_weight_grad = reduce_shared(up_grad, chunk)
        down_weight_grad = reduce_shared(down_grad, hidden_units // devices)
        out_weight_grad = reduce_heads(wo_grad)
        query_weight_grad = reduce_heads(w_grad[:, :head])
        router_grad = w_grad[:, head + 2 * width : head + 2 * width + experts].astype(F32)
        router_grad = permute_groups(router_grad.T.reshape(z_size, own_experts, model), z_at)
        router_grad = router_grad.reshape(experts, model).T
        kv_grad = w_grad[:, head : head + 2 * width].astype(F32)
        packed += [kv_grad.reshape(devices, -1), router_grad.reshape(devices, -1)]
        packed = sum_packed(packed, devices)
        kv_grad = packed[2].reshape(chunk, 2 * width)
        router_grad = packed[3].reshape(chunk, experts)
    small = packed[0].reshape(5, 1, chunk)
    shape = (micro_count, 1, slots, model)
    return (
        outputs.reshape(shape),
        input_grad.reshape(shape),
        small[0],
        small[1],
        kv_grad[None],
        router_grad[None],
        query_weight_grad,
        out_weight_grad,
        small[2],
        small[3],
        up_weight_grad[None],
        packed[1][None],
        down_weight_grad[None],
        small[4],
    )


def solution(mesh):
    shards = P(None, AXES, None, None)
    return jax.shard_map(
        local,
        mesh=mesh,
        in_specs=(
            shards,
            P(),
            P(None, None, AXES, None, None),
            P(None, "fsdp"),
            P(None, "fsdp"),
            P(None, "fsdp", None),
            P(None, "fsdp", None),
            P(None, "expert", "fsdp", None),
            P(None, "expert", "fsdp", None),
            P(None, "fsdp"),
            P(None, "fsdp"),
            P(None, "fsdp", None),
            P(None, "fsdp"),
            P(None, "fsdp", None),
            P(None, "fsdp"),
            shards,
        ),
        out_specs=(
            shards,
            shards,
            P(None, AXES),
            P(None, AXES),
            P(None, AXES, None),
            P(None, AXES, None),
            P(None, "expert", ("dp", "fsdp"), None),
            P(None, "expert", ("dp", "fsdp"), None),
            P(None, AXES),
            P(None, AXES),
            P(None, AXES, None),
            P(None, AXES),
            P(None, AXES, None),
            P(None, AXES),
        ),
        check_vma=False,
    )
```

```python
import functools

import jax
import jax.numpy as jnp
from jax import lax
from jax.experimental import pallas as pl
from jax.experimental.pallas import tpu as pltpu
from jax.sharding import PartitionSpec as P

EPSILON = 1e-05
NEGATIVE = -1e30
GELU_SCALE = 0.7978845608028654
GELU_CUBIC = 0.044715
BLOCK = 256
AXES = ("dp", "expert", "fsdp")
F32 = jnp.float32
BF16 = jnp.bfloat16
VMEM_BYTES = 60 << 20


def dot_nn(left, right):
    return lax.dot_general(left, right, (((1,), (0,)), ((), ())), preferred_element_type=F32)


def dot_nt(left, right):
    return lax.dot_general(left, right, (((1,), (1,)), ((), ())), preferred_element_type=F32)


def dot_tn(left, right):
    return lax.dot_general(left, right, (((0,), (0,)), ((), ())), preferred_element_type=F32)


def normalize(values):
    center = values - jnp.mean(values, -1, keepdims=True)
    spread = lax.rsqrt(jnp.mean(center * center, -1, keepdims=True) + EPSILON)
    return center * spread, spread


def halves(ref):
    rows = ref.shape[0] // 2
    return ref.at[pl.ds(0, rows)], ref.at[pl.ds(rows, rows)]


def fold_rows(values, combine):
    rows, columns = values.shape
    return combine(values.reshape(rows // 8, 8, columns), 0)


def pick_slots(table_ref, slot, picks, width, start=0):
    experts, span = slot.shape
    lanes = slice(start, start + span)
    picked = []
    for pick in range(picks):
        value = table_ref[pick * width : (pick + 1) * width, lanes]
        for expert in range(pick + 1, experts - picks + pick + 1):
            hit = jnp.broadcast_to(slot[expert : expert + 1, :], (width, span)) == pick
            value = jnp.where(hit, table_ref[expert * width : (expert + 1) * width, lanes], value)
        picked.append(value)
    return picked


def spread_slots(read, slot, expert, picks, width, span):
    experts = slot.shape[0]
    row = jnp.broadcast_to(slot[expert : expert + 1, :], (width, span))
    value = jnp.zeros((width, span), F32)
    for pick in range(max(0, expert - experts + picks), min(expert, picks - 1) + 1):
        value = jnp.where(row == pick, read(pick), value)
    return value


def forward_kernel(
    lens,
    ids,
    x_ref,
    route_ref,
    vec_ref,
    own_ref,
    other_ref,
    hid_ref,
    kaug_ref,
    vaug_ref,
    kt_ref,
    q_ref,
    ctx_ref,
    lse_ref,
    gate_ref,
    slot_ref,
    table,
    qaug,
    scores,
    vt,
    acc,
    w_ref,
    sems,
):
    block = pl.program_id(1)
    length = lens[pl.program_id(0)]
    first = (pl.program_id(0) == 0) & (block == 0)
    load_halves(first, ids[2], sems, [(own_ref, other_ref, w_ref)])
    span = x_ref.shape[2]
    experts = slot_ref.shape[2]
    picks = route_ref.shape[2]
    width = kt_ref.shape[3]
    half = w_ref.shape[1]
    low, high = halves(w_ref)
    rows = picks * span

    normed, _ = normalize(x_ref[0, 0].astype(F32))
    hid = (normed * vec_ref[0:1, :] + vec_ref[1:2, :]).astype(BF16)
    hid_ref[0, 0] = hid
    table[...] = dot_nt(low[...], hid[:, :half]) + dot_nt(high[...], hid[:, half:])
    head = experts * width
    kt_ref[0, 0, 0] = table[head : head + width, :].astype(BF16)
    vt[block] = table[head + width : head + 2 * width, :].astype(BF16)

    lane = lax.broadcasted_iota(jnp.int32, (span, 2 * width), 1)
    place = block * span + lax.broadcasted_iota(jnp.int32, (span, 2 * width), 0)
    ones = jnp.where(lane < width + 4, 1.0, 0.0)
    cut = jnp.where(place < length, 0.0, NEGATIVE)
    both = dot_nt(hid[:, :half], low[head : head + 2 * width, :])
    both = both + dot_nt(hid[:, half:], high[head : head + 2 * width, :])
    keys = jnp.where(lane < width, both, jnp.where(lane == width, cut, ones))
    kaug_ref[0, block] = keys.astype(BF16)
    vals = jnp.where(lane < width, pltpu.roll(both, width, 1), ones)
    vaug_ref[0, block] = vals.astype(BF16)

    logits = table[head + 2 * width : head + 2 * width + experts, :]
    expert_id = lax.broadcasted_iota(jnp.int32, (experts, span), 0)
    chosen = jnp.zeros((experts, span), F32)
    for pick in range(picks):
        chosen = jnp.where(expert_id == route_ref[0, 0, pick : pick + 1, :], 1.0, chosen)
    lower = jnp.where(
        lax.broadcasted_iota(jnp.int32, (experts, experts), 1)
        < lax.broadcasted_iota(jnp.int32, (experts, experts), 0),
        1.0,
        0.0,
    )
    slot = jnp.where(chosen > 0.0, dot_nn(lower, chosen), -1.0).astype(jnp.int32)
    slot_ref[0, 0] = slot
    masked = jnp.where(chosen > 0.0, logits, NEGATIVE)
    raised = jnp.where(chosen > 0.0, jnp.exp(masked - jnp.max(masked, 0, keepdims=True)), 0.0)
    gate_ref[0, 0] = raised / jnp.sum(raised, 0, keepdims=True)

    picked = pick_slots(table, slot, picks, width)
    for pick in range(picks):
        qaug[0:width, pick * span : (pick + 1) * span] = (
            picked[pick].astype(BF16) * (width**-0.5)
        ).astype(BF16)
    q_ref[0, 0] = qaug[0:width, :]
    side = lax.broadcasted_iota(jnp.int32, (width, rows), 0)
    qaug[width : 2 * width, :] = jnp.where(side == 0, 1.0, 0.0).astype(BF16)

    def score_step(at, top):
        part = dot_nn(kaug_ref[0, at], qaug[...])
        scores[at] = part
        return jnp.maximum(top, fold_rows(part, jnp.max))

    used = jnp.minimum(block, (length + span - 1) // span)
    top = lax.fori_loop(0, used, score_step, jnp.full((8, rows), NEGATIVE, F32))
    causal = lax.broadcasted_iota(jnp.int32, (span, rows), 0) <= (
        lax.broadcasted_iota(jnp.int32, (span, rows), 1) & (span - 1)
    )
    part = jnp.where(causal, dot_nn(kaug_ref[0, block], qaug[...]), NEGATIVE)
    top = jnp.maximum(top, fold_rows(part, jnp.max))
    top = jnp.max(top, 0, keepdims=True)
    raised = jnp.exp(part - top)
    acc[...] = dot_nn(vt[block], raised.astype(BF16))
    total = fold_rows(raised, jnp.sum)

    def value_step(at, total):
        raised = jnp.exp(scores[at] - top)
        acc[...] += dot_nn(vt[at], raised.astype(BF16))
        return total + fold_rows(raised, jnp.sum)

    total = lax.fori_loop(0, used, value_step, total)
    total = jnp.sum(total, 0, keepdims=True)
    ctx_ref[0, 0] = (acc[...] * (1.0 / total)).astype(BF16)
    lse_ref[0, 0] = top + jnp.log(total)


def middle_kernel(
    lens,
    ids,
    x_ref,
    ctx_ref,
    gate_ref,
    slot_ref,
    cot_ref,
    own_ref,
    other_ref,
    vec_ref,
    own_up_ref,
    other_up_ref,
    up_shift_ref,
    own_down_ref,
    other_down_ref,
    out_ref,
    mid_ref,
    do_ref,
    delta_ref,
    gl_ref,
    small_ref,
    up_shift_grad_ref,
    *rest,
):
    *grad_refs, gated, cexp, table, down_acc, up_acc, wo_acc, w_ref, up_ref, down_ref, sems = rest
    micro = pl.program_id(0)
    block = pl.program_id(1)
    length = lens[micro]
    subs, span, model = x_ref.shape[1:]
    tokens = subs * span
    experts = slot_ref.shape[2]
    width = ctx_ref.shape[2]
    picks = ctx_ref.shape[3] // span
    head = experts * width
    half = w_ref.shape[1]
    low, high = halves(w_ref)
    first = (micro == 0) & (block == 0)
    last = (micro == pl.num_programs(0) - 1) & (block == pl.num_programs(1) - 1)

    def clear():
        down_acc[...] = jnp.zeros_like(down_acc)
        up_acc[...] = jnp.zeros_like(up_acc)
        wo_acc[...] = jnp.zeros_like(wo_acc)
        small_ref[...] = jnp.zeros_like(small_ref)
        up_shift_grad_ref[...] = jnp.zeros_like(up_shift_grad_ref)

    load_halves(
        first,
        ids[2],
        sems,
        [
            (own_ref, other_ref, w_ref),
            (own_up_ref, other_up_ref, up_ref),
            (own_down_ref, other_down_ref, down_ref),
        ],
        clear,
    )
    slots = [slot_ref[0, sub] for sub in range(subs)]
    gate = []
    for sub in range(subs):
        gates = gate_ref[0, sub]
        gate.append(
            [
                jnp.sum(jnp.where(slots[sub] == pick, gates, 0.0), 0, keepdims=True)
                for pick in range(picks)
            ]
        )
        for pick in range(picks):
            at = slice(pick * span, (pick + 1) * span)
            gated[sub, :, at] = ctx_ref[0, sub, :, at].astype(F32) * gate[sub][pick]
        for expert in range(experts):
            cexp[expert * width : (expert + 1) * width, sub * span : (sub + 1) * span] = spread_slots(
                lambda pick: gated[sub, :, pick * span : (pick + 1) * span],
                slots[sub],
                expert,
                picks,
                width,
                span,
            ).astype(BF16)
    mixed = x_ref[0].reshape(tokens, model).astype(F32) + jnp.concatenate(
        [dot_tn(cexp[...], low[...]), dot_tn(cexp[...], high[...])], 1
    )
    normed, spread = normalize(mixed)
    hid = (normed * vec_ref[2:3, :] + vec_ref[3:4, :]).astype(BF16)
    place = block * tokens + lax.broadcasted_iota(jnp.int32, (tokens, 1), 0)
    grad = jnp.where(place < length, cot_ref[0].reshape(tokens, model), 0.0)
    grad_b = grad.astype(BF16)
    hid_t = hid.T
    out = mixed + vec_ref[4:5, :]
    back = jnp.zeros_like(mixed)
    hidden_units = up_ref.shape[1]
    step = min(hidden_units, 256)
    cuts = [slice(at, at + step) for at in range(0, hidden_units, step)]

    def ahead(cut):
        return dot_nn(hid, up_ref[:, cut]), dot_nt(grad_b, down_ref[cut, :])

    held = ahead(cuts[0])
    ready = None
    for n in range(len(cuts) + 1):
        pre, grad_act = held if held is not None else (None, None)
        held = ahead(cuts[n + 1]) if n + 1 < len(cuts) else None
        fresh = None
        if n < len(cuts):
            cut = cuts[n]
            pre = pre + up_shift_ref[:, cut]
            square = pre * pre
            bent = jnp.tanh(pre * (GELU_SCALE + (GELU_SCALE * GELU_CUBIC) * square))
            rise = 0.5 + 0.5 * bent
            slope = rise + (0.5 * pre) * (1.0 - bent * bent) * (
                GELU_SCALE + (3.0 * GELU_SCALE * GELU_CUBIC) * square
            )
            grad_pre = grad_act * slope
            up_shift_grad_ref[:, cut] += fold_rows(grad_pre, jnp.sum)
            fresh = (cut, (pre * rise).astype(BF16), grad_pre.astype(BF16))
        if ready is not None:
            cut, active, grad_pre_b = ready
            out = out + dot_nn(active, down_ref[cut, :])
            back = back + dot_nt(grad_pre_b, up_ref[:, cut])
            down_acc[cut, :] += dot_nn(active.T, grad_b)
            up_acc[:, cut] += dot_nn(hid_t, grad_pre_b)
        ready = fresh
    out_ref[0] = out.reshape(subs, span, model)
    scaled = back * vec_ref[2:3, :]
    mid = grad + spread * (
        scaled
        - jnp.mean(scaled, -1, keepdims=True)
        - normed * jnp.mean(scaled * normed, -1, keepdims=True)
    )
    mid_ref[0] = mid.reshape(subs, span, model)
    small_ref[0] += fold_rows(back * normed, jnp.sum)
    small_ref[1] += fold_rows(back, jnp.sum)
    small_ref[2] += fold_rows(grad_b.astype(F32), jnp.sum)

    mid_b = mid.astype(BF16)
    wo_acc[...] += dot_nt(mid_b.T, cexp[...])
    table[...] = dot_nt(low[...], mid_b[:, :half]) + dot_nt(high[...], mid_b[:, half:])
    for sub in range(subs):
        slot = slots[sub]
        picked = pick_slots(table, slot, picks, width, sub * span)
        grad_gate = []
        for pick in range(picks):
            at = slice(pick * span, (pick + 1) * span)
            ctx = ctx_ref[0, sub, :, at].astype(F32)
            grad_gate.append(jnp.sum(picked[pick] * ctx, 0, keepdims=True))
            grad_ctx = (picked[pick] * gate[sub][pick]).astype(BF16)
            do_ref[0, sub, :, at] = grad_ctx
            delta_ref[0, sub, :, at] = jnp.sum(grad_ctx.astype(F32) * ctx, 0, keepdims=True)
        average = gate[sub][0] * grad_gate[0]
        for pick in range(1, picks):
            average = average + gate[sub][pick] * grad_gate[pick]
        grad_logits = jnp.zeros((experts, span), F32)
        for pick in range(picks):
            grad_logits = jnp.where(
                slot == pick, gate[sub][pick] * (grad_gate[pick] - average), grad_logits
            )
        gl_ref[0, sub] = grad_logits

    @pl.when(last)
    def _():
        if len(grad_refs) == 3:
            for ref, total in zip(grad_refs, (down_acc, up_acc, wo_acc)):
                ref[...] = total[...].astype(BF16)
            return
        targets = grad_refs[0].shape[0] * grad_refs[0].shape[1]
        up_rows = up_acc.shape[0] // (2 * targets)
        down_rows = down_acc.shape[0] // (2 * targets)

        def pack(ref, to, fro, shared, heads):
            at = pack_tiles(ref, to, 0, up_acc, shared * up_rows, up_rows, 0, up_acc.shape[1])
            at = pack_tiles(ref, to, at, down_acc, shared * down_rows, down_rows, 0, down_acc.shape[1])
            rows, columns = heads_chunk(wo_acc.shape[0], head, ref)
            pack_tiles(ref, to, at, wo_acc, heads * rows, rows, fro * columns, columns)

        for_targets(ids, grad_refs, pack)


def load_halves(first, core, sems, moves, meanwhile=lambda: None):
    @pl.when(first)
    def _():
        copies = []
        for own, other, target in moves:
            half = target.shape[0] // 2
            for source, at in ((own, core), (other, 1 - core)):
                place = target.at[pl.ds(pl.multiple_of(at * half, half), half)]
                copies.append(pltpu.make_async_copy(source, place, sems.at[len(copies)]))
        for copy in copies:
            copy.start()
        meanwhile()
        for copy in copies:
            copy.wait()


def pack_tiles(ref, to, at, total, row, rows, column, columns):
    row = pl.multiple_of(row, rows)
    for lane in range(0, columns, 128):
        start = column + lane
        if not isinstance(start, int):
            start = pl.multiple_of(start, 128)
        tile = total[pl.ds(row, rows), pl.ds(start, 128)]
        ref[to[0], to[1], at : at + rows, :] = tile.astype(BF16)
        at += rows
    return at


def heads_chunk(model, head, ref):
    return model // (2 * ref.shape[0]), head // ref.shape[1]


def for_targets(ids, refs, pack):
    def body(dp_far, carry):
        dp = dp_far ^ ids[0]
        for z_far in range(refs[0].shape[1]):
            for f_far in range(2):
                f = ids[2] ^ f_far
                shared = (dp * refs[0].shape[1] + (z_far ^ ids[1])) * 2 + f
                pack(refs[f_far], (dp_far, z_far), z_far, shared, dp * 2 + f)
        return carry

    lax.fori_loop(0, refs[0].shape[0], body, 0)


def split_three(values):
    high = values.astype(BF16).astype(F32)
    rest = values - high
    middle = rest.astype(BF16).astype(F32)
    return high, middle, rest - middle


def backward_kernel(
    lens,
    ids,
    hid_ref,
    kaug_ref,
    vaug_ref,
    kt_ref,
    q_ref,
    lse_ref,
    do_ref,
    delta_ref,
    slot_ref,
    gl_ref,
    order_ref,
    r_ref,
    *rest,
):
    *grad_refs, qaug, daug, dq, dkt, dvt, w_acc = rest
    micro = pl.program_id(0)
    step = pl.program_id(1)
    blocks = pl.num_programs(1)
    block = blocks - 1 - step
    length = lens[micro]
    span = hid_ref.shape[2]
    experts = slot_ref.shape[2]
    width = q_ref.shape[2]
    rows = q_ref.shape[3]
    picks = rows // span
    head = experts * width

    @pl.when((micro == 0) & (step == 0))
    def _():
        w_acc[...] = jnp.zeros_like(w_acc)

    @pl.when(step == 0)
    def _():
        dkt[...] = jnp.zeros_like(dkt)
        dvt[...] = jnp.zeros_like(dvt)

    @pl.when(block * span >= length)
    def _():
        r_ref[...] = jnp.zeros_like(r_ref)

    @pl.when(block * span < length)
    def _():
        side = lax.broadcasted_iota(jnp.int32, (width, rows), 0)
        qaug[0:width, :] = q_ref[0, 0]
        high, middle, low = split_three(-lse_ref[0, 0])
        qaug[width : 2 * width, :] = jnp.where(
            side == 0,
            1.0,
            jnp.where(side == 1, high, jnp.where(side == 2, middle, jnp.where(side == 3, low, 0.0))),
        ).astype(BF16)
        daug[0:width, :] = do_ref[0, 0]
        high, middle, low = split_three(-delta_ref[0, 0])
        daug[width : 2 * width, :] = jnp.where(
            side == 0, high, jnp.where(side == 1, middle, jnp.where(side == 2, low, 0.0))
        ).astype(BF16)

        lanes = 256
        causal = lax.broadcasted_iota(jnp.int32, (span, lanes), 0) <= (
            lax.broadcasted_iota(jnp.int32, (span, lanes), 1) & (span - 1)
        )

        def key_step(at, diagonal):
            dv = dvt[at]
            dk = dkt[at]
            cuts = [slice(start, start + lanes) for start in range(0, rows, lanes)]

            def ahead(cut):
                return dot_nn(kaug_ref[0, at], qaug[:, cut]), dot_nn(vaug_ref[0, at], daug[:, cut])

            held = ahead(cuts[0])
            back = None
            for n in range(len(cuts) + 1):
                scores, dprobs = held if held is not None else (None, None)
                held = ahead(cuts[n + 1]) if n + 1 < len(cuts) else None
                fresh = None
                if n < len(cuts):
                    probs = jnp.exp(scores)
                    if diagonal:
                        probs = jnp.where(causal, probs, 0.0)
                    slopes = (probs * dprobs).astype(BF16)
                    fresh = (cuts[n], probs.astype(BF16), slopes)
                if back is not None:
                    cut, probs_b, slopes = back
                    dv = dv + dot_nt(daug[0:width, cut], probs_b)
                    dk = dk + dot_nt(qaug[0:width, cut], slopes)
                    part = dot_nn(kt_ref[0, at], slopes)
                    dq[:, cut] = part if diagonal else dq[:, cut] + part
                back = fresh
            dvt[at] = dv
            dkt[at] = dk

        key_step(block, True)

        def body(at, carry):
            key_step(at, False)
            return carry

        lax.fori_loop(0, block, body, 0)
        dq[...] = dq[...] * (width**-0.5)
        slot = slot_ref[0, 0]
        for expert in range(experts):
            r_ref[0, 0, expert * width : (expert + 1) * width, :] = spread_slots(
                lambda pick: dq[:, pick * span : (pick + 1) * span],
                slot,
                expert,
                picks,
                width,
                span,
            ).astype(BF16)
        r_ref[0, 0, head : head + width, :] = dkt[block].astype(BF16)
        r_ref[0, 0, head + width : head + 2 * width, :] = dvt[block].astype(BF16)
        tail = r_ref.shape[2] - head - 2 * width
        r_ref[0, 0, head + 2 * width :, :] = jnp.concatenate(
            [gl_ref[0, 0], jnp.zeros((tail - experts, span), F32)], 0
        ).astype(BF16)
        w_acc[:, : r_ref.shape[2]] += dot_nt(hid_ref[0, 0].T, r_ref[0, 0])

    @pl.when((micro == pl.num_programs(0) - 1) & (step == blocks - 1))
    def _():
        if len(grad_refs) == 1:
            grad_refs[0][...] = w_acc[:, : r_ref.shape[2]].astype(BF16)
            return
        routed = head + 2 * width
        spare = order_ref.shape[0]
        w_acc[:, routed:] = dot_nn(
            w_acc[:, routed : routed + spare].astype(BF16), order_ref[...]
        )
        targets = grad_refs[0].shape[0] * grad_refs[0].shape[1]
        shared_rows = w_acc.shape[0] // (2 * targets)

        def pack(ref, to, fro, shared, heads):
            rows, columns = heads_chunk(w_acc.shape[0], head, ref)
            at = pack_tiles(ref, to, 0, w_acc, heads * rows, rows, fro * columns, columns)
            pack_tiles(ref, to, at, w_acc, shared * shared_rows, shared_rows, head, w_acc.shape[1] - head)

        for_targets(ids, grad_refs, pack)


def input_kernel(
    ids, x_ref, mid_ref, r_ref, own_ref, other_ref, vec_ref, out_ref, small_ref, w_ref, sems
):
    first = (pl.program_id(0) == 0) & (pl.program_id(1) == 0)
    load_halves(first, ids[0], sems, [(own_ref, other_ref, w_ref)])

    @pl.when(first)
    def _():
        small_ref[...] = jnp.zeros_like(small_ref)

    low, high = halves(w_ref)
    routed = r_ref[0, 0]
    back = jnp.concatenate([dot_tn(routed, low[...]), dot_tn(routed, high[...])], 1)
    normed, spread = normalize(x_ref[0, 0].astype(F32))
    scaled = back * vec_ref[0:1, :]
    out_ref[0, 0] = mid_ref[0, 0] + spread * (
        scaled
        - jnp.mean(scaled, -1, keepdims=True)
        - normed * jnp.mean(scaled * normed, -1, keepdims=True)
    )
    small_ref[0] += fold_rows(back * normed, jnp.sum)
    small_ref[1] += fold_rows(back, jnp.sum)


def full(shape):
    return pl.BlockSpec(shape, lambda *ids: (0,) * len(shape))


def blocked(shape):
    tail = (0,) * (len(shape) - 2)
    return pl.BlockSpec((1, 1) + tuple(shape[2:]), lambda m, i, *refs: (m, i) + tail)


def grouped(shape, group):
    tail = (0,) * (len(shape) - 2)
    return pl.BlockSpec((1, group) + tuple(shape[2:]), lambda m, i, *refs: (m, i) + tail)


def in_place():
    return pl.BlockSpec(memory_space=pl.ANY)


def reversed_blocks(shape):
    tail = (0,) * (len(shape) - 2)
    last = shape[1] - 1
    return pl.BlockSpec((1, 1) + tuple(shape[2:]), lambda m, i, *refs: (m, last - i) + tail)


def whole(shape):
    tail = (0,) * (len(shape) - 1)
    return pl.BlockSpec((1,) + tuple(shape[1:]), lambda m, i, *refs: (m,) + tail)


def struct(shape, dtype):
    return jax.ShapeDtypeStruct(shape, dtype)


def params():
    return pltpu.CompilerParams(
        dimension_semantics=("arbitrary", "arbitrary"), vmem_limit_bytes=VMEM_BYTES
    )


def cost(flops, transcendentals, moved):
    return pl.CostEstimate(flops=flops, transcendentals=transcendentals, bytes_accessed=moved)


def exchange(value, axis, distance):
    count = lax.axis_size(axis)
    return lax.ppermute(value, axis, [(at, at ^ distance) for at in range(count)])


def permute_groups(value, index):
    groups = value.shape[0]
    bit = 1
    while bit < groups:
        pairs = value.reshape((groups // (2 * bit), 2, bit) + value.shape[1:])
        value = jnp.where((index & bit) != 0, pairs[:, ::-1].reshape(value.shape), value)
        bit *= 2
    return value


def pick_at(value, index, dim):
    return lax.dynamic_index_in_dim(value, index, dim, keepdims=False)


def reduce_axis(value, axis, dim, relative=False, keep=False):
    count = lax.axis_size(axis)
    me = lax.axis_index(axis)
    base = 0 if relative else me
    total = pick_at(value, base, dim).astype(F32)
    for distance in range(1, count):
        sent = pick_at(value, distance if relative else me ^ distance, dim)
        total = total + exchange(sent, axis, distance).astype(F32)
    return total if keep else total.astype(BF16)


def core_stage(grads):
    keep, send = grads
    other = exchange(send, "fsdp", 1)
    return [(keep[at].astype(F32) + other[at].astype(F32)).astype(BF16) for at in range(keep.shape[0])]


def split_targets(value, axis):
    return [value[at] for at in range(lax.axis_size(axis))]


def send_stage(parts, axis):
    return [exchange(parts[distance], axis, distance) for distance in range(1, len(parts))]


def total_up(own, received):
    total = own.astype(F32)
    for part in received:
        total = total + part.astype(F32)
    return total


def add_up(own, received):
    return total_up(own, received).astype(BF16)


def open_tiles(value, at, rows, columns):
    count = columns // 128
    tiles = value[at : at + count * rows].reshape(count, rows, 128)
    return jnp.swapaxes(tiles, 0, 1).reshape(rows, columns), at + count * rows


def sum_packed(parts, devices):
    packed = jnp.concatenate(parts, 1)
    packed = lax.all_to_all(packed, AXES, split_axis=0, concat_axis=0, tiled=True)
    packed = jnp.sum(packed.reshape(devices, -1), 0)
    result, at = [], 0
    for part in parts:
        result.append(packed[at : at + part.shape[1]])
        at += part.shape[1]
    return result


def local(
    inputs,
    lengths,
    routes,
    ln1_gain,
    ln1_bias,
    kv_weight,
    router_weight,
    query_weight,
    out_weight,
    ln2_gain,
    ln2_bias,
    up_weight,
    up_bias,
    down_weight,
    down_bias,
    out_cotangent,
):
    micro_count, _, slots, model = inputs.shape
    experts = router_weight.shape[2]
    width = query_weight.shape[3]
    picks = routes.shape[4]
    hidden_units = up_weight.shape[2]
    dp_size, z_size, f_size = (lax.axis_size(axis) for axis in AXES)
    dp_at, z_at, f_at = (lax.axis_index(axis) for axis in AXES)
    ids = jnp.stack([dp_at, z_at, f_at]).astype(jnp.int32)
    seq_index = (dp_at * z_size + z_at) * f_size + f_at
    devices = dp_size * z_size * f_size
    own_experts = experts // z_size
    half = model // f_size
    span = min(BLOCK, slots)
    blocks = slots // span
    rows = picks * span
    group = 2 if blocks % 2 == 0 else 1
    head = experts * width
    spare = -(-experts // 16) * 16
    all_rows = head + 2 * width + spare
    chunk = model // devices
    aligned = chunk % 16 == 0 and (head // z_size) % 128 == 0
    lens = lax.dynamic_index_in_dim(lengths, seq_index, 1, keepdims=False)

    def both_halves(own, other, dim):
        near = jnp.concatenate([own, other], dim)
        return jnp.where(f_at == 0, near, jnp.concatenate([other, own], dim))

    def head_parts(own):
        return [own] + [exchange(own, "expert", distance) for distance in range(1, z_size)]

    def transposed(weight):
        return jnp.swapaxes(weight[0], 1, 2).reshape(own_experts * width, half)

    def start_of(routes):
        local_routes = routes[0, :, 0]
        group = (local_routes // own_experts) ^ z_at
        local_routes = group * own_experts + local_routes % own_experts
        return jnp.swapaxes(local_routes.reshape(micro_count, blocks, span, picks), 2, 3)

    query_parts = head_parts(transposed(query_weight))
    router_t = router_weight[0].T.reshape(z_size, own_experts, half)
    router_t = permute_groups(router_t, z_at).reshape(experts, half)
    router_t = jnp.pad(router_t, ((0, spare - experts), (0, 0)))
    vectors = jnp.concatenate([ln1_gain, ln1_bias, ln2_gain, ln2_bias, down_bias], 0)
    small = jnp.concatenate([vectors, up_bias.reshape(-1, half)], 0)
    small_other = exchange(small, "fsdp", 1)
    vectors = both_halves(vectors, small_other[:5], 1).astype(F32)
    up_shift = both_halves(up_bias, small_other[5:].reshape(1, -1), 1).astype(F32)

    up_other = exchange(up_weight[0], "fsdp", 1)
    down_other = exchange(down_weight[0], "fsdp", 1)
    route_t = start_of(routes)
    lens, ids, route_t, vectors, up_shift, router_t, *query_parts = lax.optimization_barrier(
        (lens, ids, route_t, vectors, up_shift, router_t, *query_parts)
    )
    proj = jnp.concatenate(query_parts + [kv_weight[0].T, router_t], 0)
    proj_other = exchange(proj, "fsdp", 1)
    own_out, proj_other = lax.optimization_barrier((transposed(out_weight), proj_other))
    out_parts = head_parts(own_out)

    states = inputs.reshape(micro_count, blocks, span, model)
    cotangent = out_cotangent.reshape(micro_count, blocks, span, model)

    grid = (micro_count, blocks)
    hid_s = struct((micro_count, blocks, span, model), BF16)
    aug_s = struct((micro_count, blocks, span, 2 * width), BF16)
    kt_s = struct((micro_count, blocks, 1, width, span), BF16)
    q_s = struct((micro_count, blocks, width, rows), BF16)
    row_s = struct((micro_count, blocks, 1, rows), F32)
    gate_s = struct((micro_count, blocks, experts, span), F32)
    slot_s = struct((micro_count, blocks, experts, span), jnp.int32)
    tokens = micro_count * slots
    pair_flops = tokens * picks * slots * width
    hid, kaug, vaug, kt, q, ctx, lse, gates, slot = pl.pallas_call(
        forward_kernel,
        name="forward",
        grid_spec=pltpu.PrefetchScalarGridSpec(
            num_scalar_prefetch=2,
            grid=grid,
            in_specs=[
                blocked(states.shape),
                blocked(route_t.shape),
                full(vectors.shape),
                in_place(),
                in_place(),
            ],
            out_specs=[
                blocked(hid_s.shape),
                whole(aug_s.shape),
                whole(aug_s.shape),
                blocked(kt_s.shape),
                blocked(q_s.shape),
                blocked(q_s.shape),
                blocked(row_s.shape),
                blocked(gate_s.shape),
                blocked(slot_s.shape),
            ],
            scratch_shapes=[
                pltpu.VMEM((all_rows, span), F32),
                pltpu.VMEM((2 * width, rows), BF16),
                pltpu.VMEM((blocks, span, rows), F32),
                pltpu.VMEM((blocks, width, span), BF16),
                pltpu.VMEM((width, rows), F32),
                pltpu.VMEM((2 * all_rows, half), BF16),
                pltpu.SemaphoreType.DMA((2,)),
            ],
        ),
        out_shape=[hid_s, aug_s, aug_s, kt_s, q_s, q_s, row_s, gate_s, slot_s],
        compiler_params=params(),
        cost_estimate=cost(2 * tokens * model * all_rows + 16 * pair_flops, 0, 64 << 20),
    )(lens, ids, states, route_t, vectors, proj, proj_other)

    ctx, *out_parts = lax.optimization_barrier((ctx, *out_parts))
    out_proj = jnp.concatenate(out_parts, 0)
    out_other = exchange(out_proj, "fsdp", 1)
    state_s = struct((micro_count, blocks, span, model), F32)
    mid_rows = chunk * hidden_units * 2 // 128 + head // z_size * (chunk * z_size) // 128
    late_rows = head // z_size * (chunk * z_size) // 128 + 2 * chunk
    if aligned:
        mid_grads = [struct((dp_size, z_size, mid_rows, 128), BF16)] * 2
        late_grads = [struct((dp_size, z_size, late_rows, 128), BF16)] * 2
    else:
        mid_grads = [
            struct((hidden_units, model), BF16),
            struct((model, hidden_units), BF16),
            struct((model, head), BF16),
        ]
        late_grads = [struct((model, all_rows), BF16)]
    outputs, mid, grad_ctx, delta, grad_logits, small2, up_small, *mid_grads = pl.pallas_call(
        middle_kernel,
        name="middle",
        grid_spec=pltpu.PrefetchScalarGridSpec(
            num_scalar_prefetch=2,
            grid=(micro_count, blocks // group),
            in_specs=[
                grouped(states.shape, group),
                grouped(q_s.shape, group),
                grouped(gate_s.shape, group),
                grouped(slot_s.shape, group),
                grouped(cotangent.shape, group),
                in_place(),
                in_place(),
                full(vectors.shape),
                in_place(),
                in_place(),
                full(up_shift.shape),
                in_place(),
                in_place(),
            ],
            out_specs=[
                grouped(state_s.shape, group),
                grouped(state_s.shape, group),
                grouped(q_s.shape, group),
                grouped(row_s.shape, group),
                grouped(gate_s.shape, group),
                full((3, 8, model)),
                full((8, hidden_units)),
            ]
            + [full(leaf.shape) for leaf in mid_grads],
            scratch_shapes=[
                pltpu.VMEM((group, width, rows), F32),
                pltpu.VMEM((head, group * span), BF16),
                pltpu.VMEM((head, group * span), F32),
                pltpu.VMEM((hidden_units, model), F32),
                pltpu.VMEM((model, hidden_units), F32),
                pltpu.VMEM((model, head), F32),
                pltpu.VMEM((2 * head, half), BF16),
                pltpu.VMEM((model, hidden_units), BF16),
                pltpu.VMEM((hidden_units, model), BF16),
                pltpu.SemaphoreType.DMA((6,)),
            ],
        ),
        out_shape=[
            state_s,
            state_s,
            q_s,
            row_s,
            gate_s,
            struct((3, 8, model), F32),
            struct((8, hidden_units), F32),
        ]
        + mid_grads,
        compiler_params=params(),
        cost_estimate=cost(2 * tokens * model * (6 * hidden_units + 3 * head), 0, 200 << 20),
    )(
        lens,
        ids,
        states,
        ctx,
        gates,
        slot,
        cotangent,
        out_proj,
        out_other,
        vectors,
        up_weight[0],
        up_other,
        up_shift,
        down_weight[0],
        down_other,
    )

    if aligned:
        mid_sums = core_stage(mid_grads)
        grad_ctx, *mid_sums = lax.optimization_barrier((grad_ctx, *mid_sums))
        mid_received = send_stage(mid_sums, "dp")

    expert_id = jnp.arange(experts)
    moved = ((expert_id // own_experts) ^ z_at) * own_experts + expert_id % own_experts
    order = jnp.pad(
        (jnp.arange(spare)[:, None] == moved[None, :]).astype(BF16), ((0, 0), (0, 128 - experts))
    )
    r_s = struct((micro_count, blocks, all_rows, span), BF16)
    routed, *late_grads = pl.pallas_call(
        backward_kernel,
        name="backward",
        grid_spec=pltpu.PrefetchScalarGridSpec(
            num_scalar_prefetch=2,
            grid=grid,
            in_specs=[
                reversed_blocks(hid_s.shape),
                whole(aug_s.shape),
                whole(aug_s.shape),
                whole((micro_count, blocks, width, span)),
                reversed_blocks(q_s.shape),
                reversed_blocks(row_s.shape),
                reversed_blocks(q_s.shape),
                reversed_blocks(row_s.shape),
                reversed_blocks(slot_s.shape),
                reversed_blocks(gate_s.shape),
                full(order.shape),
            ],
            out_specs=[reversed_blocks(r_s.shape)] + [full(leaf.shape) for leaf in late_grads],
            scratch_shapes=[
                pltpu.VMEM((2 * width, rows), BF16),
                pltpu.VMEM((2 * width, rows), BF16),
                pltpu.VMEM((width, rows), F32),
                pltpu.VMEM((blocks, width, span), F32),
                pltpu.VMEM((blocks, width, span), F32),
                pltpu.VMEM((model, head + 2 * width + 128), F32),
            ],
        ),
        out_shape=[r_s] + late_grads,
        compiler_params=params(),
        cost_estimate=cost(2 * tokens * model * all_rows + 40 * pair_flops, 0, 100 << 20),
    )(
        lens,
        ids,
        hid,
        kaug,
        vaug,
        kt.reshape(micro_count, blocks, width, span),
        q,
        lse,
        grad_ctx,
        delta,
        slot,
        grad_logits,
        order,
    )

    if aligned:
        *mid_received, late_grads[0], late_grads[1] = lax.optimization_barrier(
            (*mid_received, *late_grads)
        )
        *mid_received, late_grads[0], late_grads[1] = lax.optimization_barrier(
            (*mid_received, *late_grads)
        )
        late_sums = core_stage(late_grads)
        *mid_received, late_sums[0] = lax.optimization_barrier((*mid_received, late_sums[0]))
        mid_sums = split_targets(add_up(mid_sums[0], mid_received), "expert")
        routed, *sums = lax.optimization_barrier((routed, *mid_sums, *late_sums))
        mid_sums, late_sums = sums[:z_size], sums[z_size:]
        mid_received = send_stage(mid_sums, "expert")
        late_received = send_stage(late_sums, "dp")

    input_grad, small1 = pl.pallas_call(
        input_kernel,
        name="input_back",
        grid_spec=pltpu.PrefetchScalarGridSpec(
            num_scalar_prefetch=1,
            grid=grid,
            in_specs=[
                blocked(states.shape),
                blocked(state_s.shape),
                blocked(r_s.shape),
                in_place(),
                in_place(),
                full(vectors.shape),
            ],
            out_specs=[blocked(state_s.shape), full((2, 8, model))],
            scratch_shapes=[
                pltpu.VMEM((2 * all_rows, half), BF16),
                pltpu.SemaphoreType.DMA((2,)),
            ],
        ),
        out_shape=[state_s, struct((2, 8, model), F32)],
        compiler_params=params(),
        cost_estimate=cost(2 * tokens * model * all_rows, 0, 40 << 20),
    )(ids[2:], states, mid, routed, proj, proj_other, vectors)

    if aligned:
        small1, *received = lax.optimization_barrier((small1, *late_received, *mid_received))
        late_received = received[: dp_size - 1]
        mid_received = received[dp_size - 1 :]
    small = jnp.concatenate([jnp.sum(small1, 1), jnp.sum(small2, 1)], 0)
    small = jnp.swapaxes(small.reshape(5, devices, chunk), 0, 1).reshape(devices, 5 * chunk)
    up_small = jnp.sum(up_small, 0).reshape(devices, hidden_units // devices)
    packed = [small, up_small]

    def open_heads(value):
        return jnp.swapaxes(value.reshape(-1, own_experts, width), 0, 1)[None]

    if aligned:
        late_sums = split_targets(add_up(late_sums[0], late_received), "expert")
        packed[0], *late_sums = lax.optimization_barrier((packed[0], *late_sums))
        packed = sum_packed(packed, devices)
        mid_total = total_up(mid_sums[0], mid_received)
        up_weight_grad, at = open_tiles(mid_total, 0, chunk, hidden_units)
        down_weight_grad, at = open_tiles(mid_total, at, hidden_units // devices, model)
        out_weight_grad, at = open_tiles(mid_total, at, chunk * z_size, head // z_size)
        late_received = send_stage(late_sums, "expert")
        late_total = total_up(late_sums[0], late_received)
        query_weight_grad, at = open_tiles(late_total, 0, chunk * z_size, head // z_size)
        kv_grad = late_total[at : at + chunk]
        router_grad = late_total[at + chunk : at + 2 * chunk, :experts]
        query_weight_grad, out_weight_grad = map(open_heads, (query_weight_grad, out_weight_grad))
    else:
        down_grad, up_grad, wo_grad = mid_grads
        w_grad = late_grads[0]

        def reduce_shared(value, part):
            value = value.reshape(dp_size, z_size, f_size, part, value.shape[1])
            value = reduce_axis(value, "fsdp", 2)
            value = reduce_axis(value, "dp", 0)
            return reduce_axis(value, "expert", 0, keep=True)

        def reduce_heads(value):
            value = value.reshape(dp_size, f_size, chunk * z_size, z_size, own_experts * width)
            value = reduce_axis(value, "fsdp", 1)
            value = reduce_axis(value, "dp", 0)
            return open_heads(reduce_axis(value, "expert", 1, relative=True, keep=True))

        up_weight_grad = reduce_shared(up_grad, chunk)
        down_weight_grad = reduce_shared(down_grad, hidden_units // devices)
        out_weight_grad = reduce_heads(wo_grad)
        query_weight_grad = reduce_heads(w_grad[:, :head])
        router_grad = w_grad[:, head + 2 * width : head + 2 * width + experts].astype(F32)
        router_grad = permute_groups(router_grad.T.reshape(z_size, own_experts, model), z_at)
        router_grad = router_grad.reshape(experts, model).T
        kv_grad = w_grad[:, head : head + 2 * width].astype(F32)
        packed += [kv_grad.reshape(devices, -1), router_grad.reshape(devices, -1)]
        packed = sum_packed(packed, devices)
        kv_grad = packed[2].reshape(chunk, 2 * width)
        router_grad = packed[3].reshape(chunk, experts)
    small = packed[0].reshape(5, 1, chunk)
    shape = (micro_count, 1, slots, model)
    return (
        outputs.reshape(shape),
        input_grad.reshape(shape),
        small[0],
        small[1],
        kv_grad[None],
        router_grad[None],
        query_weight_grad,
        out_weight_grad,
        small[2],
        small[3],
        up_weight_grad[None],
        packed[1][None],
        down_weight_grad[None],
        small[4],
    )


def solution(mesh):
    shards = P(None, AXES, None, None)
    return jax.shard_map(
        local,
        mesh=mesh,
        in_specs=(
            shards,
            P(),
            P(None, None, AXES, None, None),
            P(None, "fsdp"),
            P(None, "fsdp"),
            P(None, "fsdp", None),
            P(None, "fsdp", None),
            P(None, "expert", "fsdp", None),
            P(None, "expert", "fsdp", None),
            P(None, "fsdp"),
            P(None, "fsdp"),
            P(None, "fsdp", None),
            P(None, "fsdp"),
            P(None, "fsdp", None),
            P(None, "fsdp"),
            shards,
        ),
        out_specs=(
            shards,
            shards,
            P(None, AXES),
            P(None, AXES),
            P(None, AXES, None),
            P(None, AXES, None),
            P(None, "expert", ("dp", "fsdp"), None),
            P(None, "expert", ("dp", "fsdp"), None),
            P(None, AXES),
            P(None, AXES),
            P(None, AXES, None),
            P(None, AXES),
            P(None, AXES, None),
            P(None, AXES),
        ),
        check_vma=False,
    )
```

```python
import functools

import jax
import jax.numpy as jnp
from jax import lax
from jax.experimental import pallas as pl
from jax.experimental.pallas import tpu as pltpu
from jax.sharding import PartitionSpec as P

EPSILON = 1e-05
NEGATIVE = -1e30
GELU_SCALE = 0.7978845608028654
GELU_CUBIC = 0.044715
BLOCK = 256
AXES = ("dp", "expert", "fsdp")
F32 = jnp.float32
BF16 = jnp.bfloat16
VMEM_BYTES = 60 << 20


def dot_nn(left, right):
    return lax.dot_general(left, right, (((1,), (0,)), ((), ())), preferred_element_type=F32)


def dot_nt(left, right):
    return lax.dot_general(left, right, (((1,), (1,)), ((), ())), preferred_element_type=F32)


def dot_tn(left, right):
    return lax.dot_general(left, right, (((0,), (0,)), ((), ())), preferred_element_type=F32)


def normalize(values):
    center = values - jnp.mean(values, -1, keepdims=True)
    spread = lax.rsqrt(jnp.mean(center * center, -1, keepdims=True) + EPSILON)
    return center * spread, spread


def halves(ref):
    rows = ref.shape[0] // 2
    return ref.at[pl.ds(0, rows)], ref.at[pl.ds(rows, rows)]


def fold_rows(values, combine):
    rows, columns = values.shape
    return combine(values.reshape(rows // 8, 8, columns), 0)


def pick_slots(table_ref, slot, picks, width, start=0):
    experts, span = slot.shape
    lanes = slice(start, start + span)
    picked = []
    for pick in range(picks):
        value = table_ref[pick * width : (pick + 1) * width, lanes]
        for expert in range(pick + 1, experts - picks + pick + 1):
            hit = jnp.broadcast_to(slot[expert : expert + 1, :], (width, span)) == pick
            value = jnp.where(hit, table_ref[expert * width : (expert + 1) * width, lanes], value)
        picked.append(value)
    return picked


def spread_slots(read, slot, expert, picks, width, span):
    experts = slot.shape[0]
    row = jnp.broadcast_to(slot[expert : expert + 1, :], (width, span))
    value = jnp.zeros((width, span), F32)
    for pick in range(max(0, expert - experts + picks), min(expert, picks - 1) + 1):
        value = jnp.where(row == pick, read(pick), value)
    return value


def forward_kernel(
    lens,
    ids,
    x_ref,
    route_ref,
    vec_ref,
    own_ref,
    other_ref,
    hid_ref,
    kaug_ref,
    vaug_ref,
    kt_ref,
    q_ref,
    ctx_ref,
    lse_ref,
    gate_ref,
    slot_ref,
    table,
    qaug,
    scores,
    vt,
    acc,
    w_ref,
    sems,
):
    block = pl.program_id(1)
    length = lens[pl.program_id(0)]
    first = (pl.program_id(0) == 0) & (block == 0)
    copies = half_copies(ids[2], sems, [(own_ref, other_ref, w_ref)])
    start_all(first, copies)
    wait_all(first, copies)
    span = x_ref.shape[2]
    experts = slot_ref.shape[2]
    picks = route_ref.shape[2]
    width = kt_ref.shape[3]
    half = w_ref.shape[1]
    low, high = halves(w_ref)
    rows = picks * span

    normed, _ = normalize(x_ref[0, 0].astype(F32))
    hid = (normed * vec_ref[0:1, :] + vec_ref[1:2, :]).astype(BF16)
    hid_ref[0, 0] = hid
    table[...] = dot_nt(low[...], hid[:, :half]) + dot_nt(high[...], hid[:, half:])
    head = experts * width
    kt_ref[0, 0, 0] = table[head : head + width, :].astype(BF16)
    vt[block] = table[head + width : head + 2 * width, :].astype(BF16)

    lane = lax.broadcasted_iota(jnp.int32, (span, 2 * width), 1)
    place = block * span + lax.broadcasted_iota(jnp.int32, (span, 2 * width), 0)
    ones = jnp.where(lane < width + 4, 1.0, 0.0)
    cut = jnp.where(place < length, 0.0, NEGATIVE)
    both = dot_nt(hid[:, :half], low[head : head + 2 * width, :])
    both = both + dot_nt(hid[:, half:], high[head : head + 2 * width, :])
    keys = jnp.where(lane < width, both, jnp.where(lane == width, cut, ones))
    kaug_ref[0, block] = keys.astype(BF16)
    vals = jnp.where(lane < width, pltpu.roll(both, width, 1), ones)
    vaug_ref[0, block] = vals.astype(BF16)

    logits = table[head + 2 * width : head + 2 * width + experts, :]
    expert_id = lax.broadcasted_iota(jnp.int32, (experts, span), 0)
    chosen = jnp.zeros((experts, span), F32)
    for pick in range(picks):
        chosen = jnp.where(expert_id == route_ref[0, 0, pick : pick + 1, :], 1.0, chosen)
    lower = jnp.where(
        lax.broadcasted_iota(jnp.int32, (experts, experts), 1)
        < lax.broadcasted_iota(jnp.int32, (experts, experts), 0),
        1.0,
        0.0,
    )
    slot = jnp.where(chosen > 0.0, dot_nn(lower, chosen), -1.0).astype(jnp.int32)
    slot_ref[0, 0] = slot
    masked = jnp.where(chosen > 0.0, logits, NEGATIVE)
    raised = jnp.where(chosen > 0.0, jnp.exp(masked - jnp.max(masked, 0, keepdims=True)), 0.0)
    gate_ref[0, 0] = raised / jnp.sum(raised, 0, keepdims=True)

    picked = pick_slots(table, slot, picks, width)
    for pick in range(picks):
        qaug[0:width, pick * span : (pick + 1) * span] = (
            picked[pick].astype(BF16) * (width**-0.5)
        ).astype(BF16)
    q_ref[0, 0] = qaug[0:width, :]
    side = lax.broadcasted_iota(jnp.int32, (width, rows), 0)
    qaug[width : 2 * width, :] = jnp.where(side == 0, 1.0, 0.0).astype(BF16)

    def score_step(at, top):
        part = dot_nn(kaug_ref[0, at], qaug[...])
        scores[at] = part
        return jnp.maximum(top, fold_rows(part, jnp.max))

    used = jnp.minimum(block, (length + span - 1) // span)
    top = lax.fori_loop(0, used, score_step, jnp.full((8, rows), NEGATIVE, F32))
    causal = lax.broadcasted_iota(jnp.int32, (span, rows), 0) <= (
        lax.broadcasted_iota(jnp.int32, (span, rows), 1) & (span - 1)
    )
    part = jnp.where(causal, dot_nn(kaug_ref[0, block], qaug[...]), NEGATIVE)
    top = jnp.maximum(top, fold_rows(part, jnp.max))
    top = jnp.max(top, 0, keepdims=True)
    raised = jnp.exp(part - top)
    acc[...] = dot_nn(vt[block], raised.astype(BF16))
    total = fold_rows(raised, jnp.sum)

    def value_step(at, total):
        raised = jnp.exp(scores[at] - top)
        acc[...] += dot_nn(vt[at], raised.astype(BF16))
        return total + fold_rows(raised, jnp.sum)

    total = lax.fori_loop(0, used, value_step, total)
    total = jnp.sum(total, 0, keepdims=True)
    ctx_ref[0, 0] = (acc[...] * (1.0 / total)).astype(BF16)
    lse_ref[0, 0] = top + jnp.log(total)


def middle_kernel(
    lens,
    ids,
    x_ref,
    ctx_ref,
    gate_ref,
    slot_ref,
    cot_ref,
    own_ref,
    other_ref,
    vec_ref,
    own_up_ref,
    other_up_ref,
    up_shift_ref,
    own_down_ref,
    other_down_ref,
    out_ref,
    mid_ref,
    do_ref,
    delta_ref,
    gl_ref,
    small_ref,
    up_shift_grad_ref,
    *rest,
):
    *grad_refs, gated, cexp, table, down_acc, up_acc, wo_acc, w_ref, up_ref, down_ref, sems = rest
    micro = pl.program_id(0)
    block = pl.program_id(1)
    length = lens[micro]
    subs, span, model = x_ref.shape[1:]
    tokens = subs * span
    experts = slot_ref.shape[2]
    width = ctx_ref.shape[2]
    picks = ctx_ref.shape[3] // span
    head = experts * width
    half = w_ref.shape[1]
    low, high = halves(w_ref)
    first = (micro == 0) & (block == 0)
    last = (micro == pl.num_programs(0) - 1) & (block == pl.num_programs(1) - 1)

    def clear():
        down_acc[...] = jnp.zeros_like(down_acc)
        up_acc[...] = jnp.zeros_like(up_acc)
        wo_acc[...] = jnp.zeros_like(wo_acc)
        small_ref[...] = jnp.zeros_like(small_ref)
        up_shift_grad_ref[...] = jnp.zeros_like(up_shift_grad_ref)

    copies = half_copies(
        ids[2],
        sems,
        [
            (own_ref, other_ref, w_ref),
            (own_up_ref, other_up_ref, up_ref),
            (own_down_ref, other_down_ref, down_ref),
        ],
    )
    start_all(first, copies, clear)
    wait_all(first, copies)
    slots = [slot_ref[0, sub] for sub in range(subs)]
    gate = []
    for sub in range(subs):
        gates = gate_ref[0, sub]
        gate.append(
            [
                jnp.sum(jnp.where(slots[sub] == pick, gates, 0.0), 0, keepdims=True)
                for pick in range(picks)
            ]
        )
        for pick in range(picks):
            at = slice(pick * span, (pick + 1) * span)
            gated[sub, :, at] = ctx_ref[0, sub, :, at].astype(F32) * gate[sub][pick]
        for expert in range(experts):
            cexp[expert * width : (expert + 1) * width, sub * span : (sub + 1) * span] = spread_slots(
                lambda pick: gated[sub, :, pick * span : (pick + 1) * span],
                slots[sub],
                expert,
                picks,
                width,
                span,
            ).astype(BF16)
    mixed = x_ref[0].reshape(tokens, model).astype(F32) + jnp.concatenate(
        [dot_tn(cexp[...], low[...]), dot_tn(cexp[...], high[...])], 1
    )
    normed, spread = normalize(mixed)
    hid = (normed * vec_ref[2:3, :] + vec_ref[3:4, :]).astype(BF16)
    place = block * tokens + lax.broadcasted_iota(jnp.int32, (tokens, 1), 0)
    grad = jnp.where(place < length, cot_ref[0].reshape(tokens, model), 0.0)
    grad_b = grad.astype(BF16)
    hid_t = hid.T
    out = mixed + vec_ref[4:5, :]
    back = jnp.zeros_like(mixed)
    hidden_units = up_ref.shape[1]
    step = min(hidden_units, 256)
    cuts = [slice(at, at + step) for at in range(0, hidden_units, step)]

    def ahead(cut):
        return dot_nn(hid, up_ref[:, cut]), dot_nt(grad_b, down_ref[cut, :])

    held = ahead(cuts[0])
    ready = None
    for n in range(len(cuts) + 1):
        pre, grad_act = held if held is not None else (None, None)
        held = ahead(cuts[n + 1]) if n + 1 < len(cuts) else None
        fresh = None
        if n < len(cuts):
            cut = cuts[n]
            pre = pre + up_shift_ref[:, cut]
            square = pre * pre
            bent = jnp.tanh(pre * (GELU_SCALE + (GELU_SCALE * GELU_CUBIC) * square))
            rise = 0.5 + 0.5 * bent
            slope = rise + (0.5 * pre) * (1.0 - bent * bent) * (
                GELU_SCALE + (3.0 * GELU_SCALE * GELU_CUBIC) * square
            )
            grad_pre = grad_act * slope
            up_shift_grad_ref[:, cut] += fold_rows(grad_pre, jnp.sum)
            fresh = (cut, (pre * rise).astype(BF16), grad_pre.astype(BF16))
        if ready is not None:
            cut, active, grad_pre_b = ready
            out = out + dot_nn(active, down_ref[cut, :])
            back = back + dot_nt(grad_pre_b, up_ref[:, cut])
            down_acc[cut, :] += dot_nn(active.T, grad_b)
            up_acc[:, cut] += dot_nn(hid_t, grad_pre_b)
        ready = fresh
    out_ref[0] = out.reshape(subs, span, model)
    scaled = back * vec_ref[2:3, :]
    mid = grad + spread * (
        scaled
        - jnp.mean(scaled, -1, keepdims=True)
        - normed * jnp.mean(scaled * normed, -1, keepdims=True)
    )
    mid_ref[0] = mid.reshape(subs, span, model)
    small_ref[0] += fold_rows(back * normed, jnp.sum)
    small_ref[1] += fold_rows(back, jnp.sum)
    small_ref[2] += fold_rows(grad_b.astype(F32), jnp.sum)

    mid_b = mid.astype(BF16)
    wo_acc[...] += dot_nt(mid_b.T, cexp[...])
    table[...] = dot_nt(low[...], mid_b[:, :half]) + dot_nt(high[...], mid_b[:, half:])
    for sub in range(subs):
        slot = slots[sub]
        picked = pick_slots(table, slot, picks, width, sub * span)
        grad_gate = []
        for pick in range(picks):
            at = slice(pick * span, (pick + 1) * span)
            ctx = ctx_ref[0, sub, :, at].astype(F32)
            grad_gate.append(jnp.sum(picked[pick] * ctx, 0, keepdims=True))
            grad_ctx = (picked[pick] * gate[sub][pick]).astype(BF16)
            do_ref[0, sub, :, at] = grad_ctx
            delta_ref[0, sub, :, at] = jnp.sum(grad_ctx.astype(F32) * ctx, 0, keepdims=True)
        average = gate[sub][0] * grad_gate[0]
        for pick in range(1, picks):
            average = average + gate[sub][pick] * grad_gate[pick]
        grad_logits = jnp.zeros((experts, span), F32)
        for pick in range(picks):
            grad_logits = jnp.where(
                slot == pick, gate[sub][pick] * (grad_gate[pick] - average), grad_logits
            )
        gl_ref[0, sub] = grad_logits

    @pl.when(last)
    def _():
        if len(grad_refs) == 3:
            for ref, total in zip(grad_refs, (down_acc, up_acc, wo_acc)):
                ref[...] = total[...].astype(BF16)
            return
        targets = grad_refs[0].shape[0] * grad_refs[0].shape[1]
        up_rows = up_acc.shape[0] // (2 * targets)
        down_rows = down_acc.shape[0] // (2 * targets)

        def pack(ref, to, fro, shared, heads):
            at = pack_tiles(ref, to, 0, up_acc, shared * up_rows, up_rows, 0, up_acc.shape[1])
            at = pack_tiles(ref, to, at, down_acc, shared * down_rows, down_rows, 0, down_acc.shape[1])
            rows, columns = heads_chunk(wo_acc.shape[0], head, ref)
            pack_tiles(ref, to, at, wo_acc, heads * rows, rows, fro * columns, columns)

        for_targets(ids, grad_refs, pack)


def half_copies(core, sems, moves):
    copies = []
    for own, other, target in moves:
        half = target.shape[0] // 2
        for source, at in ((own, core), (other, 1 - core)):
            place = target.at[pl.ds(pl.multiple_of(at * half, half), half)]
            copies.append(pltpu.make_async_copy(source, place, sems.at[len(copies)]))
    return copies


def start_all(first, copies, meanwhile=lambda: None):
    @pl.when(first)
    def _():
        for copy in copies:
            copy.start()
        meanwhile()


def wait_all(first, copies):
    @pl.when(first)
    def _():
        for copy in copies:
            copy.wait()


def pack_tiles(ref, to, at, total, row, rows, column, columns):
    row = pl.multiple_of(row, rows)
    for lane in range(0, columns, 128):
        start = column + lane
        if not isinstance(start, int):
            start = pl.multiple_of(start, 128)
        tile = total[pl.ds(row, rows), pl.ds(start, 128)]
        ref[to[0], to[1], at : at + rows, :] = tile.astype(BF16)
        at += rows
    return at


def heads_chunk(model, head, ref):
    return model // (2 * ref.shape[0]), head // ref.shape[1]


def for_targets(ids, refs, pack):
    def body(dp_far, carry):
        dp = dp_far ^ ids[0]
        for z_far in range(refs[0].shape[1]):
            for f_far in range(2):
                f = ids[2] ^ f_far
                shared = (dp * refs[0].shape[1] + (z_far ^ ids[1])) * 2 + f
                pack(refs[f_far], (dp_far, z_far), z_far, shared, dp * 2 + f)
        return carry

    lax.fori_loop(0, refs[0].shape[0], body, 0)


def split_three(values):
    high = values.astype(BF16).astype(F32)
    rest = values - high
    middle = rest.astype(BF16).astype(F32)
    return high, middle, rest - middle


def backward_kernel(
    lens,
    ids,
    hid_ref,
    kaug_ref,
    vaug_ref,
    kt_ref,
    q_ref,
    lse_ref,
    do_ref,
    delta_ref,
    slot_ref,
    gl_ref,
    order_ref,
    columns_ref,
    own_ref,
    other_ref,
    r_ref,
    *rest,
):
    *grad_refs, qaug, daug, dq, dkt, dvt, w_acc, w_ref, sems = rest
    micro = pl.program_id(0)
    step = pl.program_id(1)
    blocks = pl.num_programs(1)
    block = blocks - 1 - step
    length = lens[micro]
    span = hid_ref.shape[2]
    experts = slot_ref.shape[2]
    width = q_ref.shape[2]
    rows = q_ref.shape[3]
    picks = rows // span
    head = experts * width

    def clear():
        w_acc[...] = jnp.zeros_like(w_acc)

    copies = half_copies(ids[2], sems, [(own_ref, other_ref, w_ref)])
    start_all((micro == 0) & (step == 0), copies, clear)

    @pl.when(step == 0)
    def _():
        dkt[...] = jnp.zeros_like(dkt)
        dvt[...] = jnp.zeros_like(dvt)

    @pl.when(block * span >= length)
    def _():
        r_ref[...] = jnp.zeros_like(r_ref)

    @pl.when(block * span < length)
    def _():
        side = lax.broadcasted_iota(jnp.int32, (width, rows), 0)
        qaug[0:width, :] = q_ref[0, 0]
        high, middle, low = split_three(-lse_ref[0, 0])
        qaug[width : 2 * width, :] = jnp.where(
            side == 0,
            1.0,
            jnp.where(side == 1, high, jnp.where(side == 2, middle, jnp.where(side == 3, low, 0.0))),
        ).astype(BF16)
        daug[0:width, :] = do_ref[0, 0]
        high, middle, low = split_three(-delta_ref[0, 0])
        daug[width : 2 * width, :] = jnp.where(
            side == 0, high, jnp.where(side == 1, middle, jnp.where(side == 2, low, 0.0))
        ).astype(BF16)

        lanes = 256
        causal = lax.broadcasted_iota(jnp.int32, (span, lanes), 0) <= (
            lax.broadcasted_iota(jnp.int32, (span, lanes), 1) & (span - 1)
        )

        def key_step(at, diagonal):
            dv = dvt[at]
            dk = dkt[at]
            cuts = [slice(start, start + lanes) for start in range(0, rows, lanes)]

            def ahead(cut):
                return dot_nn(kaug_ref[0, at], qaug[:, cut]), dot_nn(vaug_ref[0, at], daug[:, cut])

            held = ahead(cuts[0])
            back = None
            for n in range(len(cuts) + 1):
                scores, dprobs = held if held is not None else (None, None)
                held = ahead(cuts[n + 1]) if n + 1 < len(cuts) else None
                fresh = None
                if n < len(cuts):
                    probs = jnp.exp(scores)
                    if diagonal:
                        probs = jnp.where(causal, probs, 0.0)
                    slopes = (probs * dprobs).astype(BF16)
                    fresh = (cuts[n], probs.astype(BF16), slopes)
                if back is not None:
                    cut, probs_b, slopes = back
                    dv = dv + dot_nt(daug[0:width, cut], probs_b)
                    dk = dk + dot_nt(qaug[0:width, cut], slopes)
                    part = dot_nn(kt_ref[0, at], slopes)
                    dq[:, cut] = part if diagonal else dq[:, cut] + part
                back = fresh
            dvt[at] = dv
            dkt[at] = dk

        key_step(block, True)

        def body(at, carry):
            key_step(at, False)
            return carry

        lax.fori_loop(0, block, body, 0)
        dq[...] = dq[...] * (width**-0.5)
        slot = slot_ref[0, 0]
        for expert in range(experts):
            r_ref[0, 0, expert * width : (expert + 1) * width, :] = spread_slots(
                lambda pick: dq[:, pick * span : (pick + 1) * span],
                slot,
                expert,
                picks,
                width,
                span,
            ).astype(BF16)
        r_ref[0, 0, head : head + width, :] = dkt[block].astype(BF16)
        r_ref[0, 0, head + width : head + 2 * width, :] = dvt[block].astype(BF16)
        tail = r_ref.shape[2] - head - 2 * width
        r_ref[0, 0, head + 2 * width :, :] = jnp.concatenate(
            [gl_ref[0, 0], jnp.zeros((tail - experts, span), F32)], 0
        ).astype(BF16)
        summing = jnp.concatenate([hid_ref[0, 0].T, jnp.ones((16, span), BF16)], 0)
        w_acc[:, : r_ref.shape[2]] += dot_nt(summing, r_ref[0, 0])

    @pl.when((micro == pl.num_programs(0) - 1) & (step == blocks - 1))
    def _():
        for copy in copies:
            copy.wait()
        model = hid_ref.shape[3]
        used = r_ref.shape[2]
        low, high = halves(w_ref)
        token_sum = w_acc[model : model + 1, :used]
        gain_sum, shift_sum = [], []
        for at, part in ((0, low), (model // 2, high)):
            weight = part[...].T.astype(F32)
            total = w_acc[at : at + model // 2, :used]
            gain_sum.append(jnp.sum(weight * total, 1, keepdims=True))
            shift_sum.append(jnp.sum(weight * token_sum, 1, keepdims=True))
        gain_sum, shift_sum = jnp.concatenate(gain_sum, 0), jnp.concatenate(shift_sum, 0)
        columns = columns_ref[...]
        gain, shift = columns[:, experts : experts + 1], columns[:, experts + 1 : experts + 2]
        gain_sum = (gain_sum - shift * shift_sum) / gain
        lane = lax.broadcasted_iota(jnp.int32, columns.shape, 1)
        columns = jnp.where(
            lane == experts, gain_sum, jnp.where(lane == experts + 1, shift_sum, columns)
        )
        routed = head + 2 * width
        spare = order_ref.shape[0]
        router = w_acc[:model, routed : routed + spare].astype(BF16)
        w_acc[:model, routed:] = columns + dot_nn(router, order_ref[...])
        if len(grad_refs) == 1:
            grad_refs[0][...] = w_acc[:model, :].astype(BF16)
            return
        targets = grad_refs[0].shape[0] * grad_refs[0].shape[1]
        shared_rows = model // (2 * targets)

        def pack(ref, to, fro, shared, heads):
            rows, columns = heads_chunk(model, head, ref)
            at = pack_tiles(ref, to, 0, w_acc, heads * rows, rows, fro * columns, columns)
            pack_tiles(ref, to, at, w_acc, shared * shared_rows, shared_rows, head, w_acc.shape[1] - head)

        for_targets(ids, grad_refs, pack)


def input_kernel(
    ids, x_ref, mid_ref, r_ref, own_ref, other_ref, vec_ref, out_ref, w_ref, sems
):
    first = (pl.program_id(0) == 0) & (pl.program_id(1) == 0)
    copies = half_copies(ids[0], sems, [(own_ref, other_ref, w_ref)])
    start_all(first, copies)

    wait_all(first, copies)
    subs, span, model = x_ref.shape[1:]
    normed, spread = normalize(x_ref[0].reshape(subs * span, model).astype(F32))
    low, high = halves(w_ref)
    routed = r_ref[0, 0]
    back = jnp.concatenate([dot_tn(routed, low[...]), dot_tn(routed, high[...])], 1)
    scaled = back * vec_ref[0:1, :]
    total = mid_ref[0].reshape(subs * span, model) + spread * (
        scaled
        - jnp.mean(scaled, -1, keepdims=True)
        - normed * jnp.mean(scaled * normed, -1, keepdims=True)
    )
    out_ref[0] = total.reshape(subs, span, model)


def finish_kernel(experts, deep, *refs):
    parts, (heads_ref, kv_ref, router_ref, up_shift_ref, *vector_refs) = refs[:-9], refs[-9:]
    total = parts[0][...].astype(F32)
    for part in parts[1:]:
        total = total + part[...].astype(F32)
    _, own_experts, rows, width = heads_ref.shape
    per_tile = 128 // width
    for expert in range(own_experts):
        at = expert // per_tile * rows
        lane = expert % per_tile * width
        heads_ref[0, expert] = total[at : at + rows, lane : lane + width]
    at = own_experts // per_tile * rows
    chunk = kv_ref.shape[1]
    kv_ref[0] = total[at : at + chunk]
    tile = total[at + chunk : at + 2 * chunk]
    router_ref[0] = tile[:, :experts]
    turned = tile.T
    for ref, row in zip(vector_refs, range(experts, experts + 5)):
        ref[...] = turned[row : row + 1]
    up_shift_ref[...] = jnp.concatenate(
        [turned[row : row + 1] for row in range(experts + 5, experts + 5 + deep)], 1
    )


def full(shape):
    return pl.BlockSpec(shape, lambda *ids: (0,) * len(shape))


def blocked(shape):
    tail = (0,) * (len(shape) - 2)
    return pl.BlockSpec((1, 1) + tuple(shape[2:]), lambda m, i, *refs: (m, i) + tail)


def grouped(shape, group):
    tail = (0,) * (len(shape) - 2)
    return pl.BlockSpec((1, group) + tuple(shape[2:]), lambda m, i, *refs: (m, i) + tail)


def in_place():
    return pl.BlockSpec(memory_space=pl.ANY)


def reversed_blocks(shape):
    tail = (0,) * (len(shape) - 2)
    last = shape[1] - 1
    return pl.BlockSpec((1, 1) + tuple(shape[2:]), lambda m, i, *refs: (m, last - i) + tail)


def whole(shape):
    tail = (0,) * (len(shape) - 1)
    return pl.BlockSpec((1,) + tuple(shape[1:]), lambda m, i, *refs: (m,) + tail)


def struct(shape, dtype):
    return jax.ShapeDtypeStruct(shape, dtype)


def params():
    return pltpu.CompilerParams(
        dimension_semantics=("arbitrary", "arbitrary"), vmem_limit_bytes=VMEM_BYTES
    )


def cost(flops, transcendentals, moved):
    return pl.CostEstimate(flops=flops, transcendentals=transcendentals, bytes_accessed=moved)


def exchange(value, axis, distance):
    count = lax.axis_size(axis)
    return lax.ppermute(value, axis, [(at, at ^ distance) for at in range(count)])


def permute_groups(value, index):
    groups = value.shape[0]
    bit = 1
    while bit < groups:
        pairs = value.reshape((groups // (2 * bit), 2, bit) + value.shape[1:])
        value = jnp.where((index & bit) != 0, pairs[:, ::-1].reshape(value.shape), value)
        bit *= 2
    return value


def pick_at(value, index, dim):
    return lax.dynamic_index_in_dim(value, index, dim, keepdims=False)


def reduce_axis(value, axis, dim, relative=False, keep=False):
    count = lax.axis_size(axis)
    me = lax.axis_index(axis)
    base = 0 if relative else me
    total = pick_at(value, base, dim).astype(F32)
    for distance in range(1, count):
        sent = pick_at(value, distance if relative else me ^ distance, dim)
        total = total + exchange(sent, axis, distance).astype(F32)
    return total if keep else total.astype(BF16)


def core_stage(grads):
    keep, send = grads
    other = exchange(send, "fsdp", 1)
    return [(keep[at].astype(F32) + other[at].astype(F32)).astype(BF16) for at in range(keep.shape[0])]


def split_targets(value, axis):
    return [value[at] for at in range(lax.axis_size(axis))]


def send_stage(parts, axis):
    return [exchange(parts[distance], axis, distance) for distance in range(1, len(parts))]


def total_up(own, received):
    total = own.astype(F32)
    for part in received:
        total = total + part.astype(F32)
    return total


def add_up(own, received):
    return total_up(own, received).astype(BF16)


def open_tiles(value, at, rows, columns):
    count = columns // 128
    tiles = value[at : at + count * rows].reshape(count, rows, 128)
    return jnp.swapaxes(tiles, 0, 1).reshape(rows, columns), at + count * rows


def local(
    inputs,
    lengths,
    routes,
    ln1_gain,
    ln1_bias,
    kv_weight,
    router_weight,
    query_weight,
    out_weight,
    ln2_gain,
    ln2_bias,
    up_weight,
    up_bias,
    down_weight,
    down_bias,
    out_cotangent,
):
    micro_count, _, slots, model = inputs.shape
    experts = router_weight.shape[2]
    width = query_weight.shape[3]
    picks = routes.shape[4]
    hidden_units = up_weight.shape[2]
    dp_size, z_size, f_size = (lax.axis_size(axis) for axis in AXES)
    dp_at, z_at, f_at = (lax.axis_index(axis) for axis in AXES)
    ids = jnp.stack([dp_at, z_at, f_at]).astype(jnp.int32)
    seq_index = (dp_at * z_size + z_at) * f_size + f_at
    devices = dp_size * z_size * f_size
    own_experts = experts // z_size
    half = model // f_size
    span = min(BLOCK, slots)
    blocks = slots // span
    rows = picks * span
    group = 2 if blocks % 2 == 0 else 1
    head = experts * width
    spare = -(-experts // 16) * 16
    all_rows = head + 2 * width + spare
    chunk = model // devices
    aligned = chunk % 16 == 0 and (head // z_size) % 128 == 0
    lens = lax.dynamic_index_in_dim(lengths, seq_index, 1, keepdims=False)

    def both_halves(own, other, dim):
        near = jnp.concatenate([own, other], dim)
        return jnp.where(f_at == 0, near, jnp.concatenate([other, own], dim))

    def head_parts(own):
        return [own] + [exchange(own, "expert", distance) for distance in range(1, z_size)]

    def transposed(weight):
        return jnp.swapaxes(weight[0], 1, 2).reshape(own_experts * width, half)

    def start_of(routes):
        local_routes = routes[0, :, 0]
        group = (local_routes // own_experts) ^ z_at
        local_routes = group * own_experts + local_routes % own_experts
        return jnp.swapaxes(local_routes.reshape(micro_count, blocks, span, picks), 2, 3)

    query_parts = head_parts(transposed(query_weight))
    router_t = router_weight[0].T.reshape(z_size, own_experts, half)
    router_t = permute_groups(router_t, z_at).reshape(experts, half)
    router_t = jnp.pad(router_t, ((0, spare - experts), (0, 0)))
    vectors = jnp.concatenate([ln1_gain, ln1_bias, ln2_gain, ln2_bias, down_bias], 0)
    small = jnp.concatenate([vectors, up_bias.reshape(-1, half)], 0)
    small_other = exchange(small, "fsdp", 1)
    vectors = both_halves(vectors, small_other[:5], 1).astype(F32)
    up_shift = both_halves(up_bias, small_other[5:].reshape(1, -1), 1).astype(F32)

    up_other = exchange(up_weight[0], "fsdp", 1)
    down_other = exchange(down_weight[0], "fsdp", 1)
    route_t = start_of(routes)
    lens, ids, route_t, vectors, up_shift, router_t, *query_parts = lax.optimization_barrier(
        (lens, ids, route_t, vectors, up_shift, router_t, *query_parts)
    )
    proj = jnp.concatenate(query_parts + [kv_weight[0].T, router_t], 0)
    proj_other = exchange(proj, "fsdp", 1)
    own_out, proj_other = lax.optimization_barrier((transposed(out_weight), proj_other))
    out_parts = head_parts(own_out)

    states = inputs.reshape(micro_count, blocks, span, model)
    cotangent = out_cotangent.reshape(micro_count, blocks, span, model)

    grid = (micro_count, blocks)
    hid_s = struct((micro_count, blocks, span, model), BF16)
    aug_s = struct((micro_count, blocks, span, 2 * width), BF16)
    kt_s = struct((micro_count, blocks, 1, width, span), BF16)
    q_s = struct((micro_count, blocks, width, rows), BF16)
    row_s = struct((micro_count, blocks, 1, rows), F32)
    gate_s = struct((micro_count, blocks, experts, span), F32)
    slot_s = struct((micro_count, blocks, experts, span), jnp.int32)
    tokens = micro_count * slots
    pair_flops = tokens * picks * slots * width
    hid, kaug, vaug, kt, q, ctx, lse, gates, slot = pl.pallas_call(
        forward_kernel,
        name="forward",
        grid_spec=pltpu.PrefetchScalarGridSpec(
            num_scalar_prefetch=2,
            grid=grid,
            in_specs=[
                blocked(states.shape),
                blocked(route_t.shape),
                full(vectors.shape),
                in_place(),
                in_place(),
            ],
            out_specs=[
                blocked(hid_s.shape),
                whole(aug_s.shape),
                whole(aug_s.shape),
                blocked(kt_s.shape),
                blocked(q_s.shape),
                blocked(q_s.shape),
                blocked(row_s.shape),
                blocked(gate_s.shape),
                blocked(slot_s.shape),
            ],
            scratch_shapes=[
                pltpu.VMEM((all_rows, span), F32),
                pltpu.VMEM((2 * width, rows), BF16),
                pltpu.VMEM((blocks, span, rows), F32),
                pltpu.VMEM((blocks, width, span), BF16),
                pltpu.VMEM((width, rows), F32),
                pltpu.VMEM((2 * all_rows, half), BF16),
                pltpu.SemaphoreType.DMA((2,)),
            ],
        ),
        out_shape=[hid_s, aug_s, aug_s, kt_s, q_s, q_s, row_s, gate_s, slot_s],
        compiler_params=params(),
        cost_estimate=cost(2 * tokens * model * all_rows + 16 * pair_flops, 0, 64 << 20),
    )(lens, ids, states, route_t, vectors, proj, proj_other)

    ctx, *out_parts = lax.optimization_barrier((ctx, *out_parts))
    out_proj = jnp.concatenate(out_parts, 0)
    out_other = exchange(out_proj, "fsdp", 1)
    state_s = struct((micro_count, blocks, span, model), F32)
    mid_rows = chunk * hidden_units * 2 // 128 + head // z_size * (chunk * z_size) // 128
    late_rows = head // z_size * (chunk * z_size) // 128 + 2 * chunk
    if aligned:
        mid_grads = [struct((dp_size, z_size, mid_rows, 128), BF16)] * 2
        late_grads = [struct((dp_size, z_size, late_rows, 128), BF16)] * 2
    else:
        mid_grads = [
            struct((hidden_units, model), BF16),
            struct((model, hidden_units), BF16),
            struct((model, head), BF16),
        ]
        late_grads = [struct((model, head + 2 * width + 128), BF16)]
    outputs, mid, grad_ctx, delta, grad_logits, small2, up_small, *mid_grads = pl.pallas_call(
        middle_kernel,
        name="middle",
        grid_spec=pltpu.PrefetchScalarGridSpec(
            num_scalar_prefetch=2,
            grid=(micro_count, blocks // group),
            in_specs=[
                grouped(states.shape, group),
                grouped(q_s.shape, group),
                grouped(gate_s.shape, group),
                grouped(slot_s.shape, group),
                grouped(cotangent.shape, group),
                in_place(),
                in_place(),
                full(vectors.shape),
                in_place(),
                in_place(),
                full(up_shift.shape),
                in_place(),
                in_place(),
            ],
            out_specs=[
                grouped(state_s.shape, group),
                grouped(state_s.shape, group),
                grouped(q_s.shape, group),
                grouped(row_s.shape, group),
                grouped(gate_s.shape, group),
                full((3, 8, model)),
                full((8, hidden_units)),
            ]
            + [full(leaf.shape) for leaf in mid_grads],
            scratch_shapes=[
                pltpu.VMEM((group, width, rows), F32),
                pltpu.VMEM((head, group * span), BF16),
                pltpu.VMEM((head, group * span), F32),
                pltpu.VMEM((hidden_units, model), F32),
                pltpu.VMEM((model, hidden_units), F32),
                pltpu.VMEM((model, head), F32),
                pltpu.VMEM((2 * head, half), BF16),
                pltpu.VMEM((model, hidden_units), BF16),
                pltpu.VMEM((hidden_units, model), BF16),
                pltpu.SemaphoreType.DMA((6,)),
            ],
        ),
        out_shape=[
            state_s,
            state_s,
            q_s,
            row_s,
            gate_s,
            struct((3, 8, model), F32),
            struct((8, hidden_units), F32),
        ]
        + mid_grads,
        compiler_params=params(),
        cost_estimate=cost(2 * tokens * model * (6 * hidden_units + 3 * head), 0, 200 << 20),
    )(
        lens,
        ids,
        states,
        ctx,
        gates,
        slot,
        cotangent,
        out_proj,
        out_other,
        vectors,
        up_weight[0],
        up_other,
        up_shift,
        down_weight[0],
        down_other,
    )

    if aligned:
        mid_sums = core_stage(mid_grads)
        grad_ctx, *mid_sums = lax.optimization_barrier((grad_ctx, *mid_sums))
        mid_received = send_stage(mid_sums, "dp")

    expert_id = jnp.arange(experts)
    moved = ((expert_id // own_experts) ^ z_at) * own_experts + expert_id % own_experts
    order = jnp.pad(
        (jnp.arange(spare)[:, None] == moved[None, :]).astype(BF16), ((0, 0), (0, 128 - experts))
    )
    deep = hidden_units // model
    columns = jnp.concatenate(
        [
            vectors[:2].T,
            jnp.sum(small2, 1).T,
            jnp.swapaxes(jnp.sum(up_small, 0).reshape(devices, deep, chunk), 1, 2).reshape(model, deep),
        ],
        1,
    )
    columns = jnp.pad(columns, ((0, 0), (experts, 128 - experts - 5 - deep)))
    r_s = struct((micro_count, blocks // group, all_rows, group * span), BF16)

    def routed_block(m, i, *refs):
        block = blocks - 1 - i
        return m, block // group, 0, block % group

    routed, *late_grads = pl.pallas_call(
        backward_kernel,
        name="backward",
        grid_spec=pltpu.PrefetchScalarGridSpec(
            num_scalar_prefetch=2,
            grid=grid,
            in_specs=[
                reversed_blocks(hid_s.shape),
                whole(aug_s.shape),
                whole(aug_s.shape),
                whole((micro_count, blocks, width, span)),
                reversed_blocks(q_s.shape),
                reversed_blocks(row_s.shape),
                reversed_blocks(q_s.shape),
                reversed_blocks(row_s.shape),
                reversed_blocks(slot_s.shape),
                reversed_blocks(gate_s.shape),
                full(order.shape),
                full(columns.shape),
                in_place(),
                in_place(),
            ],
            out_specs=[pl.BlockSpec((1, 1, all_rows, span), routed_block)]
            + [full(leaf.shape) for leaf in late_grads],
            scratch_shapes=[
                pltpu.VMEM((2 * width, rows), BF16),
                pltpu.VMEM((2 * width, rows), BF16),
                pltpu.VMEM((width, rows), F32),
                pltpu.VMEM((blocks, width, span), F32),
                pltpu.VMEM((blocks, width, span), F32),
                pltpu.VMEM((model + 16, head + 2 * width + 128), F32),
                pltpu.VMEM((2 * all_rows, half), BF16),
                pltpu.SemaphoreType.DMA((2,)),
            ],
        ),
        out_shape=[r_s] + late_grads,
        compiler_params=params(),
        cost_estimate=cost(2 * tokens * model * all_rows + 40 * pair_flops, 0, 100 << 20),
    )(
        lens,
        ids,
        hid,
        kaug,
        vaug,
        kt.reshape(micro_count, blocks, width, span),
        q,
        lse,
        grad_ctx,
        delta,
        slot,
        grad_logits,
        order,
        columns,
        proj,
        proj_other,
    )

    if aligned:
        *mid_received, late_grads[0], late_grads[1] = lax.optimization_barrier(
            (*mid_received, *late_grads)
        )
        *mid_received, late_grads[0], late_grads[1] = lax.optimization_barrier(
            (*mid_received, *late_grads)
        )
        late_sums = core_stage(late_grads)
        *mid_received, late_sums[0] = lax.optimization_barrier((*mid_received, late_sums[0]))
        mid_sums = split_targets(add_up(mid_sums[0], mid_received), "expert")
        routed, *sums = lax.optimization_barrier((routed, *mid_sums, *late_sums))
        mid_sums, late_sums = sums[:z_size], sums[z_size:]
        mid_received = send_stage(mid_sums, "expert")
        late_received = send_stage(late_sums, "dp")

    input_grad = pl.pallas_call(
        input_kernel,
        name="input_back",
        grid_spec=pltpu.PrefetchScalarGridSpec(
            num_scalar_prefetch=1,
            grid=(micro_count, blocks // group),
            in_specs=[
                grouped(states.shape, group),
                grouped(state_s.shape, group),
                blocked(r_s.shape),
                in_place(),
                in_place(),
                full(vectors.shape),
            ],
            out_specs=grouped(state_s.shape, group),
            scratch_shapes=[
                pltpu.VMEM((2 * all_rows, half), BF16),
                pltpu.SemaphoreType.DMA((2,)),
            ],
        ),
        out_shape=state_s,
        compiler_params=params(),
        cost_estimate=cost(2 * tokens * model * all_rows, 0, 40 << 20),
    )(ids[2:], states, mid, routed, proj, proj_other, vectors)

    def open_heads(value):
        return jnp.swapaxes(value.reshape(-1, own_experts, width), 0, 1)[None]

    if aligned:
        input_grad, *received = lax.optimization_barrier(
            (input_grad, *late_received, *mid_received)
        )
        late_received = received[: dp_size - 1]
        mid_received = received[dp_size - 1 :]
        late_sums = split_targets(add_up(late_sums[0], late_received), "expert")
        late_received = send_stage(late_sums, "expert")
        mid_total = total_up(mid_sums[0], mid_received)
        up_weight_grad, at = open_tiles(mid_total, 0, chunk, hidden_units)
        down_weight_grad, at = open_tiles(mid_total, at, hidden_units // devices, model)
        out_weight_grad, at = open_tiles(mid_total, at, chunk * z_size, head // z_size)
        out_weight_grad = open_heads(out_weight_grad)
        query_weight_grad, kv_grad, router_grad, up_bias_grad, *small = pl.pallas_call(
            functools.partial(finish_kernel, experts, deep),
            name="finish",
            out_shape=[
                struct((1, own_experts, chunk * z_size, width), F32),
                struct((1, chunk, 2 * width), F32),
                struct((1, chunk, experts), F32),
                struct((1, deep * chunk), F32),
            ]
            + [struct((1, chunk), F32)] * 5,
        )(late_sums[0], *late_received)
    else:
        down_grad, up_grad, wo_grad = mid_grads
        w_grad = late_grads[0]

        def reduce_shared(value, part):
            value = value.reshape(dp_size, z_size, f_size, part, value.shape[1])
            value = reduce_axis(value, "fsdp", 2)
            value = reduce_axis(value, "dp", 0)
            return reduce_axis(value, "expert", 0, keep=True)

        def reduce_heads(value):
            value = value.reshape(dp_size, f_size, chunk * z_size, z_size, own_experts * width)
            value = reduce_axis(value, "fsdp", 1)
            value = reduce_axis(value, "dp", 0)
            return open_heads(reduce_axis(value, "expert", 1, relative=True, keep=True))

        up_weight_grad = reduce_shared(up_grad, chunk)
        down_weight_grad = reduce_shared(down_grad, hidden_units // devices)
        out_weight_grad = reduce_heads(wo_grad)
        query_weight_grad = reduce_heads(w_grad[:, :head])
        narrow = reduce_shared(w_grad[:, head:], chunk)
        kv_grad, router_grad = narrow[None, :, : 2 * width], narrow[None, :, 2 * width :]
        small = [router_grad[:, :, experts + at] for at in range(5)]
        up_bias_grad = router_grad[0, :, experts + 5 : experts + 5 + deep].T.reshape(1, -1)
        router_grad = router_grad[:, :, :experts]
    shape = (micro_count, 1, slots, model)
    return (
        outputs.reshape(shape),
        input_grad.reshape(shape),
        small[0],
        small[1],
        kv_grad,
        router_grad,
        query_weight_grad,
        out_weight_grad,
        small[2],
        small[3],
        up_weight_grad[None],
        up_bias_grad,
        down_weight_grad[None],
        small[4],
    )


def solution(mesh):
    shards = P(None, AXES, None, None)
    return jax.shard_map(
        local,
        mesh=mesh,
        in_specs=(
            shards,
            P(),
            P(None, None, AXES, None, None),
            P(None, "fsdp"),
            P(None, "fsdp"),
            P(None, "fsdp", None),
            P(None, "fsdp", None),
            P(None, "expert", "fsdp", None),
            P(None, "expert", "fsdp", None),
            P(None, "fsdp"),
            P(None, "fsdp"),
            P(None, "fsdp", None),
            P(None, "fsdp"),
            P(None, "fsdp", None),
            P(None, "fsdp"),
            shards,
        ),
        out_specs=(
            shards,
            shards,
            P(None, AXES),
            P(None, AXES),
            P(None, AXES, None),
            P(None, AXES, None),
            P(None, "expert", ("dp", "fsdp"), None),
            P(None, "expert", ("dp", "fsdp"), None),
            P(None, AXES),
            P(None, AXES),
            P(None, AXES, None),
            P(None, AXES),
            P(None, AXES, None),
            P(None, AXES),
        ),
        check_vma=False,
    )
```

```python
import functools

import jax
import jax.numpy as jnp
from jax import lax
from jax.experimental import pallas as pl
from jax.experimental.pallas import tpu as pltpu
from jax.sharding import PartitionSpec as P

EPSILON = 1e-05
NEGATIVE = -1e30
GELU_SCALE = 0.7978845608028654
GELU_CUBIC = 0.044715
BLOCK = 256
AXES = ("dp", "expert", "fsdp")
F32 = jnp.float32
BF16 = jnp.bfloat16
VMEM_BYTES = 60 << 20


def dot_nn(left, right):
    return lax.dot_general(left, right, (((1,), (0,)), ((), ())), preferred_element_type=F32)


def dot_nt(left, right):
    return lax.dot_general(left, right, (((1,), (1,)), ((), ())), preferred_element_type=F32)


def dot_tn(left, right):
    return lax.dot_general(left, right, (((0,), (0,)), ((), ())), preferred_element_type=F32)


def normalize(values):
    center = values - jnp.mean(values, -1, keepdims=True)
    spread = lax.rsqrt(jnp.mean(center * center, -1, keepdims=True) + EPSILON)
    return center * spread, spread


def halves(ref):
    rows = ref.shape[0] // 2
    return ref.at[pl.ds(0, rows)], ref.at[pl.ds(rows, rows)]


def fold_rows(values, combine):
    rows, columns = values.shape
    return combine(values.reshape(rows // 8, 8, columns), 0)


def pick_slots(table_ref, slot, picks, width, start=0):
    experts, span = slot.shape
    lanes = slice(start, start + span)
    slot = slot.astype(table_ref.dtype)
    picked = []
    for pick in range(picks):
        value = table_ref[pick * width : (pick + 1) * width, lanes]
        for expert in range(pick + 1, experts - picks + pick + 1):
            hit = jnp.broadcast_to(slot[expert : expert + 1, :], (width, span)) == pick
            value = jnp.where(hit, table_ref[expert * width : (expert + 1) * width, lanes], value)
        picked.append(value)
    return picked


def spread_slots(read, slot, expert, picks, width, span):
    experts = slot.shape[0]
    row = jnp.broadcast_to(slot[expert : expert + 1, :], (width, span))
    value = jnp.zeros((width, span), slot.dtype)
    for pick in range(max(0, expert - experts + picks), min(expert, picks - 1) + 1):
        value = jnp.where(row == pick, read(pick), value)
    return value


def forward_kernel(
    lens,
    ids,
    x_ref,
    route_ref,
    vec_ref,
    own_ref,
    other_ref,
    hid_ref,
    kaug_ref,
    vaug_ref,
    kt_ref,
    q_ref,
    ctx_ref,
    lse_ref,
    gate_ref,
    slot_ref,
    table,
    qaug,
    scores,
    vt,
    acc,
    w_ref,
    sems,
):
    block = pl.program_id(1)
    length = lens[pl.program_id(0)]
    first = (pl.program_id(0) == 0) & (block == 0)
    copies = half_copies(ids[2], sems, [(own_ref, other_ref, w_ref)])
    start_all(first, copies)
    wait_all(first, copies)
    span = x_ref.shape[2]
    experts = slot_ref.shape[2]
    picks = route_ref.shape[2]
    width = kt_ref.shape[3]
    half = w_ref.shape[1]
    low, high = halves(w_ref)
    rows = picks * span

    normed, _ = normalize(x_ref[0, 0].astype(F32))
    hid = (normed * vec_ref[0:1, :] + vec_ref[1:2, :]).astype(BF16)
    hid_ref[0, 0] = hid
    head = experts * width
    products = dot_nt(low[...], hid[:, :half]) + dot_nt(high[...], hid[:, half:])
    table[...] = products[:head].astype(BF16)
    kt_ref[0, 0, 0] = products[head : head + width, :].astype(BF16)
    vt[block] = products[head + width : head + 2 * width, :].astype(BF16)

    lane = lax.broadcasted_iota(jnp.int32, (span, 2 * width), 1)
    place = block * span + lax.broadcasted_iota(jnp.int32, (span, 2 * width), 0)
    ones = jnp.where(lane < width + 4, 1.0, 0.0)
    cut = jnp.where(place < length, 0.0, NEGATIVE)
    both = dot_nt(hid[:, :half], low[head : head + 2 * width, :])
    both = both + dot_nt(hid[:, half:], high[head : head + 2 * width, :])
    keys = jnp.where(lane < width, both, jnp.where(lane == width, cut, ones))
    kaug_ref[0, block] = keys.astype(BF16)
    vals = jnp.where(lane < width, pltpu.roll(both, width, 1), ones)
    vaug_ref[0, block] = vals.astype(BF16)

    logits = products[head + 2 * width : head + 2 * width + experts, :]
    expert_id = lax.broadcasted_iota(jnp.int32, (experts, span), 0)
    chosen = jnp.zeros((experts, span), F32)
    for pick in range(picks):
        chosen = jnp.where(expert_id == route_ref[0, 0, pick : pick + 1, :], 1.0, chosen)
    lower = jnp.where(
        lax.broadcasted_iota(jnp.int32, (experts, experts), 1)
        < lax.broadcasted_iota(jnp.int32, (experts, experts), 0),
        1.0,
        0.0,
    )
    slot = jnp.where(chosen > 0.0, dot_nn(lower, chosen), -1.0).astype(jnp.int32)
    slot_ref[0, 0] = slot
    masked = jnp.where(chosen > 0.0, logits, NEGATIVE)
    raised = jnp.where(chosen > 0.0, jnp.exp(masked - jnp.max(masked, 0, keepdims=True)), 0.0)
    gate_ref[0, 0] = raised / jnp.sum(raised, 0, keepdims=True)

    picked = pick_slots(table, slot, picks, width)
    for pick in range(picks):
        qaug[0:width, pick * span : (pick + 1) * span] = (
            picked[pick] * (width**-0.5)
        ).astype(BF16)
    q_ref[0, 0] = qaug[0:width, :]
    side = lax.broadcasted_iota(jnp.int32, (width, rows), 0)
    qaug[width : 2 * width, :] = jnp.where(side == 0, 1.0, 0.0).astype(BF16)

    def score_step(at, top):
        part = dot_nn(kaug_ref[0, at], qaug[...])
        scores[at] = part
        return jnp.maximum(top, fold_rows(part, jnp.max))

    used = jnp.minimum(block, (length + span - 1) // span)
    top = lax.fori_loop(0, used, score_step, jnp.full((8, rows), NEGATIVE, F32))
    causal = lax.broadcasted_iota(jnp.int32, (span, rows), 0) <= (
        lax.broadcasted_iota(jnp.int32, (span, rows), 1) & (span - 1)
    )
    part = jnp.where(causal, dot_nn(kaug_ref[0, block], qaug[...]), NEGATIVE)
    top = jnp.maximum(top, fold_rows(part, jnp.max))
    top = jnp.max(top, 0, keepdims=True)
    raised = jnp.exp(part - top)
    acc[...] = dot_nn(vt[block], raised.astype(BF16))
    total = fold_rows(raised, jnp.sum)

    def value_step(at, total):
        raised = jnp.exp(scores[at] - top)
        acc[...] += dot_nn(vt[at], raised.astype(BF16))
        return total + fold_rows(raised, jnp.sum)

    total = lax.fori_loop(0, used, value_step, total)
    total = jnp.sum(total, 0, keepdims=True)
    ctx_ref[0, 0] = (acc[...] * (1.0 / total)).astype(BF16)
    lse_ref[0, 0] = top + jnp.log(total)


def middle_kernel(
    lens,
    ids,
    x_ref,
    ctx_ref,
    gate_ref,
    slot_ref,
    cot_ref,
    own_ref,
    other_ref,
    vec_ref,
    own_up_ref,
    other_up_ref,
    up_shift_ref,
    own_down_ref,
    other_down_ref,
    out_ref,
    mid_ref,
    do_ref,
    delta_ref,
    gl_ref,
    small_ref,
    up_shift_grad_ref,
    *rest,
):
    *grad_refs, gated, cexp, table, down_acc, up_acc, wo_acc, w_ref, up_ref, down_ref, sems = rest
    micro = pl.program_id(0)
    block = pl.program_id(1)
    length = lens[micro]
    subs, span, model = x_ref.shape[1:]
    tokens = subs * span
    experts = slot_ref.shape[2]
    width = ctx_ref.shape[2]
    picks = ctx_ref.shape[3] // span
    head = experts * width
    half = w_ref.shape[1]
    low, high = halves(w_ref)
    first = (micro == 0) & (block == 0)
    last = (micro == pl.num_programs(0) - 1) & (block == pl.num_programs(1) - 1)

    def clear():
        down_acc[...] = jnp.zeros_like(down_acc)
        up_acc[...] = jnp.zeros_like(up_acc)
        wo_acc[...] = jnp.zeros_like(wo_acc)
        small_ref[...] = jnp.zeros_like(small_ref)
        up_shift_grad_ref[...] = jnp.zeros_like(up_shift_grad_ref)

    copies = half_copies(
        ids[2],
        sems,
        [
            (own_ref, other_ref, w_ref),
            (own_up_ref, other_up_ref, up_ref),
            (own_down_ref, other_down_ref, down_ref),
        ],
    )
    start_all(first, copies, clear)
    wait_all(first, copies)
    slots = [slot_ref[0, sub] for sub in range(subs)]
    gate = []
    for sub in range(subs):
        gates = gate_ref[0, sub]
        gate.append(
            [
                jnp.sum(jnp.where(slots[sub] == pick, gates, 0.0), 0, keepdims=True)
                for pick in range(picks)
            ]
        )
        for pick in range(picks):
            at = slice(pick * span, (pick + 1) * span)
            gated[sub, :, at] = (ctx_ref[0, sub, :, at].astype(F32) * gate[sub][pick]).astype(BF16)
        for expert in range(experts):
            cexp[expert * width : (expert + 1) * width, sub * span : (sub + 1) * span] = spread_slots(
                lambda pick: gated[sub, :, pick * span : (pick + 1) * span],
                slots[sub].astype(BF16),
                expert,
                picks,
                width,
                span,
            )
    mixed = x_ref[0].reshape(tokens, model).astype(F32) + jnp.concatenate(
        [dot_tn(cexp[...], low[...]), dot_tn(cexp[...], high[...])], 1
    )
    normed, spread = normalize(mixed)
    hid = (normed * vec_ref[2:3, :] + vec_ref[3:4, :]).astype(BF16)
    place = block * tokens + lax.broadcasted_iota(jnp.int32, (tokens, 1), 0)
    grad = jnp.where(place < length, cot_ref[0].reshape(tokens, model), 0.0)
    grad_b = grad.astype(BF16)
    hid_t = hid.T
    out = mixed + vec_ref[4:5, :]
    back = jnp.zeros_like(mixed)
    hidden_units = up_ref.shape[1]
    step = min(hidden_units, 256)
    cuts = [slice(at, at + step) for at in range(0, hidden_units, step)]

    def ahead(cut):
        return dot_nn(hid, up_ref[:, cut]), dot_nt(grad_b, down_ref[cut, :])

    held = ahead(cuts[0])
    ready = None
    for n in range(len(cuts) + 1):
        pre, grad_act = held if held is not None else (None, None)
        held = ahead(cuts[n + 1]) if n + 1 < len(cuts) else None
        fresh = None
        if n < len(cuts):
            cut = cuts[n]
            pre = pre + up_shift_ref[:, cut]
            square = pre * pre
            bent = jnp.tanh(pre * (GELU_SCALE + (GELU_SCALE * GELU_CUBIC) * square))
            rise = 0.5 + 0.5 * bent
            slope = rise + (0.5 * pre) * (1.0 - bent * bent) * (
                GELU_SCALE + (3.0 * GELU_SCALE * GELU_CUBIC) * square
            )
            grad_pre = grad_act * slope
            up_shift_grad_ref[:, cut] += fold_rows(grad_pre, jnp.sum)
            fresh = (cut, (pre * rise).astype(BF16), grad_pre.astype(BF16))
        if ready is not None:
            cut, active, grad_pre_b = ready
            out = out + dot_nn(active, down_ref[cut, :])
            back = back + dot_nt(grad_pre_b, up_ref[:, cut])
            down_acc[cut, :] += dot_nn(active.T, grad_b)
            up_acc[:, cut] += dot_nn(hid_t, grad_pre_b)
        ready = fresh
    out_ref[0] = out.reshape(subs, span, model)
    scaled = back * vec_ref[2:3, :]
    mid = grad + spread * (
        scaled
        - jnp.mean(scaled, -1, keepdims=True)
        - normed * jnp.mean(scaled * normed, -1, keepdims=True)
    )
    mid_ref[0] = mid.reshape(subs, span, model)
    small_ref[0] += fold_rows(back * normed, jnp.sum)
    small_ref[1] += fold_rows(back, jnp.sum)
    small_ref[2] += fold_rows(grad_b.astype(F32), jnp.sum)

    mid_b = mid.astype(BF16)
    wo_acc[...] += dot_nt(mid_b.T, cexp[...])
    products = dot_nt(low[...], mid_b[:, :half]) + dot_nt(high[...], mid_b[:, half:])
    table[...] = products.astype(BF16)
    for sub in range(subs):
        slot = slots[sub]
        picked = pick_slots(table, slot, picks, width, sub * span)
        grad_gate = []
        for pick in range(picks):
            at = slice(pick * span, (pick + 1) * span)
            ctx = ctx_ref[0, sub, :, at].astype(F32)
            found = picked[pick].astype(F32)
            grad_gate.append(jnp.sum(found * ctx, 0, keepdims=True))
            grad_ctx = (found * gate[sub][pick]).astype(BF16)
            do_ref[0, sub, :, at] = grad_ctx
            delta_ref[0, sub, :, at] = jnp.sum(grad_ctx.astype(F32) * ctx, 0, keepdims=True)
        average = gate[sub][0] * grad_gate[0]
        for pick in range(1, picks):
            average = average + gate[sub][pick] * grad_gate[pick]
        grad_logits = jnp.zeros((experts, span), F32)
        for pick in range(picks):
            grad_logits = jnp.where(
                slot == pick, gate[sub][pick] * (grad_gate[pick] - average), grad_logits
            )
        gl_ref[0, sub] = grad_logits

    @pl.when(last)
    def _():
        if len(grad_refs) == 3:
            for ref, total in zip(grad_refs, (down_acc, up_acc, wo_acc)):
                ref[...] = total[...].astype(BF16)
            return
        targets = grad_refs[0].shape[0] * grad_refs[0].shape[1]
        up_rows = up_acc.shape[0] // (2 * targets)
        down_rows = down_acc.shape[0] // (2 * targets)

        def pack(ref, to, fro, shared, heads):
            at = pack_tiles(ref, to, 0, up_acc, shared * up_rows, up_rows, 0, up_acc.shape[1])
            at = pack_tiles(ref, to, at, down_acc, shared * down_rows, down_rows, 0, down_acc.shape[1])
            rows, columns = heads_chunk(wo_acc.shape[0], head, ref)
            pack_tiles(ref, to, at, wo_acc, heads * rows, rows, fro * columns, columns)

        for_targets(ids, grad_refs, pack)


def half_copies(core, sems, moves):
    copies = []
    for own, other, target in moves:
        half = target.shape[0] // 2
        for source, at in ((own, core), (other, 1 - core)):
            place = target.at[pl.ds(pl.multiple_of(at * half, half), half)]
            copies.append(pltpu.make_async_copy(source, place, sems.at[len(copies)]))
    return copies


def start_all(first, copies, meanwhile=lambda: None):
    @pl.when(first)
    def _():
        for copy in copies:
            copy.start()
        meanwhile()


def wait_all(first, copies):
    @pl.when(first)
    def _():
        for copy in copies:
            copy.wait()


def pack_tiles(ref, to, at, total, row, rows, column, columns):
    row = pl.multiple_of(row, rows)
    for lane in range(0, columns, 128):
        start = column + lane
        if not isinstance(start, int):
            start = pl.multiple_of(start, 128)
        tile = total[pl.ds(row, rows), pl.ds(start, 128)]
        ref[to[0], to[1], at : at + rows, :] = tile.astype(BF16)
        at += rows
    return at


def heads_chunk(model, head, ref):
    return model // (2 * ref.shape[0]), head // ref.shape[1]


def for_targets(ids, refs, pack):
    def body(dp_far, carry):
        dp = dp_far ^ ids[0]
        for z_far in range(refs[0].shape[1]):
            for f_far in range(2):
                f = ids[2] ^ f_far
                shared = (dp * refs[0].shape[1] + (z_far ^ ids[1])) * 2 + f
                pack(refs[f_far], (dp_far, z_far), z_far, shared, dp * 2 + f)
        return carry

    lax.fori_loop(0, refs[0].shape[0], body, 0)


def split_three(values):
    high = values.astype(BF16).astype(F32)
    rest = values - high
    middle = rest.astype(BF16).astype(F32)
    return high, middle, rest - middle


def backward_kernel(
    lens,
    ids,
    hid_ref,
    kaug_ref,
    vaug_ref,
    kt_ref,
    q_ref,
    lse_ref,
    do_ref,
    delta_ref,
    slot_ref,
    gl_ref,
    order_ref,
    columns_ref,
    own_ref,
    other_ref,
    r_ref,
    *rest,
):
    *grad_refs, qaug, daug, dq, dkt, dvt, w_acc, w_ref, sems = rest
    micro = pl.program_id(0)
    step = pl.program_id(1)
    blocks = pl.num_programs(1)
    block = blocks - 1 - step
    length = lens[micro]
    span = hid_ref.shape[2]
    experts = slot_ref.shape[2]
    width = q_ref.shape[2]
    rows = q_ref.shape[3]
    picks = rows // span
    head = experts * width

    def clear():
        w_acc[...] = jnp.zeros_like(w_acc)

    copies = half_copies(ids[2], sems, [(own_ref, other_ref, w_ref)])
    start_all((micro == 0) & (step == 0), copies, clear)

    @pl.when(step == 0)
    def _():
        dkt[...] = jnp.zeros_like(dkt)
        dvt[...] = jnp.zeros_like(dvt)

    @pl.when(block * span >= length)
    def _():
        r_ref[...] = jnp.zeros_like(r_ref)

    @pl.when(block * span < length)
    def _():
        side = lax.broadcasted_iota(jnp.int32, (width, rows), 0)
        qaug[0:width, :] = q_ref[0, 0]
        high, middle, low = split_three(-lse_ref[0, 0])
        qaug[width : 2 * width, :] = jnp.where(
            side == 0,
            1.0,
            jnp.where(side == 1, high, jnp.where(side == 2, middle, jnp.where(side == 3, low, 0.0))),
        ).astype(BF16)
        daug[0:width, :] = do_ref[0, 0]
        high, middle, low = split_three(-delta_ref[0, 0])
        daug[width : 2 * width, :] = jnp.where(
            side == 0, high, jnp.where(side == 1, middle, jnp.where(side == 2, low, 0.0))
        ).astype(BF16)

        lanes = 256
        causal = lax.broadcasted_iota(jnp.int32, (span, lanes), 0) <= (
            lax.broadcasted_iota(jnp.int32, (span, lanes), 1) & (span - 1)
        )

        def key_step(at, diagonal):
            dv = dvt[at]
            dk = dkt[at]
            cuts = [slice(start, start + lanes) for start in range(0, rows, lanes)]

            def ahead(cut):
                return dot_nn(kaug_ref[0, at], qaug[:, cut]), dot_nn(vaug_ref[0, at], daug[:, cut])

            held = ahead(cuts[0])
            back = None
            for n in range(len(cuts) + 1):
                scores, dprobs = held if held is not None else (None, None)
                held = ahead(cuts[n + 1]) if n + 1 < len(cuts) else None
                fresh = None
                if n < len(cuts):
                    probs = jnp.exp(scores)
                    if diagonal:
                        probs = jnp.where(causal, probs, 0.0)
                    slopes = (probs * dprobs).astype(BF16)
                    fresh = (cuts[n], probs.astype(BF16), slopes)
                if back is not None:
                    cut, probs_b, slopes = back
                    dv = dv + dot_nt(daug[0:width, cut], probs_b)
                    dk = dk + dot_nt(qaug[0:width, cut], slopes)
                    part = dot_nn(kt_ref[0, at], slopes)
                    dq[:, cut] = part if diagonal else dq[:, cut] + part
                back = fresh
            dvt[at] = dv
            dkt[at] = dk

        key_step(block, True)

        def body(at, carry):
            key_step(at, False)
            return carry

        lax.fori_loop(0, block, body, 0)
        scaled = (dq[...] * (width**-0.5)).astype(BF16)
        slot = slot_ref[0, 0].astype(BF16)
        for expert in range(experts):
            r_ref[0, 0, expert * width : (expert + 1) * width, :] = spread_slots(
                lambda pick: scaled[:, pick * span : (pick + 1) * span],
                slot,
                expert,
                picks,
                width,
                span,
            )
        r_ref[0, 0, head : head + width, :] = dkt[block].astype(BF16)
        r_ref[0, 0, head + width : head + 2 * width, :] = dvt[block].astype(BF16)
        tail = r_ref.shape[2] - head - 2 * width
        r_ref[0, 0, head + 2 * width :, :] = jnp.concatenate(
            [gl_ref[0, 0], jnp.zeros((tail - experts, span), F32)], 0
        ).astype(BF16)
        summing = jnp.concatenate([hid_ref[0, 0].T, jnp.ones((16, span), BF16)], 0)
        w_acc[:, : r_ref.shape[2]] += dot_nt(summing, r_ref[0, 0])

    @pl.when((micro == pl.num_programs(0) - 1) & (step == blocks - 1))
    def _():
        for copy in copies:
            copy.wait()
        model = hid_ref.shape[3]
        used = r_ref.shape[2]
        low, high = halves(w_ref)
        token_sum = w_acc[model : model + 1, :used]
        gain_sum, shift_sum = [], []
        for at, part in ((0, low), (model // 2, high)):
            weight = part[...].T.astype(F32)
            total = w_acc[at : at + model // 2, :used]
            gain_sum.append(jnp.sum(weight * total, 1, keepdims=True))
            shift_sum.append(jnp.sum(weight * token_sum, 1, keepdims=True))
        gain_sum, shift_sum = jnp.concatenate(gain_sum, 0), jnp.concatenate(shift_sum, 0)
        columns = columns_ref[...]
        gain, shift = columns[:, experts : experts + 1], columns[:, experts + 1 : experts + 2]
        gain_sum = (gain_sum - shift * shift_sum) / gain
        lane = lax.broadcasted_iota(jnp.int32, columns.shape, 1)
        columns = jnp.where(
            lane == experts, gain_sum, jnp.where(lane == experts + 1, shift_sum, columns)
        )
        routed = head + 2 * width
        spare = order_ref.shape[0]
        router = w_acc[:model, routed : routed + spare].astype(BF16)
        w_acc[:model, routed:] = columns + dot_nn(router, order_ref[...])
        if len(grad_refs) == 1:
            grad_refs[0][...] = w_acc[:model, :].astype(BF16)
            return
        targets = grad_refs[0].shape[0] * grad_refs[0].shape[1]
        shared_rows = model // (2 * targets)

        def pack(ref, to, fro, shared, heads):
            rows, columns = heads_chunk(model, head, ref)
            at = pack_tiles(ref, to, 0, w_acc, heads * rows, rows, fro * columns, columns)
            pack_tiles(ref, to, at, w_acc, shared * shared_rows, shared_rows, head, w_acc.shape[1] - head)

        for_targets(ids, grad_refs, pack)


def input_kernel(
    ids, x_ref, mid_ref, r_ref, own_ref, other_ref, vec_ref, out_ref, w_ref, sems
):
    first = (pl.program_id(0) == 0) & (pl.program_id(1) == 0)
    copies = half_copies(ids[0], sems, [(own_ref, other_ref, w_ref)])
    start_all(first, copies)

    wait_all(first, copies)
    subs, span, model = x_ref.shape[1:]
    normed, spread = normalize(x_ref[0].reshape(subs * span, model).astype(F32))
    low, high = halves(w_ref)
    routed = r_ref[0, 0]
    back = jnp.concatenate([dot_tn(routed, low[...]), dot_tn(routed, high[...])], 1)
    scaled = back * vec_ref[0:1, :]
    total = mid_ref[0].reshape(subs * span, model) + spread * (
        scaled
        - jnp.mean(scaled, -1, keepdims=True)
        - normed * jnp.mean(scaled * normed, -1, keepdims=True)
    )
    out_ref[0] = total.reshape(subs, span, model)


def finish_kernel(experts, deep, *refs):
    parts, (heads_ref, kv_ref, router_ref, up_shift_ref, *vector_refs) = refs[:-9], refs[-9:]
    total = parts[0][...].astype(F32)
    for part in parts[1:]:
        total = total + part[...].astype(F32)
    _, own_experts, rows, width = heads_ref.shape
    per_tile = 128 // width
    for expert in range(own_experts):
        at = expert // per_tile * rows
        lane = expert % per_tile * width
        heads_ref[0, expert] = total[at : at + rows, lane : lane + width]
    at = own_experts // per_tile * rows
    chunk = kv_ref.shape[1]
    kv_ref[0] = total[at : at + chunk]
    tile = total[at + chunk : at + 2 * chunk]
    router_ref[0] = tile[:, :experts]
    turned = tile.T
    for ref, row in zip(vector_refs, range(experts, experts + 5)):
        ref[...] = turned[row : row + 1]
    up_shift_ref[...] = jnp.concatenate(
        [turned[row : row + 1] for row in range(experts + 5, experts + 5 + deep)], 1
    )


def full(shape):
    return pl.BlockSpec(shape, lambda *ids: (0,) * len(shape))


def blocked(shape):
    tail = (0,) * (len(shape) - 2)
    return pl.BlockSpec((1, 1) + tuple(shape[2:]), lambda m, i, *refs: (m, i) + tail)


def grouped(shape, group):
    tail = (0,) * (len(shape) - 2)
    return pl.BlockSpec((1, group) + tuple(shape[2:]), lambda m, i, *refs: (m, i) + tail)


def in_place():
    return pl.BlockSpec(memory_space=pl.ANY)


def reversed_blocks(shape):
    tail = (0,) * (len(shape) - 2)
    last = shape[1] - 1
    return pl.BlockSpec((1, 1) + tuple(shape[2:]), lambda m, i, *refs: (m, last - i) + tail)


def whole(shape):
    tail = (0,) * (len(shape) - 1)
    return pl.BlockSpec((1,) + tuple(shape[1:]), lambda m, i, *refs: (m,) + tail)


def struct(shape, dtype):
    return jax.ShapeDtypeStruct(shape, dtype)


def params():
    return pltpu.CompilerParams(
        dimension_semantics=("arbitrary", "arbitrary"), vmem_limit_bytes=VMEM_BYTES
    )


def cost(flops, transcendentals, moved):
    return pl.CostEstimate(flops=flops, transcendentals=transcendentals, bytes_accessed=moved)


def exchange(value, axis, distance):
    count = lax.axis_size(axis)
    return lax.ppermute(value, axis, [(at, at ^ distance) for at in range(count)])


def permute_groups(value, index):
    groups = value.shape[0]
    bit = 1
    while bit < groups:
        pairs = value.reshape((groups // (2 * bit), 2, bit) + value.shape[1:])
        value = jnp.where((index & bit) != 0, pairs[:, ::-1].reshape(value.shape), value)
        bit *= 2
    return value


def pick_at(value, index, dim):
    return lax.dynamic_index_in_dim(value, index, dim, keepdims=False)


def reduce_axis(value, axis, dim, relative=False, keep=False):
    count = lax.axis_size(axis)
    me = lax.axis_index(axis)
    base = 0 if relative else me
    total = pick_at(value, base, dim).astype(F32)
    for distance in range(1, count):
        sent = pick_at(value, distance if relative else me ^ distance, dim)
        total = total + exchange(sent, axis, distance).astype(F32)
    return total if keep else total.astype(BF16)


def core_stage(grads):
    keep, send = grads
    other = exchange(send, "fsdp", 1)
    return [(keep[at].astype(F32) + other[at].astype(F32)).astype(BF16) for at in range(keep.shape[0])]


def split_targets(value, axis):
    return [value[at] for at in range(lax.axis_size(axis))]


def send_stage(parts, axis):
    return [exchange(parts[distance], axis, distance) for distance in range(1, len(parts))]


def total_up(own, received):
    total = own.astype(F32)
    for part in received:
        total = total + part.astype(F32)
    return total


def add_up(own, received):
    return total_up(own, received).astype(BF16)


def open_tiles(value, at, rows, columns):
    count = columns // 128
    tiles = value[at : at + count * rows].reshape(count, rows, 128)
    return jnp.swapaxes(tiles, 0, 1).reshape(rows, columns), at + count * rows


def local(
    inputs,
    lengths,
    routes,
    ln1_gain,
    ln1_bias,
    kv_weight,
    router_weight,
    query_weight,
    out_weight,
    ln2_gain,
    ln2_bias,
    up_weight,
    up_bias,
    down_weight,
    down_bias,
    out_cotangent,
):
    micro_count, _, slots, model = inputs.shape
    experts = router_weight.shape[2]
    width = query_weight.shape[3]
    picks = routes.shape[4]
    hidden_units = up_weight.shape[2]
    dp_size, z_size, f_size = (lax.axis_size(axis) for axis in AXES)
    dp_at, z_at, f_at = (lax.axis_index(axis) for axis in AXES)
    ids = jnp.stack([dp_at, z_at, f_at]).astype(jnp.int32)
    seq_index = (dp_at * z_size + z_at) * f_size + f_at
    devices = dp_size * z_size * f_size
    own_experts = experts // z_size
    half = model // f_size
    span = min(BLOCK, slots)
    blocks = slots // span
    rows = picks * span
    group = 2 if blocks % 2 == 0 else 1
    head = experts * width
    spare = -(-experts // 16) * 16
    all_rows = head + 2 * width + spare
    chunk = model // devices
    aligned = chunk % 16 == 0 and (head // z_size) % 128 == 0
    lens = lax.dynamic_index_in_dim(lengths, seq_index, 1, keepdims=False)

    def both_halves(own, other, dim):
        near = jnp.concatenate([own, other], dim)
        return jnp.where(f_at == 0, near, jnp.concatenate([other, own], dim))

    def head_parts(own):
        return [own] + [exchange(own, "expert", distance) for distance in range(1, z_size)]

    def transposed(weight):
        return jnp.swapaxes(weight[0], 1, 2).reshape(own_experts * width, half)

    def start_of(routes):
        local_routes = routes[0, :, 0]
        group = (local_routes // own_experts) ^ z_at
        local_routes = group * own_experts + local_routes % own_experts
        return jnp.swapaxes(local_routes.reshape(micro_count, blocks, span, picks), 2, 3)

    query_parts = head_parts(transposed(query_weight))
    router_t = router_weight[0].T.reshape(z_size, own_experts, half)
    router_t = permute_groups(router_t, z_at).reshape(experts, half)
    router_t = jnp.pad(router_t, ((0, spare - experts), (0, 0)))
    vectors = jnp.concatenate([ln1_gain, ln1_bias, ln2_gain, ln2_bias, down_bias], 0)
    small = jnp.concatenate([vectors, up_bias.reshape(-1, half)], 0)
    small_other = exchange(small, "fsdp", 1)
    vectors = both_halves(vectors, small_other[:5], 1).astype(F32)
    up_shift = both_halves(up_bias, small_other[5:].reshape(1, -1), 1).astype(F32)

    up_other = exchange(up_weight[0], "fsdp", 1)
    down_other = exchange(down_weight[0], "fsdp", 1)
    route_t = start_of(routes)
    lens, ids, route_t, vectors, up_shift, router_t, *query_parts = lax.optimization_barrier(
        (lens, ids, route_t, vectors, up_shift, router_t, *query_parts)
    )
    proj = jnp.concatenate(query_parts + [kv_weight[0].T, router_t], 0)
    proj_other = exchange(proj, "fsdp", 1)
    own_out, proj_other = lax.optimization_barrier((transposed(out_weight), proj_other))
    out_parts = head_parts(own_out)

    states = inputs.reshape(micro_count, blocks, span, model)
    cotangent = out_cotangent.reshape(micro_count, blocks, span, model)

    grid = (micro_count, blocks)
    hid_s = struct((micro_count, blocks, span, model), BF16)
    aug_s = struct((micro_count, blocks, span, 2 * width), BF16)
    kt_s = struct((micro_count, blocks, 1, width, span), BF16)
    q_s = struct((micro_count, blocks, width, rows), BF16)
    row_s = struct((micro_count, blocks, 1, rows), F32)
    gate_s = struct((micro_count, blocks, experts, span), F32)
    slot_s = struct((micro_count, blocks, experts, span), jnp.int32)
    tokens = micro_count * slots
    pair_flops = tokens * picks * slots * width
    hid, kaug, vaug, kt, q, ctx, lse, gates, slot = pl.pallas_call(
        forward_kernel,
        name="forward",
        grid_spec=pltpu.PrefetchScalarGridSpec(
            num_scalar_prefetch=2,
            grid=grid,
            in_specs=[
                blocked(states.shape),
                blocked(route_t.shape),
                full(vectors.shape),
                in_place(),
                in_place(),
            ],
            out_specs=[
                blocked(hid_s.shape),
                whole(aug_s.shape),
                whole(aug_s.shape),
                blocked(kt_s.shape),
                blocked(q_s.shape),
                blocked(q_s.shape),
                blocked(row_s.shape),
                blocked(gate_s.shape),
                blocked(slot_s.shape),
            ],
            scratch_shapes=[
                pltpu.VMEM((head, span), BF16),
                pltpu.VMEM((2 * width, rows), BF16),
                pltpu.VMEM((blocks, span, rows), F32),
                pltpu.VMEM((blocks, width, span), BF16),
                pltpu.VMEM((width, rows), F32),
                pltpu.VMEM((2 * all_rows, half), BF16),
                pltpu.SemaphoreType.DMA((2,)),
            ],
        ),
        out_shape=[hid_s, aug_s, aug_s, kt_s, q_s, q_s, row_s, gate_s, slot_s],
        compiler_params=params(),
        cost_estimate=cost(2 * tokens * model * all_rows + 16 * pair_flops, 0, 64 << 20),
    )(lens, ids, states, route_t, vectors, proj, proj_other)

    ctx, *out_parts = lax.optimization_barrier((ctx, *out_parts))
    out_proj = jnp.concatenate(out_parts, 0)
    out_other = exchange(out_proj, "fsdp", 1)
    state_s = struct((micro_count, blocks, span, model), F32)
    mid_rows = chunk * hidden_units * 2 // 128 + head // z_size * (chunk * z_size) // 128
    late_rows = head // z_size * (chunk * z_size) // 128 + 2 * chunk
    if aligned:
        mid_grads = [struct((dp_size, z_size, mid_rows, 128), BF16)] * 2
        late_grads = [struct((dp_size, z_size, late_rows, 128), BF16)] * 2
    else:
        mid_grads = [
            struct((hidden_units, model), BF16),
            struct((model, hidden_units), BF16),
            struct((model, head), BF16),
        ]
        late_grads = [struct((model, head + 2 * width + 128), BF16)]
    outputs, mid, grad_ctx, delta, grad_logits, small2, up_small, *mid_grads = pl.pallas_call(
        middle_kernel,
        name="middle",
        grid_spec=pltpu.PrefetchScalarGridSpec(
            num_scalar_prefetch=2,
            grid=(micro_count, blocks // group),
            in_specs=[
                grouped(states.shape, group),
                grouped(q_s.shape, group),
                grouped(gate_s.shape, group),
                grouped(slot_s.shape, group),
                grouped(cotangent.shape, group),
                in_place(),
                in_place(),
                full(vectors.shape),
                in_place(),
                in_place(),
                full(up_shift.shape),
                in_place(),
                in_place(),
            ],
            out_specs=[
                grouped(state_s.shape, group),
                grouped(state_s.shape, group),
                grouped(q_s.shape, group),
                grouped(row_s.shape, group),
                grouped(gate_s.shape, group),
                full((3, 8, model)),
                full((8, hidden_units)),
            ]
            + [full(leaf.shape) for leaf in mid_grads],
            scratch_shapes=[
                pltpu.VMEM((group, width, rows), BF16),
                pltpu.VMEM((head, group * span), BF16),
                pltpu.VMEM((head, group * span), BF16),
                pltpu.VMEM((hidden_units, model), F32),
                pltpu.VMEM((model, hidden_units), F32),
                pltpu.VMEM((model, head), F32),
                pltpu.VMEM((2 * head, half), BF16),
                pltpu.VMEM((model, hidden_units), BF16),
                pltpu.VMEM((hidden_units, model), BF16),
                pltpu.SemaphoreType.DMA((6,)),
            ],
        ),
        out_shape=[
            state_s,
            state_s,
            q_s,
            row_s,
            gate_s,
            struct((3, 8, model), F32),
            struct((8, hidden_units), F32),
        ]
        + mid_grads,
        compiler_params=params(),
        cost_estimate=cost(2 * tokens * model * (6 * hidden_units + 3 * head), 0, 200 << 20),
    )(
        lens,
        ids,
        states,
        ctx,
        gates,
        slot,
        cotangent,
        out_proj,
        out_other,
        vectors,
        up_weight[0],
        up_other,
        up_shift,
        down_weight[0],
        down_other,
    )

    if aligned:
        mid_sums = core_stage(mid_grads)
        grad_ctx, *mid_sums = lax.optimization_barrier((grad_ctx, *mid_sums))
        mid_received = send_stage(mid_sums, "dp")

    expert_id = jnp.arange(experts)
    moved = ((expert_id // own_experts) ^ z_at) * own_experts + expert_id % own_experts
    order = jnp.pad(
        (jnp.arange(spare)[:, None] == moved[None, :]).astype(BF16), ((0, 0), (0, 128 - experts))
    )
    deep = hidden_units // model
    columns = jnp.concatenate(
        [
            vectors[:2].T,
            jnp.sum(small2, 1).T,
            jnp.swapaxes(jnp.sum(up_small, 0).reshape(devices, deep, chunk), 1, 2).reshape(model, deep),
        ],
        1,
    )
    columns = jnp.pad(columns, ((0, 0), (experts, 128 - experts - 5 - deep)))
    r_s = struct((micro_count, blocks // group, all_rows, group * span), BF16)

    def routed_block(m, i, *refs):
        block = blocks - 1 - i
        return m, block // group, 0, block % group

    routed, *late_grads = pl.pallas_call(
        backward_kernel,
        name="backward",
        grid_spec=pltpu.PrefetchScalarGridSpec(
            num_scalar_prefetch=2,
            grid=grid,
            in_specs=[
                reversed_blocks(hid_s.shape),
                whole(aug_s.shape),
                whole(aug_s.shape),
                whole((micro_count, blocks, width, span)),
                reversed_blocks(q_s.shape),
                reversed_blocks(row_s.shape),
                reversed_blocks(q_s.shape),
                reversed_blocks(row_s.shape),
                reversed_blocks(slot_s.shape),
                reversed_blocks(gate_s.shape),
                full(order.shape),
                full(columns.shape),
                in_place(),
                in_place(),
            ],
            out_specs=[pl.BlockSpec((1, 1, all_rows, span), routed_block)]
            + [full(leaf.shape) for leaf in late_grads],
            scratch_shapes=[
                pltpu.VMEM((2 * width, rows), BF16),
                pltpu.VMEM((2 * width, rows), BF16),
                pltpu.VMEM((width, rows), F32),
                pltpu.VMEM((blocks, width, span), F32),
                pltpu.VMEM((blocks, width, span), F32),
                pltpu.VMEM((model + 16, head + 2 * width + 128), F32),
                pltpu.VMEM((2 * all_rows, half), BF16),
                pltpu.SemaphoreType.DMA((2,)),
            ],
        ),
        out_shape=[r_s] + late_grads,
        compiler_params=params(),
        cost_estimate=cost(2 * tokens * model * all_rows + 40 * pair_flops, 0, 100 << 20),
    )(
        lens,
        ids,
        hid,
        kaug,
        vaug,
        kt.reshape(micro_count, blocks, width, span),
        q,
        lse,
        grad_ctx,
        delta,
        slot,
        grad_logits,
        order,
        columns,
        proj,
        proj_other,
    )

    if aligned:
        *mid_received, late_grads[0], late_grads[1] = lax.optimization_barrier(
            (*mid_received, *late_grads)
        )
        *mid_received, late_grads[0], late_grads[1] = lax.optimization_barrier(
            (*mid_received, *late_grads)
        )
        late_sums = core_stage(late_grads)
        *mid_received, late_sums[0] = lax.optimization_barrier((*mid_received, late_sums[0]))
        mid_sums = split_targets(add_up(mid_sums[0], mid_received), "expert")
        routed, *sums = lax.optimization_barrier((routed, *mid_sums, *late_sums))
        mid_sums, late_sums = sums[:z_size], sums[z_size:]
        mid_received = send_stage(mid_sums, "expert")
        late_received = send_stage(late_sums, "dp")

    input_grad = pl.pallas_call(
        input_kernel,
        name="input_back",
        grid_spec=pltpu.PrefetchScalarGridSpec(
            num_scalar_prefetch=1,
            grid=(micro_count, blocks // group),
            in_specs=[
                grouped(states.shape, group),
                grouped(state_s.shape, group),
                blocked(r_s.shape),
                in_place(),
                in_place(),
                full(vectors.shape),
            ],
            out_specs=grouped(state_s.shape, group),
            scratch_shapes=[
                pltpu.VMEM((2 * all_rows, half), BF16),
                pltpu.SemaphoreType.DMA((2,)),
            ],
        ),
        out_shape=state_s,
        compiler_params=params(),
        cost_estimate=cost(2 * tokens * model * all_rows, 0, 40 << 20),
    )(ids[2:], states, mid, routed, proj, proj_other, vectors)

    def open_heads(value):
        return jnp.swapaxes(value.reshape(-1, own_experts, width), 0, 1)[None]

    if aligned:
        input_grad, *received = lax.optimization_barrier(
            (input_grad, *late_received, *mid_received)
        )
        late_received = received[: dp_size - 1]
        mid_received = received[dp_size - 1 :]
        late_sums = split_targets(add_up(late_sums[0], late_received), "expert")
        late_received = send_stage(late_sums, "expert")
        mid_total = total_up(mid_sums[0], mid_received)
        up_weight_grad, at = open_tiles(mid_total, 0, chunk, hidden_units)
        down_weight_grad, at = open_tiles(mid_total, at, hidden_units // devices, model)
        out_weight_grad, at = open_tiles(mid_total, at, chunk * z_size, head // z_size)
        out_weight_grad = open_heads(out_weight_grad)
        query_weight_grad, kv_grad, router_grad, up_bias_grad, *small = pl.pallas_call(
            functools.partial(finish_kernel, experts, deep),
            name="finish",
            out_shape=[
                struct((1, own_experts, chunk * z_size, width), F32),
                struct((1, chunk, 2 * width), F32),
                struct((1, chunk, experts), F32),
                struct((1, deep * chunk), F32),
            ]
            + [struct((1, chunk), F32)] * 5,
        )(late_sums[0], *late_received)
    else:
        down_grad, up_grad, wo_grad = mid_grads
        w_grad = late_grads[0]

        def reduce_shared(value, part):
            value = value.reshape(dp_size, z_size, f_size, part, value.shape[1])
            value = reduce_axis(value, "fsdp", 2)
            value = reduce_axis(value, "dp", 0)
            return reduce_axis(value, "expert", 0, keep=True)

        def reduce_heads(value):
            value = value.reshape(dp_size, f_size, chunk * z_size, z_size, own_experts * width)
            value = reduce_axis(value, "fsdp", 1)
            value = reduce_axis(value, "dp", 0)
            return open_heads(reduce_axis(value, "expert", 1, relative=True, keep=True))

        up_weight_grad = reduce_shared(up_grad, chunk)
        down_weight_grad = reduce_shared(down_grad, hidden_units // devices)
        out_weight_grad = reduce_heads(wo_grad)
        query_weight_grad = reduce_heads(w_grad[:, :head])
        narrow = reduce_shared(w_grad[:, head:], chunk)
        kv_grad, router_grad = narrow[None, :, : 2 * width], narrow[None, :, 2 * width :]
        small = [router_grad[:, :, experts + at] for at in range(5)]
        up_bias_grad = router_grad[0, :, experts + 5 : experts + 5 + deep].T.reshape(1, -1)
        router_grad = router_grad[:, :, :experts]
    shape = (micro_count, 1, slots, model)
    return (
        outputs.reshape(shape),
        input_grad.reshape(shape),
        small[0],
        small[1],
        kv_grad,
        router_grad,
        query_weight_grad,
        out_weight_grad,
        small[2],
        small[3],
        up_weight_grad[None],
        up_bias_grad,
        down_weight_grad[None],
        small[4],
    )


def solution(mesh):
    shards = P(None, AXES, None, None)
    return jax.shard_map(
        local,
        mesh=mesh,
        in_specs=(
            shards,
            P(),
            P(None, None, AXES, None, None),
            P(None, "fsdp"),
            P(None, "fsdp"),
            P(None, "fsdp", None),
            P(None, "fsdp", None),
            P(None, "expert", "fsdp", None),
            P(None, "expert", "fsdp", None),
            P(None, "fsdp"),
            P(None, "fsdp"),
            P(None, "fsdp", None),
            P(None, "fsdp"),
            P(None, "fsdp", None),
            P(None, "fsdp"),
            shards,
        ),
        out_specs=(
            shards,
            shards,
            P(None, AXES),
            P(None, AXES),
            P(None, AXES, None),
            P(None, AXES, None),
            P(None, "expert", ("dp", "fsdp"), None),
            P(None, "expert", ("dp", "fsdp"), None),
            P(None, AXES),
            P(None, AXES),
            P(None, AXES, None),
            P(None, AXES),
            P(None, AXES, None),
            P(None, AXES),
        ),
        check_vma=False,
    )
```

```python
import functools

import jax
import jax.numpy as jnp
from jax import lax
from jax.experimental import pallas as pl
from jax.experimental.pallas import tpu as pltpu
from jax.sharding import PartitionSpec as P

EPSILON = 1e-05
NEGATIVE = -1e30
GELU_SCALE = 0.7978845608028654
GELU_CUBIC = 0.044715
BLOCK = 256
AXES = ("dp", "expert", "fsdp")
F32 = jnp.float32
BF16 = jnp.bfloat16
VMEM_BYTES = 60 << 20


def dot_nn(left, right):
    return lax.dot_general(left, right, (((1,), (0,)), ((), ())), preferred_element_type=F32)


def dot_nt(left, right):
    return lax.dot_general(left, right, (((1,), (1,)), ((), ())), preferred_element_type=F32)


def dot_tn(left, right):
    return lax.dot_general(left, right, (((0,), (0,)), ((), ())), preferred_element_type=F32)


def normalize(values):
    center = values - jnp.mean(values, -1, keepdims=True)
    spread = lax.rsqrt(jnp.mean(center * center, -1, keepdims=True) + EPSILON)
    return center * spread, spread


def halves(ref):
    rows = ref.shape[0] // 2
    return ref.at[pl.ds(0, rows)], ref.at[pl.ds(rows, rows)]


def fold_rows(values, combine):
    rows, columns = values.shape
    return combine(values.reshape(rows // 8, 8, columns), 0)


def pick_slots(table_ref, slot, picks, width, start=0):
    experts, span = slot.shape
    lanes = slice(start, start + span)
    slot = slot.astype(table_ref.dtype)
    picked = []
    for pick in range(picks):
        value = table_ref[pick * width : (pick + 1) * width, lanes]
        for expert in range(pick + 1, experts - picks + pick + 1):
            hit = jnp.broadcast_to(slot[expert : expert + 1, :], (width, span)) == pick
            value = jnp.where(hit, table_ref[expert * width : (expert + 1) * width, lanes], value)
        picked.append(value)
    return picked


def spread_slots(read, slot, expert, picks, width, span):
    experts = slot.shape[0]
    row = jnp.broadcast_to(slot[expert : expert + 1, :], (width, span))
    value = jnp.zeros((width, span), slot.dtype)
    for pick in range(max(0, expert - experts + picks), min(expert, picks - 1) + 1):
        value = jnp.where(row == pick, read(pick), value)
    return value


def forward_kernel(
    lens,
    ids,
    x_ref,
    route_ref,
    vec_ref,
    own_ref,
    other_ref,
    hid_ref,
    kaug_ref,
    vaug_ref,
    kt_ref,
    q_ref,
    ctx_ref,
    lse_ref,
    gate_ref,
    slot_ref,
    table,
    qaug,
    scores,
    vt,
    acc,
    w_ref,
    sems,
):
    block = pl.program_id(1)
    length = lens[pl.program_id(0)]
    first = (pl.program_id(0) == 0) & (block == 0)
    copies = half_copies(ids[2], sems, [(own_ref, other_ref, w_ref)])
    start_all(first, copies)
    wait_all(first, copies)
    span = x_ref.shape[2]
    experts = slot_ref.shape[2]
    picks = route_ref.shape[2]
    width = kt_ref.shape[3]
    half = w_ref.shape[1]
    low, high = halves(w_ref)
    rows = picks * span

    normed, _ = normalize(x_ref[0, 0].astype(F32))
    hid = (normed * vec_ref[0:1, :] + vec_ref[1:2, :]).astype(BF16)
    hid_ref[0, 0] = hid
    head = experts * width
    products = dot_nt(low[...], hid[:, :half]) + dot_nt(high[...], hid[:, half:])
    table[...] = products[:head].astype(BF16)
    kt_ref[0, 0, 0] = products[head : head + width, :].astype(BF16)
    vt[block] = products[head + width : head + 2 * width, :].astype(BF16)

    lane = lax.broadcasted_iota(jnp.int32, (span, 2 * width), 1)
    place = block * span + lax.broadcasted_iota(jnp.int32, (span, 2 * width), 0)
    ones = jnp.where(lane < width + 4, 1.0, 0.0)
    cut = jnp.where(place < length, 0.0, NEGATIVE)
    both = dot_nt(hid[:, :half], low[head : head + 2 * width, :])
    both = both + dot_nt(hid[:, half:], high[head : head + 2 * width, :])
    keys = jnp.where(lane < width, both, jnp.where(lane == width, cut, ones))
    kaug_ref[0, block] = keys.astype(BF16)
    vals = jnp.where(lane < width, pltpu.roll(both, width, 1), ones)
    vaug_ref[0, block] = vals.astype(BF16)

    logits = products[head + 2 * width : head + 2 * width + experts, :]
    expert_id = lax.broadcasted_iota(jnp.int32, (experts, span), 0)
    chosen = jnp.zeros((experts, span), F32)
    for pick in range(picks):
        chosen = jnp.where(expert_id == route_ref[0, 0, pick : pick + 1, :], 1.0, chosen)
    lower = jnp.where(
        lax.broadcasted_iota(jnp.int32, (experts, experts), 1)
        < lax.broadcasted_iota(jnp.int32, (experts, experts), 0),
        1.0,
        0.0,
    )
    slot = jnp.where(chosen > 0.0, dot_nn(lower, chosen), -1.0).astype(jnp.int32)
    slot_ref[0, 0] = slot
    masked = jnp.where(chosen > 0.0, logits, NEGATIVE)
    raised = jnp.where(chosen > 0.0, jnp.exp(masked - jnp.max(masked, 0, keepdims=True)), 0.0)
    gate_ref[0, 0] = raised / jnp.sum(raised, 0, keepdims=True)

    picked = pick_slots(table, slot, picks, width)
    for pick in range(picks):
        qaug[0:width, pick * span : (pick + 1) * span] = (
            picked[pick] * (width**-0.5)
        ).astype(BF16)
    q_ref[0, 0] = qaug[0:width, :]
    side = lax.broadcasted_iota(jnp.int32, (width, rows), 0)
    qaug[width : 2 * width, :] = jnp.where(side == 0, 1.0, 0.0).astype(BF16)

    def score_step(at, top):
        part = dot_nn(kaug_ref[0, at], qaug[...])
        scores[at] = part
        return jnp.maximum(top, fold_rows(part, jnp.max))

    used = jnp.minimum(block, (length + span - 1) // span)
    top = lax.fori_loop(0, used, score_step, jnp.full((8, rows), NEGATIVE, F32))
    causal = lax.broadcasted_iota(jnp.int32, (span, rows), 0) <= (
        lax.broadcasted_iota(jnp.int32, (span, rows), 1) & (span - 1)
    )
    part = jnp.where(causal, dot_nn(kaug_ref[0, block], qaug[...]), NEGATIVE)
    top = jnp.maximum(top, fold_rows(part, jnp.max))
    top = jnp.max(top, 0, keepdims=True)
    raised = jnp.exp(part - top)
    acc[...] = dot_nn(vt[block], raised.astype(BF16))
    total = fold_rows(raised, jnp.sum)

    def value_step(at, total):
        raised = jnp.exp(scores[at] - top)
        acc[...] += dot_nn(vt[at], raised.astype(BF16))
        return total + fold_rows(raised, jnp.sum)

    total = lax.fori_loop(0, used, value_step, total)
    total = jnp.sum(total, 0, keepdims=True)
    ctx_ref[0, 0] = (acc[...] * (1.0 / total)).astype(BF16)
    lse_ref[0, 0] = top + jnp.log(total)


def middle_kernel(
    lens,
    ids,
    x_ref,
    ctx_ref,
    gate_ref,
    slot_ref,
    cot_ref,
    own_ref,
    other_ref,
    vec_ref,
    own_up_ref,
    other_up_ref,
    up_shift_ref,
    own_down_ref,
    other_down_ref,
    out_ref,
    mid_ref,
    do_ref,
    delta_ref,
    gl_ref,
    small_ref,
    up_shift_grad_ref,
    *rest,
):
    *grad_refs, gated, cexp, table, down_acc, up_acc, wo_acc, w_ref, up_ref, down_ref, sems = rest
    micro = pl.program_id(0)
    block = pl.program_id(1)
    length = lens[micro]
    subs, span, model = x_ref.shape[1:]
    tokens = subs * span
    experts = slot_ref.shape[2]
    width = ctx_ref.shape[2]
    picks = ctx_ref.shape[3] // span
    head = experts * width
    half = w_ref.shape[1]
    low, high = halves(w_ref)
    first = (micro == 0) & (block == 0)
    last = (micro == pl.num_programs(0) - 1) & (block == pl.num_programs(1) - 1)

    def clear():
        down_acc[...] = jnp.zeros_like(down_acc)
        up_acc[...] = jnp.zeros_like(up_acc)
        wo_acc[...] = jnp.zeros_like(wo_acc)
        small_ref[...] = jnp.zeros_like(small_ref)
        up_shift_grad_ref[...] = jnp.zeros_like(up_shift_grad_ref)

    copies = half_copies(
        ids[2],
        sems,
        [
            (own_ref, other_ref, w_ref),
            (own_up_ref, other_up_ref, up_ref),
            (own_down_ref, other_down_ref, down_ref),
        ],
    )
    start_all(first, copies, clear)
    wait_all(first, copies)
    slots = [slot_ref[0, sub] for sub in range(subs)]
    gate = []
    for sub in range(subs):
        gates = gate_ref[0, sub]
        gate.append(
            [
                jnp.sum(jnp.where(slots[sub] == pick, gates, 0.0), 0, keepdims=True)
                for pick in range(picks)
            ]
        )
        for pick in range(picks):
            at = slice(pick * span, (pick + 1) * span)
            gated[sub, :, at] = (ctx_ref[0, sub, :, at].astype(F32) * gate[sub][pick]).astype(BF16)
        for expert in range(experts):
            cexp[expert * width : (expert + 1) * width, sub * span : (sub + 1) * span] = spread_slots(
                lambda pick: gated[sub, :, pick * span : (pick + 1) * span],
                slots[sub].astype(BF16),
                expert,
                picks,
                width,
                span,
            )
    mixed = x_ref[0].reshape(tokens, model).astype(F32) + jnp.concatenate(
        [dot_tn(cexp[...], low[...]), dot_tn(cexp[...], high[...])], 1
    )
    normed, spread = normalize(mixed)
    hid = (normed * vec_ref[2:3, :] + vec_ref[3:4, :]).astype(BF16)
    place = block * tokens + lax.broadcasted_iota(jnp.int32, (tokens, 1), 0)
    grad = jnp.where(place < length, cot_ref[0].reshape(tokens, model), 0.0)
    grad_b = grad.astype(BF16)
    hid_t = hid.T
    out = mixed + vec_ref[4:5, :]
    back = jnp.zeros_like(mixed)
    hidden_units = up_ref.shape[1]
    step = min(hidden_units, 256)
    cuts = [slice(at, at + step) for at in range(0, hidden_units, step)]

    def ahead(cut):
        return dot_nn(hid, up_ref[:, cut]), dot_nt(grad_b, down_ref[cut, :])

    held = ahead(cuts[0])
    ready = None
    for n in range(len(cuts) + 1):
        pre, grad_act = held if held is not None else (None, None)
        held = ahead(cuts[n + 1]) if n + 1 < len(cuts) else None
        fresh = None
        if n < len(cuts):
            cut = cuts[n]
            pre = pre + up_shift_ref[:, cut]
            square = pre * pre
            bent = jnp.tanh(pre * (GELU_SCALE + (GELU_SCALE * GELU_CUBIC) * square))
            rise = 0.5 + 0.5 * bent
            slope = rise + (0.5 * pre) * (1.0 - bent * bent) * (
                GELU_SCALE + (3.0 * GELU_SCALE * GELU_CUBIC) * square
            )
            grad_pre = grad_act * slope
            up_shift_grad_ref[:, cut] += fold_rows(grad_pre, jnp.sum)
            fresh = (cut, (pre * rise).astype(BF16), grad_pre.astype(BF16))
        if ready is not None:
            cut, active, grad_pre_b = ready
            out = out + dot_nn(active, down_ref[cut, :])
            back = back + dot_nt(grad_pre_b, up_ref[:, cut])
            down_acc[cut, :] += dot_nn(active.T, grad_b)
            up_acc[:, cut] += dot_nn(hid_t, grad_pre_b)
        ready = fresh
    out_ref[0] = out.reshape(subs, span, model)
    scaled = back * vec_ref[2:3, :]
    mid = grad + spread * (
        scaled
        - jnp.mean(scaled, -1, keepdims=True)
        - normed * jnp.mean(scaled * normed, -1, keepdims=True)
    )
    small_ref[0] += fold_rows(back * normed, jnp.sum)
    small_ref[1] += fold_rows(back, jnp.sum)
    small_ref[2] += fold_rows(grad_b.astype(F32), jnp.sum)

    mid_b = mid.astype(BF16)
    mid_ref[0] = mid_b.reshape(subs, span, model)
    wo_acc[...] += dot_nt(mid_b.T, cexp[...])
    products = dot_nt(low[...], mid_b[:, :half]) + dot_nt(high[...], mid_b[:, half:])
    table[...] = products.astype(BF16)
    for sub in range(subs):
        slot = slots[sub]
        picked = pick_slots(table, slot, picks, width, sub * span)
        grad_gate = []
        for pick in range(picks):
            at = slice(pick * span, (pick + 1) * span)
            ctx = ctx_ref[0, sub, :, at].astype(F32)
            found = picked[pick].astype(F32)
            grad_gate.append(jnp.sum(found * ctx, 0, keepdims=True))
            grad_ctx = (found * gate[sub][pick]).astype(BF16)
            do_ref[0, sub, :, at] = grad_ctx
            delta_ref[0, sub, :, at] = jnp.sum(grad_ctx.astype(F32) * ctx, 0, keepdims=True)
        average = gate[sub][0] * grad_gate[0]
        for pick in range(1, picks):
            average = average + gate[sub][pick] * grad_gate[pick]
        grad_logits = jnp.zeros((experts, span), F32)
        for pick in range(picks):
            grad_logits = jnp.where(
                slot == pick, gate[sub][pick] * (grad_gate[pick] - average), grad_logits
            )
        gl_ref[0, sub] = grad_logits

    @pl.when(last)
    def _():
        if len(grad_refs) == 3:
            for ref, total in zip(grad_refs, (down_acc, up_acc, wo_acc)):
                ref[...] = total[...].astype(BF16)
            return
        targets = grad_refs[0].shape[0] * grad_refs[0].shape[1]
        up_rows = up_acc.shape[0] // (2 * targets)
        down_rows = down_acc.shape[0] // (2 * targets)

        def pack(ref, to, fro, shared, heads):
            at = pack_tiles(ref, to, 0, up_acc, shared * up_rows, up_rows, 0, up_acc.shape[1])
            at = pack_tiles(ref, to, at, down_acc, shared * down_rows, down_rows, 0, down_acc.shape[1])
            rows, columns = heads_chunk(wo_acc.shape[0], head, ref)
            pack_tiles(ref, to, at, wo_acc, heads * rows, rows, fro * columns, columns)

        for_targets(ids, grad_refs, pack)


def half_copies(core, sems, moves):
    copies = []
    for own, other, target in moves:
        half = target.shape[0] // 2
        for source, at in ((own, core), (other, 1 - core)):
            place = target.at[pl.ds(pl.multiple_of(at * half, half), half)]
            copies.append(pltpu.make_async_copy(source, place, sems.at[len(copies)]))
    return copies


def start_all(first, copies, meanwhile=lambda: None):
    @pl.when(first)
    def _():
        for copy in copies:
            copy.start()
        meanwhile()


def wait_all(first, copies):
    @pl.when(first)
    def _():
        for copy in copies:
            copy.wait()


def pack_tiles(ref, to, at, total, row, rows, column, columns):
    row = pl.multiple_of(row, rows)
    for lane in range(0, columns, 128):
        start = column + lane
        if not isinstance(start, int):
            start = pl.multiple_of(start, 128)
        tile = total[pl.ds(row, rows), pl.ds(start, 128)]
        ref[to[0], to[1], at : at + rows, :] = tile.astype(BF16)
        at += rows
    return at


def heads_chunk(model, head, ref):
    return model // (2 * ref.shape[0]), head // ref.shape[1]


def for_targets(ids, refs, pack):
    def body(dp_far, carry):
        dp = dp_far ^ ids[0]
        for z_far in range(refs[0].shape[1]):
            for f_far in range(2):
                f = ids[2] ^ f_far
                shared = (dp * refs[0].shape[1] + (z_far ^ ids[1])) * 2 + f
                pack(refs[f_far], (dp_far, z_far), z_far, shared, dp * 2 + f)
        return carry

    lax.fori_loop(0, refs[0].shape[0], body, 0)


def split_three(values):
    high = values.astype(BF16).astype(F32)
    rest = values - high
    middle = rest.astype(BF16).astype(F32)
    return high, middle, rest - middle


def backward_kernel(
    lens,
    ids,
    hid_ref,
    kaug_ref,
    vaug_ref,
    kt_ref,
    q_ref,
    lse_ref,
    do_ref,
    delta_ref,
    slot_ref,
    gl_ref,
    order_ref,
    columns_ref,
    own_ref,
    other_ref,
    r_ref,
    *rest,
):
    *grad_refs, qaug, daug, dq, dkt, dvt, w_acc, w_ref, sems = rest
    micro = pl.program_id(0)
    step = pl.program_id(1)
    blocks = pl.num_programs(1)
    block = blocks - 1 - step
    length = lens[micro]
    span = hid_ref.shape[2]
    experts = slot_ref.shape[2]
    width = q_ref.shape[2]
    rows = q_ref.shape[3]
    picks = rows // span
    head = experts * width

    def clear():
        w_acc[...] = jnp.zeros_like(w_acc)

    copies = half_copies(ids[2], sems, [(own_ref, other_ref, w_ref)])
    start_all((micro == 0) & (step == 0), copies, clear)

    @pl.when(step == 0)
    def _():
        dkt[...] = jnp.zeros_like(dkt)
        dvt[...] = jnp.zeros_like(dvt)

    @pl.when(block * span >= length)
    def _():
        r_ref[...] = jnp.zeros_like(r_ref)

    @pl.when(block * span < length)
    def _():
        side = lax.broadcasted_iota(jnp.int32, (width, rows), 0)
        qaug[0:width, :] = q_ref[0, 0]
        high, middle, low = split_three(-lse_ref[0, 0])
        qaug[width : 2 * width, :] = jnp.where(
            side == 0,
            1.0,
            jnp.where(side == 1, high, jnp.where(side == 2, middle, jnp.where(side == 3, low, 0.0))),
        ).astype(BF16)
        daug[0:width, :] = do_ref[0, 0]
        high, middle, low = split_three(-delta_ref[0, 0])
        daug[width : 2 * width, :] = jnp.where(
            side == 0, high, jnp.where(side == 1, middle, jnp.where(side == 2, low, 0.0))
        ).astype(BF16)

        lanes = 256
        causal = lax.broadcasted_iota(jnp.int32, (span, lanes), 0) <= (
            lax.broadcasted_iota(jnp.int32, (span, lanes), 1) & (span - 1)
        )

        def key_step(at, diagonal):
            dv = dvt[at]
            dk = dkt[at]
            cuts = [slice(start, start + lanes) for start in range(0, rows, lanes)]

            def ahead(cut):
                return dot_nn(kaug_ref[0, at], qaug[:, cut]), dot_nn(vaug_ref[0, at], daug[:, cut])

            held = ahead(cuts[0])
            back = None
            for n in range(len(cuts) + 1):
                scores, dprobs = held if held is not None else (None, None)
                held = ahead(cuts[n + 1]) if n + 1 < len(cuts) else None
                fresh = None
                if n < len(cuts):
                    probs = jnp.exp(scores)
                    if diagonal:
                        probs = jnp.where(causal, probs, 0.0)
                    slopes = (probs * dprobs).astype(BF16)
                    fresh = (cuts[n], probs.astype(BF16), slopes)
                if back is not None:
                    cut, probs_b, slopes = back
                    dv = dv + dot_nt(daug[0:width, cut], probs_b)
                    dk = dk + dot_nt(qaug[0:width, cut], slopes)
                    part = dot_nn(kt_ref[0, at], slopes)
                    dq[:, cut] = part if diagonal else dq[:, cut] + part
                back = fresh
            dvt[at] = dv
            dkt[at] = dk

        key_step(block, True)

        def body(at, carry):
            key_step(at, False)
            return carry

        lax.fori_loop(0, block, body, 0)
        scaled = (dq[...] * (width**-0.5)).astype(BF16)
        slot = slot_ref[0, 0].astype(BF16)
        for expert in range(experts):
            r_ref[0, 0, expert * width : (expert + 1) * width, :] = spread_slots(
                lambda pick: scaled[:, pick * span : (pick + 1) * span],
                slot,
                expert,
                picks,
                width,
                span,
            )
        r_ref[0, 0, head : head + width, :] = dkt[block].astype(BF16)
        r_ref[0, 0, head + width : head + 2 * width, :] = dvt[block].astype(BF16)
        tail = r_ref.shape[2] - head - 2 * width
        r_ref[0, 0, head + 2 * width :, :] = jnp.concatenate(
            [gl_ref[0, 0], jnp.zeros((tail - experts, span), F32)], 0
        ).astype(BF16)
        summing = jnp.concatenate([hid_ref[0, 0].T, jnp.ones((16, span), BF16)], 0)
        w_acc[:, : r_ref.shape[2]] += dot_nt(summing, r_ref[0, 0])

    @pl.when((micro == pl.num_programs(0) - 1) & (step == blocks - 1))
    def _():
        for copy in copies:
            copy.wait()
        model = hid_ref.shape[3]
        used = r_ref.shape[2]
        low, high = halves(w_ref)
        token_sum = w_acc[model : model + 1, :used]
        gain_sum, shift_sum = [], []
        for at, part in ((0, low), (model // 2, high)):
            weight = part[...].T.astype(F32)
            total = w_acc[at : at + model // 2, :used]
            gain_sum.append(jnp.sum(weight * total, 1, keepdims=True))
            shift_sum.append(jnp.sum(weight * token_sum, 1, keepdims=True))
        gain_sum, shift_sum = jnp.concatenate(gain_sum, 0), jnp.concatenate(shift_sum, 0)
        columns = columns_ref[...]
        gain, shift = columns[:, experts : experts + 1], columns[:, experts + 1 : experts + 2]
        gain_sum = (gain_sum - shift * shift_sum) / gain
        lane = lax.broadcasted_iota(jnp.int32, columns.shape, 1)
        columns = jnp.where(
            lane == experts, gain_sum, jnp.where(lane == experts + 1, shift_sum, columns)
        )
        routed = head + 2 * width
        spare = order_ref.shape[0]
        router = w_acc[:model, routed : routed + spare].astype(BF16)
        w_acc[:model, routed:] = columns + dot_nn(router, order_ref[...])
        if len(grad_refs) == 1:
            grad_refs[0][...] = w_acc[:model, :].astype(BF16)
            return
        targets = grad_refs[0].shape[0] * grad_refs[0].shape[1]
        shared_rows = model // (2 * targets)

        def pack(ref, to, fro, shared, heads):
            rows, columns = heads_chunk(model, head, ref)
            at = pack_tiles(ref, to, 0, w_acc, heads * rows, rows, fro * columns, columns)
            pack_tiles(ref, to, at, w_acc, shared * shared_rows, shared_rows, head, w_acc.shape[1] - head)

        for_targets(ids, grad_refs, pack)


def input_kernel(
    ids, x_ref, mid_ref, r_ref, own_ref, other_ref, vec_ref, out_ref, w_ref, sems
):
    first = (pl.program_id(0) == 0) & (pl.program_id(1) == 0)
    copies = half_copies(ids[0], sems, [(own_ref, other_ref, w_ref)])
    start_all(first, copies)

    wait_all(first, copies)
    subs, span, model = x_ref.shape[1:]
    normed, spread = normalize(x_ref[0].reshape(subs * span, model).astype(F32))
    low, high = halves(w_ref)
    routed = r_ref[0, 0]
    back = jnp.concatenate([dot_tn(routed, low[...]), dot_tn(routed, high[...])], 1)
    scaled = back * vec_ref[0:1, :]
    total = mid_ref[0].reshape(subs * span, model).astype(F32) + spread * (
        scaled
        - jnp.mean(scaled, -1, keepdims=True)
        - normed * jnp.mean(scaled * normed, -1, keepdims=True)
    )
    out_ref[0] = total.reshape(subs, span, model)


def finish_kernel(experts, deep, *refs):
    parts, (heads_ref, kv_ref, router_ref, up_shift_ref, *vector_refs) = refs[:-9], refs[-9:]
    total = parts[0][...].astype(F32)
    for part in parts[1:]:
        total = total + part[...].astype(F32)
    _, own_experts, rows, width = heads_ref.shape
    per_tile = 128 // width
    for expert in range(own_experts):
        at = expert // per_tile * rows
        lane = expert % per_tile * width
        heads_ref[0, expert] = total[at : at + rows, lane : lane + width]
    at = own_experts // per_tile * rows
    chunk = kv_ref.shape[1]
    kv_ref[0] = total[at : at + chunk]
    tile = total[at + chunk : at + 2 * chunk]
    router_ref[0] = tile[:, :experts]
    turned = tile.T
    for ref, row in zip(vector_refs, range(experts, experts + 5)):
        ref[...] = turned[row : row + 1]
    up_shift_ref[...] = jnp.concatenate(
        [turned[row : row + 1] for row in range(experts + 5, experts + 5 + deep)], 1
    )


def full(shape):
    return pl.BlockSpec(shape, lambda *ids: (0,) * len(shape))


def blocked(shape):
    tail = (0,) * (len(shape) - 2)
    return pl.BlockSpec((1, 1) + tuple(shape[2:]), lambda m, i, *refs: (m, i) + tail)


def grouped(shape, group):
    tail = (0,) * (len(shape) - 2)
    return pl.BlockSpec((1, group) + tuple(shape[2:]), lambda m, i, *refs: (m, i) + tail)


def in_place():
    return pl.BlockSpec(memory_space=pl.ANY)


def reversed_blocks(shape):
    tail = (0,) * (len(shape) - 2)
    last = shape[1] - 1
    return pl.BlockSpec((1, 1) + tuple(shape[2:]), lambda m, i, *refs: (m, last - i) + tail)


def whole(shape):
    tail = (0,) * (len(shape) - 1)
    return pl.BlockSpec((1,) + tuple(shape[1:]), lambda m, i, *refs: (m,) + tail)


def struct(shape, dtype):
    return jax.ShapeDtypeStruct(shape, dtype)


def params():
    return pltpu.CompilerParams(
        dimension_semantics=("arbitrary", "arbitrary"), vmem_limit_bytes=VMEM_BYTES
    )


def cost(flops, transcendentals, moved):
    return pl.CostEstimate(flops=flops, transcendentals=transcendentals, bytes_accessed=moved)


def exchange(value, axis, distance):
    count = lax.axis_size(axis)
    return lax.ppermute(value, axis, [(at, at ^ distance) for at in range(count)])


def permute_groups(value, index):
    groups = value.shape[0]
    bit = 1
    while bit < groups:
        pairs = value.reshape((groups // (2 * bit), 2, bit) + value.shape[1:])
        value = jnp.where((index & bit) != 0, pairs[:, ::-1].reshape(value.shape), value)
        bit *= 2
    return value


def pick_at(value, index, dim):
    return lax.dynamic_index_in_dim(value, index, dim, keepdims=False)


def reduce_axis(value, axis, dim, relative=False, keep=False):
    count = lax.axis_size(axis)
    me = lax.axis_index(axis)
    base = 0 if relative else me
    total = pick_at(value, base, dim).astype(F32)
    for distance in range(1, count):
        sent = pick_at(value, distance if relative else me ^ distance, dim)
        total = total + exchange(sent, axis, distance).astype(F32)
    return total if keep else total.astype(BF16)


def core_stage(grads):
    keep, send = grads
    other = exchange(send, "fsdp", 1)
    return [(keep[at].astype(F32) + other[at].astype(F32)).astype(BF16) for at in range(keep.shape[0])]


def split_targets(value, axis):
    return [value[at] for at in range(lax.axis_size(axis))]


def send_stage(parts, axis):
    return [exchange(parts[distance], axis, distance) for distance in range(1, len(parts))]


def total_up(own, received):
    total = own.astype(F32)
    for part in received:
        total = total + part.astype(F32)
    return total


def add_up(own, received):
    return total_up(own, received).astype(BF16)


def open_tiles(value, at, rows, columns):
    count = columns // 128
    tiles = value[at : at + count * rows].reshape(count, rows, 128)
    return jnp.swapaxes(tiles, 0, 1).reshape(rows, columns), at + count * rows


def local(
    inputs,
    lengths,
    routes,
    ln1_gain,
    ln1_bias,
    kv_weight,
    router_weight,
    query_weight,
    out_weight,
    ln2_gain,
    ln2_bias,
    up_weight,
    up_bias,
    down_weight,
    down_bias,
    out_cotangent,
):
    micro_count, _, slots, model = inputs.shape
    experts = router_weight.shape[2]
    width = query_weight.shape[3]
    picks = routes.shape[4]
    hidden_units = up_weight.shape[2]
    dp_size, z_size, f_size = (lax.axis_size(axis) for axis in AXES)
    dp_at, z_at, f_at = (lax.axis_index(axis) for axis in AXES)
    ids = jnp.stack([dp_at, z_at, f_at]).astype(jnp.int32)
    seq_index = (dp_at * z_size + z_at) * f_size + f_at
    devices = dp_size * z_size * f_size
    own_experts = experts // z_size
    half = model // f_size
    span = min(BLOCK, slots)
    blocks = slots // span
    rows = picks * span
    group = 2 if blocks % 2 == 0 else 1
    head = experts * width
    spare = -(-experts // 16) * 16
    all_rows = head + 2 * width + spare
    chunk = model // devices
    aligned = chunk % 16 == 0 and (head // z_size) % 128 == 0
    lens = lax.dynamic_index_in_dim(lengths, seq_index, 1, keepdims=False)

    def both_halves(own, other, dim):
        near = jnp.concatenate([own, other], dim)
        return jnp.where(f_at == 0, near, jnp.concatenate([other, own], dim))

    def head_parts(own):
        return [own] + [exchange(own, "expert", distance) for distance in range(1, z_size)]

    def transposed(weight):
        return jnp.swapaxes(weight[0], 1, 2).reshape(own_experts * width, half)

    def start_of(routes):
        local_routes = routes[0, :, 0]
        group = (local_routes // own_experts) ^ z_at
        local_routes = group * own_experts + local_routes % own_experts
        return jnp.swapaxes(local_routes.reshape(micro_count, blocks, span, picks), 2, 3)

    query_parts = head_parts(transposed(query_weight))
    router_t = router_weight[0].T.reshape(z_size, own_experts, half)
    router_t = permute_groups(router_t, z_at).reshape(experts, half)
    router_t = jnp.pad(router_t, ((0, spare - experts), (0, 0)))
    vectors = jnp.concatenate([ln1_gain, ln1_bias, ln2_gain, ln2_bias, down_bias], 0)
    small = jnp.concatenate([vectors, up_bias.reshape(-1, half)], 0)
    small_other = exchange(small, "fsdp", 1)
    vectors = both_halves(vectors, small_other[:5], 1).astype(F32)
    up_shift = both_halves(up_bias, small_other[5:].reshape(1, -1), 1).astype(F32)

    up_other = exchange(up_weight[0], "fsdp", 1)
    down_other = exchange(down_weight[0], "fsdp", 1)
    route_t = start_of(routes)
    own_out = transposed(out_weight)
    lens, ids, route_t, vectors, up_shift, router_t, own_out, *query_parts = (
        lax.optimization_barrier(
            (lens, ids, route_t, vectors, up_shift, router_t, own_out, *query_parts)
        )
    )
    proj = jnp.concatenate(query_parts + [kv_weight[0].T, router_t], 0)
    proj_other = exchange(proj, "fsdp", 1)
    out_parts = head_parts(own_out)

    states = inputs.reshape(micro_count, blocks, span, model)
    cotangent = out_cotangent.reshape(micro_count, blocks, span, model)

    grid = (micro_count, blocks)
    hid_s = struct((micro_count, blocks, span, model), BF16)
    aug_s = struct((micro_count, blocks, span, 2 * width), BF16)
    kt_s = struct((micro_count, blocks, 1, width, span), BF16)
    q_s = struct((micro_count, blocks, width, rows), BF16)
    row_s = struct((micro_count, blocks, 1, rows), F32)
    gate_s = struct((micro_count, blocks, experts, span), F32)
    slot_s = struct((micro_count, blocks, experts, span), jnp.int32)
    tokens = micro_count * slots
    pair_flops = tokens * picks * slots * width
    hid, kaug, vaug, kt, q, ctx, lse, gates, slot = pl.pallas_call(
        forward_kernel,
        name="forward",
        grid_spec=pltpu.PrefetchScalarGridSpec(
            num_scalar_prefetch=2,
            grid=grid,
            in_specs=[
                blocked(states.shape),
                blocked(route_t.shape),
                full(vectors.shape),
                in_place(),
                in_place(),
            ],
            out_specs=[
                blocked(hid_s.shape),
                whole(aug_s.shape),
                whole(aug_s.shape),
                blocked(kt_s.shape),
                blocked(q_s.shape),
                blocked(q_s.shape),
                blocked(row_s.shape),
                blocked(gate_s.shape),
                blocked(slot_s.shape),
            ],
            scratch_shapes=[
                pltpu.VMEM((head, span), BF16),
                pltpu.VMEM((2 * width, rows), BF16),
                pltpu.VMEM((blocks, span, rows), F32),
                pltpu.VMEM((blocks, width, span), BF16),
                pltpu.VMEM((width, rows), F32),
                pltpu.VMEM((2 * all_rows, half), BF16),
                pltpu.SemaphoreType.DMA((2,)),
            ],
        ),
        out_shape=[hid_s, aug_s, aug_s, kt_s, q_s, q_s, row_s, gate_s, slot_s],
        compiler_params=params(),
        cost_estimate=cost(2 * tokens * model * all_rows + 16 * pair_flops, 0, 64 << 20),
    )(lens, ids, states, route_t, vectors, proj, proj_other)

    ctx, *out_parts = lax.optimization_barrier((ctx, *out_parts))
    out_proj = jnp.concatenate(out_parts, 0)
    out_other = exchange(out_proj, "fsdp", 1)
    state_s = struct((micro_count, blocks, span, model), F32)
    mid_rows = chunk * hidden_units * 2 // 128 + head // z_size * (chunk * z_size) // 128
    late_rows = head // z_size * (chunk * z_size) // 128 + 2 * chunk
    if aligned:
        mid_grads = [struct((dp_size, z_size, mid_rows, 128), BF16)] * 2
        late_grads = [struct((dp_size, z_size, late_rows, 128), BF16)] * 2
    else:
        mid_grads = [
            struct((hidden_units, model), BF16),
            struct((model, hidden_units), BF16),
            struct((model, head), BF16),
        ]
        late_grads = [struct((model, head + 2 * width + 128), BF16)]
    outputs, mid, grad_ctx, delta, grad_logits, small2, up_small, *mid_grads = pl.pallas_call(
        middle_kernel,
        name="middle",
        grid_spec=pltpu.PrefetchScalarGridSpec(
            num_scalar_prefetch=2,
            grid=(micro_count, blocks // group),
            in_specs=[
                grouped(states.shape, group),
                grouped(q_s.shape, group),
                grouped(gate_s.shape, group),
                grouped(slot_s.shape, group),
                grouped(cotangent.shape, group),
                in_place(),
                in_place(),
                full(vectors.shape),
                in_place(),
                in_place(),
                full(up_shift.shape),
                in_place(),
                in_place(),
            ],
            out_specs=[
                grouped(state_s.shape, group),
                grouped(state_s.shape, group),
                grouped(q_s.shape, group),
                grouped(row_s.shape, group),
                grouped(gate_s.shape, group),
                full((3, 8, model)),
                full((8, hidden_units)),
            ]
            + [full(leaf.shape) for leaf in mid_grads],
            scratch_shapes=[
                pltpu.VMEM((group, width, rows), BF16),
                pltpu.VMEM((head, group * span), BF16),
                pltpu.VMEM((head, group * span), BF16),
                pltpu.VMEM((hidden_units, model), F32),
                pltpu.VMEM((model, hidden_units), F32),
                pltpu.VMEM((model, head), F32),
                pltpu.VMEM((2 * head, half), BF16),
                pltpu.VMEM((model, hidden_units), BF16),
                pltpu.VMEM((hidden_units, model), BF16),
                pltpu.SemaphoreType.DMA((6,)),
            ],
        ),
        out_shape=[
            state_s,
            hid_s,
            q_s,
            row_s,
            gate_s,
            struct((3, 8, model), F32),
            struct((8, hidden_units), F32),
        ]
        + mid_grads,
        compiler_params=params(),
        cost_estimate=cost(2 * tokens * model * (6 * hidden_units + 3 * head), 0, 200 << 20),
    )(
        lens,
        ids,
        states,
        ctx,
        gates,
        slot,
        cotangent,
        out_proj,
        out_other,
        vectors,
        up_weight[0],
        up_other,
        up_shift,
        down_weight[0],
        down_other,
    )

    if aligned:
        mid_sums = core_stage(mid_grads)
        grad_ctx, *mid_sums = lax.optimization_barrier((grad_ctx, *mid_sums))
        mid_received = send_stage(mid_sums, "dp")

    expert_id = jnp.arange(experts)
    moved = ((expert_id // own_experts) ^ z_at) * own_experts + expert_id % own_experts
    order = jnp.pad(
        (jnp.arange(spare)[:, None] == moved[None, :]).astype(BF16), ((0, 0), (0, 128 - experts))
    )
    deep = hidden_units // model
    columns = jnp.concatenate(
        [
            vectors[:2].T,
            jnp.sum(small2, 1).T,
            jnp.swapaxes(jnp.sum(up_small, 0).reshape(devices, deep, chunk), 1, 2).reshape(model, deep),
        ],
        1,
    )
    columns = jnp.pad(columns, ((0, 0), (experts, 128 - experts - 5 - deep)))
    r_s = struct((micro_count, blocks // group, all_rows, group * span), BF16)

    def routed_block(m, i, *refs):
        block = blocks - 1 - i
        return m, block // group, 0, block % group

    routed, *late_grads = pl.pallas_call(
        backward_kernel,
        name="backward",
        grid_spec=pltpu.PrefetchScalarGridSpec(
            num_scalar_prefetch=2,
            grid=grid,
            in_specs=[
                reversed_blocks(hid_s.shape),
                whole(aug_s.shape),
                whole(aug_s.shape),
                whole((micro_count, blocks, width, span)),
                reversed_blocks(q_s.shape),
                reversed_blocks(row_s.shape),
                reversed_blocks(q_s.shape),
                reversed_blocks(row_s.shape),
                reversed_blocks(slot_s.shape),
                reversed_blocks(gate_s.shape),
                full(order.shape),
                full(columns.shape),
                in_place(),
                in_place(),
            ],
            out_specs=[pl.BlockSpec((1, 1, all_rows, span), routed_block)]
            + [full(leaf.shape) for leaf in late_grads],
            scratch_shapes=[
                pltpu.VMEM((2 * width, rows), BF16),
                pltpu.VMEM((2 * width, rows), BF16),
                pltpu.VMEM((width, rows), F32),
                pltpu.VMEM((blocks, width, span), F32),
                pltpu.VMEM((blocks, width, span), F32),
                pltpu.VMEM((model + 16, head + 2 * width + 128), F32),
                pltpu.VMEM((2 * all_rows, half), BF16),
                pltpu.SemaphoreType.DMA((2,)),
            ],
        ),
        out_shape=[r_s] + late_grads,
        compiler_params=params(),
        cost_estimate=cost(2 * tokens * model * all_rows + 40 * pair_flops, 0, 100 << 20),
    )(
        lens,
        ids,
        hid,
        kaug,
        vaug,
        kt.reshape(micro_count, blocks, width, span),
        q,
        lse,
        grad_ctx,
        delta,
        slot,
        grad_logits,
        order,
        columns,
        proj,
        proj_other,
    )

    if aligned:
        *mid_received, late_grads[0], late_grads[1] = lax.optimization_barrier(
            (*mid_received, *late_grads)
        )
        *mid_received, late_grads[0], late_grads[1] = lax.optimization_barrier(
            (*mid_received, *late_grads)
        )
        late_sums = core_stage(late_grads)
        *mid_received, late_sums[0] = lax.optimization_barrier((*mid_received, late_sums[0]))
        mid_sums = split_targets(add_up(mid_sums[0], mid_received), "expert")
        routed, *sums = lax.optimization_barrier((routed, *mid_sums, *late_sums))
        mid_sums, late_sums = sums[:z_size], sums[z_size:]
        mid_received = send_stage(mid_sums, "expert")
        late_received = send_stage(late_sums, "dp")

    input_grad = pl.pallas_call(
        input_kernel,
        name="input_back",
        grid_spec=pltpu.PrefetchScalarGridSpec(
            num_scalar_prefetch=1,
            grid=(micro_count, blocks // group),
            in_specs=[
                grouped(states.shape, group),
                grouped(state_s.shape, group),
                blocked(r_s.shape),
                in_place(),
                in_place(),
                full(vectors.shape),
            ],
            out_specs=grouped(state_s.shape, group),
            scratch_shapes=[
                pltpu.VMEM((2 * all_rows, half), BF16),
                pltpu.SemaphoreType.DMA((2,)),
            ],
        ),
        out_shape=state_s,
        compiler_params=params(),
        cost_estimate=cost(2 * tokens * model * all_rows, 0, 40 << 20),
    )(ids[2:], states, mid, routed, proj, proj_other, vectors)

    def open_heads(value):
        return jnp.swapaxes(value.reshape(-1, own_experts, width), 0, 1)[None]

    if aligned:
        input_grad, *received = lax.optimization_barrier(
            (input_grad, *late_received, *mid_received)
        )
        late_received = received[: dp_size - 1]
        mid_received = received[dp_size - 1 :]
        late_sums = split_targets(add_up(late_sums[0], late_received), "expert")
        late_received = send_stage(late_sums, "expert")
        mid_total = total_up(mid_sums[0], mid_received)
        up_weight_grad, at = open_tiles(mid_total, 0, chunk, hidden_units)
        down_weight_grad, at = open_tiles(mid_total, at, hidden_units // devices, model)
        out_weight_grad, at = open_tiles(mid_total, at, chunk * z_size, head // z_size)
        out_weight_grad = open_heads(out_weight_grad)
        query_weight_grad, kv_grad, router_grad, up_bias_grad, *small = pl.pallas_call(
            functools.partial(finish_kernel, experts, deep),
            name="finish",
            out_shape=[
                struct((1, own_experts, chunk * z_size, width), F32),
                struct((1, chunk, 2 * width), F32),
                struct((1, chunk, experts), F32),
                struct((1, deep * chunk), F32),
            ]
            + [struct((1, chunk), F32)] * 5,
        )(late_sums[0], *late_received)
    else:
        down_grad, up_grad, wo_grad = mid_grads
        w_grad = late_grads[0]

        def reduce_shared(value, part):
            value = value.reshape(dp_size, z_size, f_size, part, value.shape[1])
            value = reduce_axis(value, "fsdp", 2)
            value = reduce_axis(value, "dp", 0)
            return reduce_axis(value, "expert", 0, keep=True)

        def reduce_heads(value):
            value = value.reshape(dp_size, f_size, chunk * z_size, z_size, own_experts * width)
            value = reduce_axis(value, "fsdp", 1)
            value = reduce_axis(value, "dp", 0)
            return open_heads(reduce_axis(value, "expert", 1, relative=True, keep=True))

        up_weight_grad = reduce_shared(up_grad, chunk)
        down_weight_grad = reduce_shared(down_grad, hidden_units // devices)
        out_weight_grad = reduce_heads(wo_grad)
        query_weight_grad = reduce_heads(w_grad[:, :head])
        narrow = reduce_shared(w_grad[:, head:], chunk)
        kv_grad, router_grad = narrow[None, :, : 2 * width], narrow[None, :, 2 * width :]
        small = [router_grad[:, :, experts + at] for at in range(5)]
        up_bias_grad = router_grad[0, :, experts + 5 : experts + 5 + deep].T.reshape(1, -1)
        router_grad = router_grad[:, :, :experts]
    shape = (micro_count, 1, slots, model)
    return (
        outputs.reshape(shape),
        input_grad.reshape(shape),
        small[0],
        small[1],
        kv_grad,
        router_grad,
        query_weight_grad,
        out_weight_grad,
        small[2],
        small[3],
        up_weight_grad[None],
        up_bias_grad,
        down_weight_grad[None],
        small[4],
    )


def solution(mesh):
    shards = P(None, AXES, None, None)
    return jax.shard_map(
        local,
        mesh=mesh,
        in_specs=(
            shards,
            P(),
            P(None, None, AXES, None, None),
            P(None, "fsdp"),
            P(None, "fsdp"),
            P(None, "fsdp", None),
            P(None, "fsdp", None),
            P(None, "expert", "fsdp", None),
            P(None, "expert", "fsdp", None),
            P(None, "fsdp"),
            P(None, "fsdp"),
            P(None, "fsdp", None),
            P(None, "fsdp"),
            P(None, "fsdp", None),
            P(None, "fsdp"),
            shards,
        ),
        out_specs=(
            shards,
            shards,
            P(None, AXES),
            P(None, AXES),
            P(None, AXES, None),
            P(None, AXES, None),
            P(None, "expert", ("dp", "fsdp"), None),
            P(None, "expert", ("dp", "fsdp"), None),
            P(None, AXES),
            P(None, AXES),
            P(None, AXES, None),
            P(None, AXES),
            P(None, AXES, None),
            P(None, AXES),
        ),
        check_vma=False,
    )
```

```python
import functools

import jax
import jax.numpy as jnp
from jax import lax
from jax.experimental import pallas as pl
from jax.experimental.pallas import tpu as pltpu
from jax.sharding import PartitionSpec as P

EPSILON = 1e-05
NEGATIVE = -1e30
GELU_SCALE = 0.7978845608028654
GELU_CUBIC = 0.044715
BLOCK = 256
AXES = ("dp", "expert", "fsdp")
F32 = jnp.float32
BF16 = jnp.bfloat16
VMEM_BYTES = 60 << 20


def dot_nn(left, right):
    return lax.dot_general(left, right, (((1,), (0,)), ((), ())), preferred_element_type=F32)


def dot_nt(left, right):
    return lax.dot_general(left, right, (((1,), (1,)), ((), ())), preferred_element_type=F32)


def dot_tn(left, right):
    return lax.dot_general(left, right, (((0,), (0,)), ((), ())), preferred_element_type=F32)


def normalize(values):
    center = values - jnp.mean(values, -1, keepdims=True)
    spread = lax.rsqrt(jnp.mean(center * center, -1, keepdims=True) + EPSILON)
    return center * spread, spread


def halves(ref):
    rows = ref.shape[0] // 2
    return ref.at[pl.ds(0, rows)], ref.at[pl.ds(rows, rows)]


def fold_rows(values, combine):
    rows, columns = values.shape
    return combine(values.reshape(rows // 8, 8, columns), 0)


def pick_slots(table_ref, slot, picks, width, start=0):
    experts, span = slot.shape
    lanes = slice(start, start + span)
    slot = slot.astype(table_ref.dtype)
    picked = []
    for pick in range(picks):
        value = table_ref[pick * width : (pick + 1) * width, lanes]
        for expert in range(pick + 1, experts - picks + pick + 1):
            hit = jnp.broadcast_to(slot[expert : expert + 1, :], (width, span)) == pick
            value = jnp.where(hit, table_ref[expert * width : (expert + 1) * width, lanes], value)
        picked.append(value)
    return picked


def spread_slots(read, slot, expert, picks, width, span):
    experts = slot.shape[0]
    row = jnp.broadcast_to(slot[expert : expert + 1, :], (width, span))
    value = jnp.zeros((width, span), slot.dtype)
    for pick in range(max(0, expert - experts + picks), min(expert, picks - 1) + 1):
        value = jnp.where(row == pick, read(pick), value)
    return value


def forward_kernel(
    lens,
    ids,
    x_ref,
    route_ref,
    vec_ref,
    own_ref,
    other_ref,
    hid_ref,
    kaug_ref,
    vaug_ref,
    kt_ref,
    q_ref,
    ctx_ref,
    lse_ref,
    gate_ref,
    slot_ref,
    table,
    qaug,
    scores,
    vt,
    acc,
    w_ref,
    sems,
):
    block = pl.program_id(1)
    length = lens[pl.program_id(0)]
    first = (pl.program_id(0) == 0) & (block == 0)
    copies = half_copies(ids[2], sems, [(own_ref, other_ref, w_ref)])
    start_all(first, copies)
    wait_all(first, copies)
    span = x_ref.shape[2]
    experts = slot_ref.shape[2]
    picks = route_ref.shape[2]
    width = kt_ref.shape[3]
    half = w_ref.shape[1]
    low, high = halves(w_ref)
    rows = picks * span

    normed, _ = normalize(x_ref[0, 0].astype(F32))
    hid = (normed * vec_ref[0:1, :] + vec_ref[1:2, :]).astype(BF16)
    hid_ref[0, 0] = hid
    head = experts * width
    products = dot_nt(low[...], hid[:, :half]) + dot_nt(high[...], hid[:, half:])
    table[...] = products[:head].astype(BF16)
    kt_ref[0, 0, 0] = products[head : head + width, :].astype(BF16)
    vt[block] = products[head + width : head + 2 * width, :].astype(BF16)

    lane = lax.broadcasted_iota(jnp.int32, (span, 2 * width), 1)
    place = block * span + lax.broadcasted_iota(jnp.int32, (span, 2 * width), 0)
    ones = jnp.where(lane < width + 4, 1.0, 0.0)
    cut = jnp.where(place < length, 0.0, NEGATIVE)
    both = dot_nt(hid[:, :half], low[head : head + 2 * width, :])
    both = both + dot_nt(hid[:, half:], high[head : head + 2 * width, :])
    keys = jnp.where(lane < width, both, jnp.where(lane == width, cut, ones))
    kaug_ref[0, block] = keys.astype(BF16)
    vals = jnp.where(lane < width, pltpu.roll(both, width, 1), ones)
    vaug_ref[0, block] = vals.astype(BF16)

    logits = products[head + 2 * width : head + 2 * width + experts, :]
    expert_id = lax.broadcasted_iota(jnp.int32, (experts, span), 0)
    chosen = jnp.zeros((experts, span), F32)
    for pick in range(picks):
        chosen = jnp.where(expert_id == route_ref[0, 0, pick : pick + 1, :], 1.0, chosen)
    lower = jnp.where(
        lax.broadcasted_iota(jnp.int32, (experts, experts), 1)
        < lax.broadcasted_iota(jnp.int32, (experts, experts), 0),
        1.0,
        0.0,
    )
    slot = jnp.where(chosen > 0.0, dot_nn(lower, chosen), -1.0).astype(jnp.int32)
    slot_ref[0, 0] = slot
    masked = jnp.where(chosen > 0.0, logits, NEGATIVE)
    raised = jnp.where(chosen > 0.0, jnp.exp(masked - jnp.max(masked, 0, keepdims=True)), 0.0)
    gate_ref[0, 0] = raised / jnp.sum(raised, 0, keepdims=True)

    picked = pick_slots(table, slot, picks, width)
    for pick in range(picks):
        qaug[0:width, pick * span : (pick + 1) * span] = (
            picked[pick] * (width**-0.5)
        ).astype(BF16)
    q_ref[0, 0] = qaug[0:width, :]
    side = lax.broadcasted_iota(jnp.int32, (width, rows), 0)
    qaug[width : 2 * width, :] = jnp.where(side == 0, 1.0, 0.0).astype(BF16)

    def score_step(at, top):
        part = dot_nn(kaug_ref[0, at], qaug[...])
        scores[at] = part
        return jnp.maximum(top, fold_rows(part, jnp.max))

    used = jnp.minimum(block, (length + span - 1) // span)
    top = lax.fori_loop(0, used, score_step, jnp.full((8, rows), NEGATIVE, F32))
    causal = lax.broadcasted_iota(jnp.int32, (span, rows), 0) <= (
        lax.broadcasted_iota(jnp.int32, (span, rows), 1) & (span - 1)
    )
    part = jnp.where(causal, dot_nn(kaug_ref[0, block], qaug[...]), NEGATIVE)
    top = jnp.maximum(top, fold_rows(part, jnp.max))
    top = jnp.max(top, 0, keepdims=True)
    raised = jnp.exp(part - top)
    acc[...] = dot_nn(vt[block], raised.astype(BF16))
    total = fold_rows(raised, jnp.sum)

    def value_step(at, total):
        raised = jnp.exp(scores[at] - top)
        acc[...] += dot_nn(vt[at], raised.astype(BF16))
        return total + fold_rows(raised, jnp.sum)

    total = lax.fori_loop(0, used, value_step, total)
    total = jnp.sum(total, 0, keepdims=True)
    ctx_ref[0, 0] = (acc[...] * (1.0 / total)).astype(BF16)
    lse_ref[0, 0] = top + jnp.log(total)


def middle_kernel(
    lens,
    ids,
    x_ref,
    ctx_ref,
    gate_ref,
    slot_ref,
    cot_ref,
    own_ref,
    other_ref,
    vec_ref,
    own_up_ref,
    other_up_ref,
    up_shift_ref,
    own_down_ref,
    other_down_ref,
    out_ref,
    mid_ref,
    do_ref,
    delta_ref,
    gl_ref,
    small_ref,
    up_shift_grad_ref,
    *rest,
):
    *grad_refs, gated, cexp, table, down_acc, up_acc, wo_acc, w_ref, up_ref, down_ref, sems = rest
    micro = pl.program_id(0)
    block = pl.program_id(1)
    length = lens[micro]
    subs, span, model = x_ref.shape[1:]
    tokens = subs * span
    experts = slot_ref.shape[2]
    width = ctx_ref.shape[2]
    picks = ctx_ref.shape[3] // span
    head = experts * width
    half = w_ref.shape[1]
    low, high = halves(w_ref)
    first = (micro == 0) & (block == 0)
    last = (micro == pl.num_programs(0) - 1) & (block == pl.num_programs(1) - 1)

    def clear():
        down_acc[...] = jnp.zeros_like(down_acc)
        up_acc[...] = jnp.zeros_like(up_acc)
        wo_acc[...] = jnp.zeros_like(wo_acc)
        small_ref[...] = jnp.zeros_like(small_ref)
        up_shift_grad_ref[...] = jnp.zeros_like(up_shift_grad_ref)

    copies = half_copies(
        ids[2],
        sems,
        [
            (own_ref, other_ref, w_ref),
            (own_up_ref, other_up_ref, up_ref),
            (own_down_ref, other_down_ref, down_ref),
        ],
    )
    start_all(first, copies, clear)
    wait_all(first, copies)
    slots = [slot_ref[0, sub] for sub in range(subs)]
    gate = []
    for sub in range(subs):
        gates = gate_ref[0, sub]
        gate.append(
            [
                jnp.sum(jnp.where(slots[sub] == pick, gates, 0.0), 0, keepdims=True)
                for pick in range(picks)
            ]
        )
        for pick in range(picks):
            at = slice(pick * span, (pick + 1) * span)
            gated[sub, :, at] = (ctx_ref[0, sub, :, at].astype(F32) * gate[sub][pick]).astype(BF16)
        for expert in range(experts):
            cexp[expert * width : (expert + 1) * width, sub * span : (sub + 1) * span] = spread_slots(
                lambda pick: gated[sub, :, pick * span : (pick + 1) * span],
                slots[sub].astype(BF16),
                expert,
                picks,
                width,
                span,
            )
    mixed = x_ref[0].reshape(tokens, model).astype(F32) + jnp.concatenate(
        [dot_tn(cexp[...], low[...]), dot_tn(cexp[...], high[...])], 1
    )
    normed, spread = normalize(mixed)
    hid = (normed * vec_ref[2:3, :] + vec_ref[3:4, :]).astype(BF16)
    place = block * tokens + lax.broadcasted_iota(jnp.int32, (tokens, 1), 0)
    grad = jnp.where(place < length, cot_ref[0].reshape(tokens, model), 0.0)
    grad_b = grad.astype(BF16)
    hid_t = hid.T
    out = mixed + vec_ref[4:5, :]
    back = jnp.zeros_like(mixed)
    hidden_units = up_ref.shape[1]
    step = min(hidden_units, 256)
    cuts = [slice(at, at + step) for at in range(0, hidden_units, step)]

    def ahead(cut):
        return dot_nn(hid, up_ref[:, cut]), dot_nt(grad_b, down_ref[cut, :])

    held = ahead(cuts[0])
    ready = None
    for n in range(len(cuts) + 1):
        pre, grad_act = held if held is not None else (None, None)
        held = ahead(cuts[n + 1]) if n + 1 < len(cuts) else None
        fresh = None
        if n < len(cuts):
            cut = cuts[n]
            pre = pre + up_shift_ref[:, cut]
            square = pre * pre
            bent = jnp.tanh(pre * (GELU_SCALE + (GELU_SCALE * GELU_CUBIC) * square))
            rise = 0.5 + 0.5 * bent
            slope = rise + (0.5 * pre) * (1.0 - bent * bent) * (
                GELU_SCALE + (3.0 * GELU_SCALE * GELU_CUBIC) * square
            )
            grad_pre = grad_act * slope
            up_shift_grad_ref[:, cut] += fold_rows(grad_pre, jnp.sum)
            fresh = (cut, (pre * rise).astype(BF16), grad_pre.astype(BF16))
        if ready is not None:
            cut, active, grad_pre_b = ready
            out = out + dot_nn(active, down_ref[cut, :])
            back = back + dot_nt(grad_pre_b, up_ref[:, cut])
            down_acc[cut, :] += dot_nn(active.T, grad_b)
            up_acc[:, cut] += dot_nn(hid_t, grad_pre_b)
        ready = fresh
    out_ref[0] = out.reshape(subs, span, model)
    scaled = back * vec_ref[2:3, :]
    mid = grad + spread * (
        scaled
        - jnp.mean(scaled, -1, keepdims=True)
        - normed * jnp.mean(scaled * normed, -1, keepdims=True)
    )
    small_ref[0] += fold_rows(back * normed, jnp.sum)
    small_ref[1] += fold_rows(back, jnp.sum)
    small_ref[2] += fold_rows(grad_b.astype(F32), jnp.sum)

    mid_b = mid.astype(BF16)
    mid_ref[0] = mid_b.reshape(subs, span, model)
    wo_acc[...] += dot_nt(mid_b.T, cexp[...])
    products = dot_nt(low[...], mid_b[:, :half]) + dot_nt(high[...], mid_b[:, half:])
    table[...] = products.astype(BF16)
    for sub in range(subs):
        slot = slots[sub]
        picked = pick_slots(table, slot, picks, width, sub * span)
        grad_gate = []
        for pick in range(picks):
            at = slice(pick * span, (pick + 1) * span)
            ctx = ctx_ref[0, sub, :, at].astype(F32)
            found = picked[pick].astype(F32)
            grad_gate.append(jnp.sum(found * ctx, 0, keepdims=True))
            grad_ctx = (found * gate[sub][pick]).astype(BF16)
            do_ref[0, sub, :, at] = grad_ctx
            delta_ref[0, sub, :, at] = jnp.sum(grad_ctx.astype(F32) * ctx, 0, keepdims=True)
        average = gate[sub][0] * grad_gate[0]
        for pick in range(1, picks):
            average = average + gate[sub][pick] * grad_gate[pick]
        grad_logits = jnp.zeros((experts, span), F32)
        for pick in range(picks):
            grad_logits = jnp.where(
                slot == pick, gate[sub][pick] * (grad_gate[pick] - average), grad_logits
            )
        gl_ref[0, sub] = grad_logits

    @pl.when(last)
    def _():
        if len(grad_refs) == 3:
            for ref, total in zip(grad_refs, (down_acc, up_acc, wo_acc)):
                ref[...] = total[...].astype(BF16)
            return
        targets = grad_refs[0].shape[0] * grad_refs[0].shape[1]
        up_rows = up_acc.shape[0] // (2 * targets)
        down_rows = down_acc.shape[0] // (2 * targets)

        def pack(ref, to, fro, shared, heads):
            at = pack_tiles(ref, to, 0, up_acc, shared * up_rows, up_rows, 0, up_acc.shape[1])
            at = pack_tiles(ref, to, at, down_acc, shared * down_rows, down_rows, 0, down_acc.shape[1])
            rows, columns = heads_chunk(wo_acc.shape[0], head, ref)
            pack_tiles(ref, to, at, wo_acc, heads * rows, rows, fro * columns, columns)

        for_targets(ids, grad_refs, pack)


def half_copies(core, sems, moves):
    copies = []
    for own, other, target in moves:
        half = target.shape[0] // 2
        for source, at in ((own, core), (other, 1 - core)):
            place = target.at[pl.ds(pl.multiple_of(at * half, half), half)]
            copies.append(pltpu.make_async_copy(source, place, sems.at[len(copies)]))
    return copies


def start_all(first, copies, meanwhile=lambda: None):
    @pl.when(first)
    def _():
        for copy in copies:
            copy.start()
        meanwhile()


def wait_all(first, copies):
    @pl.when(first)
    def _():
        for copy in copies:
            copy.wait()


def pack_tiles(ref, to, at, total, row, rows, column, columns):
    row = pl.multiple_of(row, rows)
    for lane in range(0, columns, 128):
        start = column + lane
        if not isinstance(start, int):
            start = pl.multiple_of(start, 128)
        tile = total[pl.ds(row, rows), pl.ds(start, 128)]
        ref[to[0], to[1], at : at + rows, :] = tile.astype(BF16)
        at += rows
    return at


def heads_chunk(model, head, ref):
    return model // (2 * ref.shape[0]), head // ref.shape[1]


def for_targets(ids, refs, pack):
    def body(dp_far, carry):
        dp = dp_far ^ ids[0]
        for z_far in range(refs[0].shape[1]):
            for f_far in range(2):
                f = ids[2] ^ f_far
                shared = (dp * refs[0].shape[1] + (z_far ^ ids[1])) * 2 + f
                pack(refs[f_far], (dp_far, z_far), z_far, shared, dp * 2 + f)
        return carry

    lax.fori_loop(0, refs[0].shape[0], body, 0)


def split_three(values):
    high = values.astype(BF16).astype(F32)
    rest = values - high
    middle = rest.astype(BF16).astype(F32)
    return high, middle, rest - middle


def backward_kernel(
    lens,
    ids,
    hid_ref,
    kaug_ref,
    vaug_ref,
    kt_ref,
    q_ref,
    lse_ref,
    do_ref,
    delta_ref,
    slot_ref,
    gl_ref,
    order_ref,
    columns_ref,
    own_ref,
    other_ref,
    r_ref,
    *rest,
):
    *grad_refs, qaug, daug, dq, dkt, dvt, w_acc, w_ref, sems = rest
    micro = pl.program_id(0)
    step = pl.program_id(1)
    blocks = pl.num_programs(1)
    block = blocks - 1 - step
    length = lens[micro]
    span = hid_ref.shape[2]
    experts = slot_ref.shape[2]
    width = q_ref.shape[2]
    rows = q_ref.shape[3]
    picks = rows // span
    head = experts * width

    def clear():
        w_acc[...] = jnp.zeros_like(w_acc)

    copies = half_copies(ids[2], sems, [(own_ref, other_ref, w_ref)])
    start_all((micro == 0) & (step == 0), copies, clear)

    @pl.when(step == 0)
    def _():
        dkt[...] = jnp.zeros_like(dkt)
        dvt[...] = jnp.zeros_like(dvt)

    @pl.when(block * span >= length)
    def _():
        r_ref[...] = jnp.zeros_like(r_ref)

    @pl.when(block * span < length)
    def _():
        side = lax.broadcasted_iota(jnp.int32, (width, rows), 0)
        qaug[0:width, :] = q_ref[0, 0]
        high, middle, low = split_three(-lse_ref[0, 0])
        qaug[width : 2 * width, :] = jnp.where(
            side == 0,
            1.0,
            jnp.where(side == 1, high, jnp.where(side == 2, middle, jnp.where(side == 3, low, 0.0))),
        ).astype(BF16)
        daug[0:width, :] = do_ref[0, 0]
        high, middle, low = split_three(-delta_ref[0, 0])
        daug[width : 2 * width, :] = jnp.where(
            side == 0, high, jnp.where(side == 1, middle, jnp.where(side == 2, low, 0.0))
        ).astype(BF16)

        lanes = 256
        causal = lax.broadcasted_iota(jnp.int32, (span, lanes), 0) <= (
            lax.broadcasted_iota(jnp.int32, (span, lanes), 1) & (span - 1)
        )

        def key_step(at, diagonal):
            dv = dvt[at]
            dk = dkt[at]
            cuts = [slice(start, start + lanes) for start in range(0, rows, lanes)]

            def ahead(cut):
                return dot_nn(kaug_ref[0, at], qaug[:, cut]), dot_nn(vaug_ref[0, at], daug[:, cut])

            held = ahead(cuts[0])
            back = None
            for n in range(len(cuts) + 1):
                scores, dprobs = held if held is not None else (None, None)
                held = ahead(cuts[n + 1]) if n + 1 < len(cuts) else None
                fresh = None
                if n < len(cuts):
                    probs = jnp.exp(scores)
                    if diagonal:
                        probs = jnp.where(causal, probs, 0.0)
                    slopes = (probs * dprobs).astype(BF16)
                    fresh = (cuts[n], probs.astype(BF16), slopes)
                if back is not None:
                    cut, probs_b, slopes = back
                    dv = dv + dot_nt(daug[0:width, cut], probs_b)
                    dk = dk + dot_nt(qaug[0:width, cut], slopes)
                    part = dot_nn(kt_ref[0, at], slopes)
                    dq[:, cut] = part if diagonal else dq[:, cut] + part
                back = fresh
            dvt[at] = dv
            dkt[at] = dk

        key_step(block, True)

        def body(at, carry):
            key_step(at, False)
            return carry

        lax.fori_loop(0, block, body, 0)
        scaled = (dq[...] * (width**-0.5)).astype(BF16)
        slot = slot_ref[0, 0].astype(BF16)
        for expert in range(experts):
            r_ref[0, 0, expert * width : (expert + 1) * width, :] = spread_slots(
                lambda pick: scaled[:, pick * span : (pick + 1) * span],
                slot,
                expert,
                picks,
                width,
                span,
            )
        r_ref[0, 0, head : head + width, :] = dkt[block].astype(BF16)
        r_ref[0, 0, head + width : head + 2 * width, :] = dvt[block].astype(BF16)
        tail = r_ref.shape[2] - head - 2 * width
        r_ref[0, 0, head + 2 * width :, :] = jnp.concatenate(
            [gl_ref[0, 0], jnp.zeros((tail - experts, span), F32)], 0
        ).astype(BF16)
        summing = jnp.concatenate([hid_ref[0, 0].T, jnp.ones((16, span), BF16)], 0)
        w_acc[:, : r_ref.shape[2]] += dot_nt(summing, r_ref[0, 0])

    @pl.when((micro == pl.num_programs(0) - 1) & (step == blocks - 1))
    def _():
        for copy in copies:
            copy.wait()
        model = hid_ref.shape[3]
        used = r_ref.shape[2]
        low, high = halves(w_ref)
        token_sum = w_acc[model : model + 1, :used]
        gain_sum, shift_sum = [], []
        for at, part in ((0, low), (model // 2, high)):
            weight = part[...].T.astype(F32)
            total = w_acc[at : at + model // 2, :used]
            gain_sum.append(jnp.sum(weight * total, 1, keepdims=True))
            shift_sum.append(jnp.sum(weight * token_sum, 1, keepdims=True))
        gain_sum, shift_sum = jnp.concatenate(gain_sum, 0), jnp.concatenate(shift_sum, 0)
        columns = columns_ref[...]
        gain, shift = columns[:, experts : experts + 1], columns[:, experts + 1 : experts + 2]
        gain_sum = (gain_sum - shift * shift_sum) / gain
        lane = lax.broadcasted_iota(jnp.int32, columns.shape, 1)
        columns = jnp.where(
            lane == experts, gain_sum, jnp.where(lane == experts + 1, shift_sum, columns)
        )
        routed = head + 2 * width
        spare = order_ref.shape[0]
        router = w_acc[:model, routed : routed + spare].astype(BF16)
        w_acc[:model, routed:] = columns + dot_nn(router, order_ref[...])
        if len(grad_refs) == 1:
            grad_refs[0][...] = w_acc[:model, :].astype(BF16)
            return
        targets = grad_refs[0].shape[0] * grad_refs[0].shape[1]
        shared_rows = model // (2 * targets)

        def pack(ref, to, fro, shared, heads):
            rows, columns = heads_chunk(model, head, ref)
            at = pack_tiles(ref, to, 0, w_acc, heads * rows, rows, fro * columns, columns)
            pack_tiles(ref, to, at, w_acc, shared * shared_rows, shared_rows, head, w_acc.shape[1] - head)

        for_targets(ids, grad_refs, pack)


def input_kernel(
    ids, x_ref, mid_ref, r_ref, own_ref, other_ref, vec_ref, out_ref, w_ref, sems
):
    first = (pl.program_id(0) == 0) & (pl.program_id(1) == 0)
    copies = half_copies(ids[2], sems, [(own_ref, other_ref, w_ref)])
    start_all(first, copies)

    wait_all(first, copies)
    subs, span, model = x_ref.shape[1:]
    normed, spread = normalize(x_ref[0].reshape(subs * span, model).astype(F32))
    low, high = halves(w_ref)
    routed = r_ref[0, 0]
    back = jnp.concatenate([dot_tn(routed, low[...]), dot_tn(routed, high[...])], 1)
    scaled = back * vec_ref[0:1, :]
    total = mid_ref[0].reshape(subs * span, model).astype(F32) + spread * (
        scaled
        - jnp.mean(scaled, -1, keepdims=True)
        - normed * jnp.mean(scaled * normed, -1, keepdims=True)
    )
    out_ref[0] = total.reshape(subs, span, model)


def finish_kernel(experts, deep, *refs):
    parts, (heads_ref, kv_ref, router_ref, up_shift_ref, *vector_refs) = refs[:-9], refs[-9:]
    total = parts[0][...].astype(F32)
    for part in parts[1:]:
        total = total + part[...].astype(F32)
    _, own_experts, rows, width = heads_ref.shape
    per_tile = 128 // width
    for expert in range(own_experts):
        at = expert // per_tile * rows
        lane = expert % per_tile * width
        heads_ref[0, expert] = total[at : at + rows, lane : lane + width]
    at = own_experts // per_tile * rows
    chunk = kv_ref.shape[1]
    kv_ref[0] = total[at : at + chunk]
    tile = total[at + chunk : at + 2 * chunk]
    router_ref[0] = tile[:, :experts]
    turned = tile.T
    for ref, row in zip(vector_refs, range(experts, experts + 5)):
        ref[...] = turned[row : row + 1]
    up_shift_ref[...] = jnp.concatenate(
        [turned[row : row + 1] for row in range(experts + 5, experts + 5 + deep)], 1
    )


def full(shape):
    return pl.BlockSpec(shape, lambda *ids: (0,) * len(shape))


def blocked(shape):
    tail = (0,) * (len(shape) - 2)
    return pl.BlockSpec((1, 1) + tuple(shape[2:]), lambda m, i, *refs: (m, i) + tail)


def grouped(shape, group):
    tail = (0,) * (len(shape) - 2)
    return pl.BlockSpec((1, group) + tuple(shape[2:]), lambda m, i, *refs: (m, i) + tail)


def in_place():
    return pl.BlockSpec(memory_space=pl.ANY)


def reversed_blocks(shape):
    tail = (0,) * (len(shape) - 2)
    last = shape[1] - 1
    return pl.BlockSpec((1, 1) + tuple(shape[2:]), lambda m, i, *refs: (m, last - i) + tail)


def whole(shape):
    tail = (0,) * (len(shape) - 1)
    return pl.BlockSpec((1,) + tuple(shape[1:]), lambda m, i, *refs: (m,) + tail)


def struct(shape, dtype):
    return jax.ShapeDtypeStruct(shape, dtype)


def params():
    return pltpu.CompilerParams(
        dimension_semantics=("arbitrary", "arbitrary"), vmem_limit_bytes=VMEM_BYTES
    )


def cost(flops, transcendentals, moved):
    return pl.CostEstimate(flops=flops, transcendentals=transcendentals, bytes_accessed=moved)


def exchange(value, axis, distance):
    count = lax.axis_size(axis)
    return lax.ppermute(value, axis, [(at, at ^ distance) for at in range(count)])


def permute_groups(value, index):
    groups = value.shape[0]
    bit = 1
    while bit < groups:
        pairs = value.reshape((groups // (2 * bit), 2, bit) + value.shape[1:])
        value = jnp.where((index & bit) != 0, pairs[:, ::-1].reshape(value.shape), value)
        bit *= 2
    return value


def pick_at(value, index, dim):
    return lax.dynamic_index_in_dim(value, index, dim, keepdims=False)


def reduce_axis(value, axis, dim, relative=False, keep=False):
    count = lax.axis_size(axis)
    me = lax.axis_index(axis)
    base = 0 if relative else me
    total = pick_at(value, base, dim).astype(F32)
    for distance in range(1, count):
        sent = pick_at(value, distance if relative else me ^ distance, dim)
        total = total + exchange(sent, axis, distance).astype(F32)
    return total if keep else total.astype(BF16)


def core_stage(grads):
    keep, send = grads
    other = exchange(send, "fsdp", 1)
    return [(keep[at].astype(F32) + other[at].astype(F32)).astype(BF16) for at in range(keep.shape[0])]


def split_targets(value, axis):
    return [value[at] for at in range(lax.axis_size(axis))]


def send_stage(parts, axis):
    return [exchange(parts[distance], axis, distance) for distance in range(1, len(parts))]


def total_up(own, received):
    total = own.astype(F32)
    for part in received:
        total = total + part.astype(F32)
    return total


def add_up(own, received):
    return total_up(own, received).astype(BF16)


def open_tiles(value, at, rows, columns):
    count = columns // 128
    tiles = value[at : at + count * rows].reshape(count, rows, 128)
    return jnp.swapaxes(tiles, 0, 1).reshape(rows, columns), at + count * rows


def local(
    inputs,
    lengths,
    routes,
    ln1_gain,
    ln1_bias,
    kv_weight,
    router_weight,
    query_weight,
    out_weight,
    ln2_gain,
    ln2_bias,
    up_weight,
    up_bias,
    down_weight,
    down_bias,
    out_cotangent,
):
    micro_count, _, slots, model = inputs.shape
    experts = router_weight.shape[2]
    width = query_weight.shape[3]
    picks = routes.shape[4]
    hidden_units = up_weight.shape[2]
    dp_size, z_size, f_size = (lax.axis_size(axis) for axis in AXES)
    dp_at, z_at, f_at = (lax.axis_index(axis) for axis in AXES)
    ids = jnp.stack([dp_at, z_at, f_at]).astype(jnp.int32)
    seq_index = (dp_at * z_size + z_at) * f_size + f_at
    devices = dp_size * z_size * f_size
    own_experts = experts // z_size
    half = model // f_size
    span = min(BLOCK, slots)
    blocks = slots // span
    rows = picks * span
    group = 2 if blocks % 2 == 0 else 1
    head = experts * width
    spare = -(-experts // 16) * 16
    all_rows = head + 2 * width + spare
    chunk = model // devices
    aligned = chunk % 16 == 0 and (head // z_size) % 128 == 0
    lens = lax.dynamic_index_in_dim(lengths, seq_index, 1, keepdims=False)

    def both_halves(own, other, dim):
        near = jnp.concatenate([own, other], dim)
        return jnp.where(f_at == 0, near, jnp.concatenate([other, own], dim))

    def head_parts(own):
        return [own] + [exchange(own, "expert", distance) for distance in range(1, z_size)]

    def transposed(weight):
        return jnp.swapaxes(weight[0], 1, 2).reshape(own_experts * width, half)

    def start_of(routes):
        local_routes = routes[0, :, 0]
        group = (local_routes // own_experts) ^ z_at
        local_routes = group * own_experts + local_routes % own_experts
        return jnp.swapaxes(local_routes.reshape(micro_count, blocks, span, picks), 2, 3)

    query_parts = head_parts(transposed(query_weight))
    router_t = router_weight[0].T.reshape(z_size, own_experts, half)
    router_t = permute_groups(router_t, z_at).reshape(experts, half)
    router_t = jnp.pad(router_t, ((0, spare - experts), (0, 0)))
    vectors = jnp.concatenate([ln1_gain, ln1_bias, ln2_gain, ln2_bias, down_bias], 0)
    small = jnp.concatenate([vectors, up_bias.reshape(-1, half)], 0)
    small_other = exchange(small, "fsdp", 1)
    vectors = both_halves(vectors, small_other[:5], 1).astype(F32)
    up_shift = both_halves(up_bias, small_other[5:].reshape(1, -1), 1).astype(F32)

    up_other = exchange(up_weight[0], "fsdp", 1)
    down_other = exchange(down_weight[0], "fsdp", 1)
    route_t = start_of(routes)
    own_out = transposed(out_weight)
    lens, ids, route_t, vectors, up_shift, router_t, own_out, *query_parts = (
        lax.optimization_barrier(
            (lens, ids, route_t, vectors, up_shift, router_t, own_out, *query_parts)
        )
    )
    proj = jnp.concatenate(query_parts + [kv_weight[0].T, router_t], 0)
    proj_other = exchange(proj, "fsdp", 1)
    out_parts = head_parts(own_out)

    states = inputs.reshape(micro_count, blocks, span, model)
    cotangent = out_cotangent.reshape(micro_count, blocks, span, model)

    grid = (micro_count, blocks)
    hid_s = struct((micro_count, blocks, span, model), BF16)
    aug_s = struct((micro_count, blocks, span, 2 * width), BF16)
    kt_s = struct((micro_count, blocks, 1, width, span), BF16)
    q_s = struct((micro_count, blocks, width, rows), BF16)
    row_s = struct((micro_count, blocks, 1, rows), F32)
    gate_s = struct((micro_count, blocks, experts, span), F32)
    slot_s = struct((micro_count, blocks, experts, span), jnp.int32)
    tokens = micro_count * slots
    pair_flops = tokens * picks * slots * width
    hid, kaug, vaug, kt, q, ctx, lse, gates, slot = pl.pallas_call(
        forward_kernel,
        name="forward",
        grid_spec=pltpu.PrefetchScalarGridSpec(
            num_scalar_prefetch=2,
            grid=grid,
            in_specs=[
                blocked(states.shape),
                blocked(route_t.shape),
                full(vectors.shape),
                in_place(),
                in_place(),
            ],
            out_specs=[
                blocked(hid_s.shape),
                whole(aug_s.shape),
                whole(aug_s.shape),
                blocked(kt_s.shape),
                blocked(q_s.shape),
                blocked(q_s.shape),
                blocked(row_s.shape),
                blocked(gate_s.shape),
                blocked(slot_s.shape),
            ],
            scratch_shapes=[
                pltpu.VMEM((head, span), BF16),
                pltpu.VMEM((2 * width, rows), BF16),
                pltpu.VMEM((blocks, span, rows), F32),
                pltpu.VMEM((blocks, width, span), BF16),
                pltpu.VMEM((width, rows), F32),
                pltpu.VMEM((2 * all_rows, half), BF16),
                pltpu.SemaphoreType.DMA((2,)),
            ],
        ),
        out_shape=[hid_s, aug_s, aug_s, kt_s, q_s, q_s, row_s, gate_s, slot_s],
        compiler_params=params(),
        cost_estimate=cost(2 * tokens * model * all_rows + 16 * pair_flops, 0, 64 << 20),
    )(lens, ids, states, route_t, vectors, proj, proj_other)

    ctx, *out_parts = lax.optimization_barrier((ctx, *out_parts))
    out_proj = jnp.concatenate(out_parts, 0)
    out_other = exchange(out_proj, "fsdp", 1)
    state_s = struct((micro_count, blocks, span, model), F32)
    mid_rows = chunk * hidden_units * 2 // 128 + head // z_size * (chunk * z_size) // 128
    late_rows = head // z_size * (chunk * z_size) // 128 + 2 * chunk
    if aligned:
        mid_grads = [struct((dp_size, z_size, mid_rows, 128), BF16)] * 2
        late_grads = [struct((dp_size, z_size, late_rows, 128), BF16)] * 2
    else:
        mid_grads = [
            struct((hidden_units, model), BF16),
            struct((model, hidden_units), BF16),
            struct((model, head), BF16),
        ]
        late_grads = [struct((model, head + 2 * width + 128), BF16)]
    outputs, mid, grad_ctx, delta, grad_logits, small2, up_small, *mid_grads = pl.pallas_call(
        middle_kernel,
        name="middle",
        grid_spec=pltpu.PrefetchScalarGridSpec(
            num_scalar_prefetch=2,
            grid=(micro_count, blocks // group),
            in_specs=[
                grouped(states.shape, group),
                grouped(q_s.shape, group),
                grouped(gate_s.shape, group),
                grouped(slot_s.shape, group),
                grouped(cotangent.shape, group),
                in_place(),
                in_place(),
                full(vectors.shape),
                in_place(),
                in_place(),
                full(up_shift.shape),
                in_place(),
                in_place(),
            ],
            out_specs=[
                grouped(state_s.shape, group),
                grouped(state_s.shape, group),
                grouped(q_s.shape, group),
                grouped(row_s.shape, group),
                grouped(gate_s.shape, group),
                full((3, 8, model)),
                full((8, hidden_units)),
            ]
            + [full(leaf.shape) for leaf in mid_grads],
            scratch_shapes=[
                pltpu.VMEM((group, width, rows), BF16),
                pltpu.VMEM((head, group * span), BF16),
                pltpu.VMEM((head, group * span), BF16),
                pltpu.VMEM((hidden_units, model), F32),
                pltpu.VMEM((model, hidden_units), F32),
                pltpu.VMEM((model, head), F32),
                pltpu.VMEM((2 * head, half), BF16),
                pltpu.VMEM((model, hidden_units), BF16),
                pltpu.VMEM((hidden_units, model), BF16),
                pltpu.SemaphoreType.DMA((6,)),
            ],
        ),
        out_shape=[
            state_s,
            hid_s,
            q_s,
            row_s,
            gate_s,
            struct((3, 8, model), F32),
            struct((8, hidden_units), F32),
        ]
        + mid_grads,
        compiler_params=params(),
        cost_estimate=cost(2 * tokens * model * (6 * hidden_units + 3 * head), 0, 200 << 20),
    )(
        lens,
        ids,
        states,
        ctx,
        gates,
        slot,
        cotangent,
        out_proj,
        out_other,
        vectors,
        up_weight[0],
        up_other,
        up_shift,
        down_weight[0],
        down_other,
    )

    if aligned:
        mid_sums = core_stage(mid_grads)
        grad_ctx, *mid_sums = lax.optimization_barrier((grad_ctx, *mid_sums))
        mid_received = send_stage(mid_sums, "dp")

    expert_id = jnp.arange(experts)
    moved = ((expert_id // own_experts) ^ z_at) * own_experts + expert_id % own_experts
    order = jnp.pad(
        (jnp.arange(spare)[:, None] == moved[None, :]).astype(BF16), ((0, 0), (0, 128 - experts))
    )
    deep = hidden_units // model
    columns = jnp.concatenate(
        [
            vectors[:2].T,
            jnp.sum(small2, 1).T,
            jnp.swapaxes(jnp.sum(up_small, 0).reshape(devices, deep, chunk), 1, 2).reshape(model, deep),
        ],
        1,
    )
    columns = jnp.pad(columns, ((0, 0), (experts, 128 - experts - 5 - deep)))
    r_s = struct((micro_count, blocks // group, all_rows, group * span), BF16)

    def routed_block(m, i, *refs):
        block = blocks - 1 - i
        return m, block // group, 0, block % group

    routed, *late_grads = pl.pallas_call(
        backward_kernel,
        name="backward",
        grid_spec=pltpu.PrefetchScalarGridSpec(
            num_scalar_prefetch=2,
            grid=grid,
            in_specs=[
                reversed_blocks(hid_s.shape),
                whole(aug_s.shape),
                whole(aug_s.shape),
                whole((micro_count, blocks, width, span)),
                reversed_blocks(q_s.shape),
                reversed_blocks(row_s.shape),
                reversed_blocks(q_s.shape),
                reversed_blocks(row_s.shape),
                reversed_blocks(slot_s.shape),
                reversed_blocks(gate_s.shape),
                full(order.shape),
                full(columns.shape),
                in_place(),
                in_place(),
            ],
            out_specs=[pl.BlockSpec((1, 1, all_rows, span), routed_block)]
            + [full(leaf.shape) for leaf in late_grads],
            scratch_shapes=[
                pltpu.VMEM((2 * width, rows), BF16),
                pltpu.VMEM((2 * width, rows), BF16),
                pltpu.VMEM((width, rows), F32),
                pltpu.VMEM((blocks, width, span), F32),
                pltpu.VMEM((blocks, width, span), F32),
                pltpu.VMEM((model + 16, head + 2 * width + 128), F32),
                pltpu.VMEM((2 * all_rows, half), BF16),
                pltpu.SemaphoreType.DMA((2,)),
            ],
        ),
        out_shape=[r_s] + late_grads,
        compiler_params=params(),
        cost_estimate=cost(2 * tokens * model * all_rows + 40 * pair_flops, 0, 100 << 20),
    )(
        lens,
        ids,
        hid,
        kaug,
        vaug,
        kt.reshape(micro_count, blocks, width, span),
        q,
        lse,
        grad_ctx,
        delta,
        slot,
        grad_logits,
        order,
        columns,
        proj,
        proj_other,
    )

    if aligned:
        *mid_received, late_grads[0], late_grads[1] = lax.optimization_barrier(
            (*mid_received, *late_grads)
        )
        *mid_received, late_grads[0], late_grads[1] = lax.optimization_barrier(
            (*mid_received, *late_grads)
        )
        late_sums = core_stage(late_grads)
        *mid_received, late_sums[0] = lax.optimization_barrier((*mid_received, late_sums[0]))
        mid_sums = split_targets(add_up(mid_sums[0], mid_received), "expert")
        routed, *sums = lax.optimization_barrier((routed, *mid_sums, *late_sums))
        mid_sums, late_sums = sums[:z_size], sums[z_size:]
        mid_received = send_stage(mid_sums, "expert")
        late_received = send_stage(late_sums, "dp")

    input_grad = pl.pallas_call(
        input_kernel,
        name="input_back",
        grid_spec=pltpu.PrefetchScalarGridSpec(
            num_scalar_prefetch=1,
            grid=(micro_count, blocks // group),
            in_specs=[
                grouped(states.shape, group),
                grouped(state_s.shape, group),
                blocked(r_s.shape),
                in_place(),
                in_place(),
                full(vectors.shape),
            ],
            out_specs=grouped(state_s.shape, group),
            scratch_shapes=[
                pltpu.VMEM((2 * all_rows, half), BF16),
                pltpu.SemaphoreType.DMA((2,)),
            ],
        ),
        out_shape=state_s,
        compiler_params=params(),
        cost_estimate=cost(2 * tokens * model * all_rows, 0, 40 << 20),
    )(ids, states, mid, routed, proj, proj_other, vectors)

    def open_heads(value):
        return jnp.swapaxes(value.reshape(-1, own_experts, width), 0, 1)[None]

    if aligned:
        input_grad, *received = lax.optimization_barrier(
            (input_grad, *late_received, *mid_received)
        )
        late_received = received[: dp_size - 1]
        mid_received = received[dp_size - 1 :]
        late_sums = split_targets(add_up(late_sums[0], late_received), "expert")
        late_received = send_stage(late_sums, "expert")
        mid_total = total_up(mid_sums[0], mid_received)
        up_weight_grad, at = open_tiles(mid_total, 0, chunk, hidden_units)
        down_weight_grad, at = open_tiles(mid_total, at, hidden_units // devices, model)
        out_weight_grad, at = open_tiles(mid_total, at, chunk * z_size, head // z_size)
        out_weight_grad = open_heads(out_weight_grad)
        query_weight_grad, kv_grad, router_grad, up_bias_grad, *small = pl.pallas_call(
            functools.partial(finish_kernel, experts, deep),
            name="finish",
            out_shape=[
                struct((1, own_experts, chunk * z_size, width), F32),
                struct((1, chunk, 2 * width), F32),
                struct((1, chunk, experts), F32),
                struct((1, deep * chunk), F32),
            ]
            + [struct((1, chunk), F32)] * 5,
        )(late_sums[0], *late_received)
    else:
        down_grad, up_grad, wo_grad = mid_grads
        w_grad = late_grads[0]

        def reduce_shared(value, part):
            value = value.reshape(dp_size, z_size, f_size, part, value.shape[1])
            value = reduce_axis(value, "fsdp", 2)
            value = reduce_axis(value, "dp", 0)
            return reduce_axis(value, "expert", 0, keep=True)

        def reduce_heads(value):
            value = value.reshape(dp_size, f_size, chunk * z_size, z_size, own_experts * width)
            value = reduce_axis(value, "fsdp", 1)
            value = reduce_axis(value, "dp", 0)
            return open_heads(reduce_axis(value, "expert", 1, relative=True, keep=True))

        up_weight_grad = reduce_shared(up_grad, chunk)
        down_weight_grad = reduce_shared(down_grad, hidden_units // devices)
        out_weight_grad = reduce_heads(wo_grad)
        query_weight_grad = reduce_heads(w_grad[:, :head])
        narrow = reduce_shared(w_grad[:, head:], chunk)
        kv_grad, router_grad = narrow[None, :, : 2 * width], narrow[None, :, 2 * width :]
        small = [router_grad[:, :, experts + at] for at in range(5)]
        up_bias_grad = router_grad[0, :, experts + 5 : experts + 5 + deep].T.reshape(1, -1)
        router_grad = router_grad[:, :, :experts]
    shape = (micro_count, 1, slots, model)
    return (
        outputs.reshape(shape),
        input_grad.reshape(shape),
        small[0],
        small[1],
        kv_grad,
        router_grad,
        query_weight_grad,
        out_weight_grad,
        small[2],
        small[3],
        up_weight_grad[None],
        up_bias_grad,
        down_weight_grad[None],
        small[4],
    )


def solution(mesh):
    shards = P(None, AXES, None, None)
    return jax.shard_map(
        local,
        mesh=mesh,
        in_specs=(
            shards,
            P(),
            P(None, None, AXES, None, None),
            P(None, "fsdp"),
            P(None, "fsdp"),
            P(None, "fsdp", None),
            P(None, "fsdp", None),
            P(None, "expert", "fsdp", None),
            P(None, "expert", "fsdp", None),
            P(None, "fsdp"),
            P(None, "fsdp"),
            P(None, "fsdp", None),
            P(None, "fsdp"),
            P(None, "fsdp", None),
            P(None, "fsdp"),
            shards,
        ),
        out_specs=(
            shards,
            shards,
            P(None, AXES),
            P(None, AXES),
            P(None, AXES, None),
            P(None, AXES, None),
            P(None, "expert", ("dp", "fsdp"), None),
            P(None, "expert", ("dp", "fsdp"), None),
            P(None, AXES),
            P(None, AXES),
            P(None, AXES, None),
            P(None, AXES),
            P(None, AXES, None),
            P(None, AXES),
        ),
        check_vma=False,
    )
```
